256 devices in a mesh: dp: 8 (over z_hi, core), expert: 32 (over x, z_lo, y).
Axes of the slice: x: 4, y: 4, z: 8 (z_hi: 4, z_lo: 2; z = z_hi * 2 + z_lo), core: 2. Of those that a mesh axis runs over, the one named last changes fastest.
Arguments:
- tokens: bfloat16 [256, 256, 1024], P(('dp', 'expert'))
- router: bfloat16 [1024, 128], replicated
- weight_in: bfloat16 [128, 1024, 2048], P('expert', None, 'dp'), may hold values from -0.1875 to 0.1875
- weight_out: bfloat16 [128, 2048, 1024], P('expert', 'dp'), may hold values from -0.125 to 0.125
- cotangent: bfloat16 [256, 256, 1024], P(('dp', 'expert')), may hold values from -6 to 6
Outputs:
- mixed: bfloat16 [256, 256, 1024], P(('dp', 'expert'))
- grad_tokens: bfloat16 [256, 256, 1024], P(('dp', 'expert'))
- grad_router: float32 [1024, 128], replicated
- grad_weight_in: bfloat16 [128, 1024, 2048], P('expert', None, 'dp')
- grad_weight_out: bfloat16 [128, 2048, 1024], P('expert', 'dp')
The draws below stay inside these ranges and needn't reach their ends.
All inputs are finite; a program needn't handle non-finite values.
Results may differ from the reference program's by a relative error of at most 0.018.
Values may be sent and summed in bfloat16 or wider, within the bound.
A program may use at most 64 MiB of HBM per device.

```python
import math
import jax
import jax.numpy as jnp
from jax import lax

D = 1024
FF = 2048
S = 256
EXPERTS = 128
IMAGES = 256
N_DP = 8


def draw_tokens(key, part):
    first_key = jax.random.fold_in(jax.random.fold_in(key, 11), 0)
    shape = (IMAGES, S, D)
    values = jnp.clip(jax.random.normal(first_key, shape, jnp.float32), -6.0, 6.0)
    return values.astype(jnp.bfloat16)


def draw_router(key, part):
    first_key = jax.random.fold_in(key, 23)
    shape = (D, EXPERTS)
    values = jnp.clip(jax.random.normal(first_key, shape, jnp.float32), -6.0, 6.0) / math.sqrt(D)
    return values.astype(jnp.bfloat16)


def steps_of(rng, dims, cuts, low, top_value):
    loudness, own = 1.0, jax.random.fold_in(rng, 6)
    for dim, shards_of in cuts:
        steps = jnp.exp(jax.random.uniform(jax.random.fold_in(own, dim), (shards_of,), jnp.float32, low / len(cuts), top_value / len(cuts)))
        loudness = loudness * jnp.repeat(steps, dims[dim] // shards_of).reshape([-1 if axis == dim else 1 for axis in range(len(dims))])
    return loudness


def bell_draw(stream_key, shape, scale, most, shards=(), held_as=jnp.bfloat16):
    loudness = steps_of(stream_key, shape, shards, -0.22, 0.18) if shards else 1.0
    values = jax.random.normal(stream_key, shape, jnp.float32) * scale * loudness
    return jnp.minimum(jnp.maximum(values, -most), most).astype(held_as)


def setup_inputs(seed: int = 0) -> dict:
    key_of = jax.random.split(jax.random.key(seed), 6)
    tokens = draw_tokens(jax.random.fold_in(key_of[5], 71), 0)
    router = draw_router(jax.random.fold_in(key_of[5], 71), 0)
    weight_in = bell_draw(key_of[2], (EXPERTS, D, FF), D ** -0.5, 0.1875, ((0, 32), (2, 8)))
    weight_out = bell_draw(key_of[3], (EXPERTS, FF, D), FF ** -0.5, 0.125, ((0, 32), (1, 8)))
    cotangent = bell_draw(key_of[4], (IMAGES, S, D), 1.0, 6.0, ((0, 256),))
    return dict(tokens=tokens, router=router, weight_in=weight_in, weight_out=weight_out, cotangent=cotangent)


def gelu_exact(values):
    return jax.nn.gelu(values, approximate=False)

def group_total(pieces):
    rounded = lax.optimization_barrier(pieces.astype(jnp.bfloat16))
    return lax.optimization_barrier(jnp.sum(rounded.astype(jnp.float32), axis=1)).astype(jnp.bfloat16)

def reference(tokens, router, weight_in, weight_out, cotangent):
    ff_dev = FF // N_DP

    def router_probs(image):
        logits = jnp.dot(image, router, preferred_element_type=jnp.float32)
        return (jax.nn.softmax(logits, axis=0), jax.nn.softmax(logits, axis=1))

    def front_side(pair):
        image, grad_image = pair
        dispatch_prob, combine_prob = router_probs(image)
        dispatch = dispatch_prob.astype(jnp.bfloat16)
        combine = combine_prob.astype(jnp.bfloat16)
        slots = jnp.dot(dispatch.T, image, preferred_element_type=jnp.float32).astype(jnp.bfloat16)
        grad_slots = jnp.dot(combine.T, grad_image, preferred_element_type=jnp.float32).astype(jnp.bfloat16)
        return (slots, grad_slots)
    slots, grad_slots = lax.map(front_side, (tokens, cotangent))

    def expert_side(group):
        slot_rows, grad_rows, w_first, w_second = group
        pre_act = jnp.dot(slot_rows, w_first, preferred_element_type=jnp.float32)
        hidden = gelu_exact(pre_act).astype(jnp.bfloat16)
        pieces = jnp.einsum('ipf,pfd->ipd', hidden.reshape(IMAGES, N_DP, ff_dev).astype(jnp.float32), w_second.reshape(N_DP, ff_dev, D).astype(jnp.float32))
        expert_out = group_total(pieces)
        grad_hidden = jnp.dot(grad_rows, w_second.T, preferred_element_type=jnp.float32)
        _, gelu_back = jax.vjp(gelu_exact, pre_act)
        grad_pre = gelu_back(grad_hidden)[0].astype(jnp.bfloat16)
        grad_second = jnp.dot(hidden.T, grad_rows, preferred_element_type=jnp.float32).astype(jnp.bfloat16)
        grad_first = jnp.dot(slot_rows.T, grad_pre, preferred_element_type=jnp.float32).astype(jnp.bfloat16)
        first_parts = jnp.transpose(w_first.reshape(D, N_DP, ff_dev), (1, 0, 2))
        back_pieces = jnp.einsum('ipf,pdf->ipd', grad_pre.reshape(IMAGES, N_DP, ff_dev).astype(jnp.float32), first_parts.astype(jnp.float32))
        grad_slot = group_total(back_pieces)
        return (expert_out, grad_slot, grad_first, grad_second)
    outs_by_expert, grad_by_expert, grad_weight_in, grad_weight_out = lax.map(expert_side, (jnp.transpose(slots, (1, 0, 2)), jnp.transpose(grad_slots, (1, 0, 2)), weight_in, weight_out))
    expert_outs = jnp.transpose(outs_by_expert, (1, 0, 2))
    grad_slot_all = jnp.transpose(grad_by_expert, (1, 0, 2))

    def back_side(total, group):
        image, grad_image, expert_out, grad_slot = group
        dispatch_prob, combine_prob = router_probs(image)
        dispatch = dispatch_prob.astype(jnp.bfloat16)
        combine = combine_prob.astype(jnp.bfloat16)
        mixed = jnp.dot(combine, expert_out, preferred_element_type=jnp.float32).astype(jnp.bfloat16)
        grad_comb = jnp.dot(grad_image, expert_out.T, preferred_element_type=jnp.float32)
        grad_disp = jnp.dot(image, grad_slot.T, preferred_element_type=jnp.float32)
        part_disp = dispatch_prob * (grad_disp - lax.optimization_barrier(jnp.sum(dispatch_prob * grad_disp, axis=0, keepdims=True)))
        part_comb = combine_prob * (grad_comb - lax.optimization_barrier(jnp.sum(combine_prob * grad_comb, axis=1, keepdims=True)))
        grad_logits = (part_disp + part_comb).astype(jnp.bfloat16)
        grad_image_out = (jnp.dot(dispatch, grad_slot, preferred_element_type=jnp.float32) + jnp.dot(grad_logits, router.T, preferred_element_type=jnp.float32)).astype(jnp.bfloat16)
        router_term = jnp.dot(image.T, grad_logits, preferred_element_type=jnp.float32)
        return (total + router_term, (mixed, grad_image_out))
    start = jnp.zeros((D, EXPERTS), jnp.float32)
    grad_router, (mixed, grad_tokens) = lax.scan(back_side, start, (tokens, cotangent, expert_outs, grad_slot_all))
    return (mixed, grad_tokens, grad_router, grad_weight_in, grad_weight_out)
```

```python
import functools

import jax
import jax.numpy as jnp
from jax import lax
from jax.sharding import PartitionSpec as P


def gelu_exact(values):
    return jax.nn.gelu(values, approximate=False)


def all_sum(value, n_dp, n_expert):
    rows, cols = value.shape
    part = value.reshape(n_expert, rows // n_expert, cols)
    part = lax.all_to_all(part, "expert", 0, 0, tiled=True).sum(0)
    part = part.reshape(n_dp, rows // (n_expert * n_dp), cols)
    part = lax.all_to_all(part, "dp", 0, 0, tiled=True).sum(0)
    whole = jnp.broadcast_to(part[None], (n_dp,) + part.shape)
    whole = lax.all_to_all(whole, "dp", 0, 0, tiled=True).reshape(rows // n_expert, cols)
    whole = jnp.broadcast_to(whole[None], (n_expert,) + whole.shape)
    whole = lax.all_to_all(whole, "expert", 0, 0, tiled=True)
    return whole.reshape(rows, cols)


def local(n_dp, n_expert, tokens, router, weight_in, weight_out, cotangent):
    experts_dev = weight_in.shape[0]
    width = tokens.shape[2]
    logits = jnp.einsum("isd,de->ise", tokens, router, preferred_element_type=jnp.float32)
    dispatch_prob = jax.nn.softmax(logits, axis=1)
    combine_prob = jax.nn.softmax(logits, axis=2)
    dispatch = dispatch_prob.astype(jnp.bfloat16)
    combine = combine_prob.astype(jnp.bfloat16)
    slots = jnp.einsum("ise,isd->ied", dispatch, tokens, preferred_element_type=jnp.float32).astype(
        jnp.bfloat16
    )
    grad_slots = jnp.einsum(
        "ise,isd->ied", combine, cotangent, preferred_element_type=jnp.float32
    ).astype(jnp.bfloat16)

    def to_owners(local_rows):
        arrived = lax.all_to_all(local_rows, "expert", split_axis=1, concat_axis=1, tiled=True)
        return lax.all_gather(arrived, "dp", axis=0, tiled=True)

    def from_owners(partial_value):
        summed = lax.psum_scatter(partial_value, "dp", scatter_dimension=0, tiled=True).astype(
            jnp.float32
        )
        return lax.all_to_all(
            summed.astype(jnp.bfloat16), "expert", split_axis=1, concat_axis=1, tiled=True
        )

    slot_rows = to_owners(slots)
    blocks = slot_rows.reshape(-1, experts_dev, width)
    pre_act = jnp.einsum("rkd,kdf->rkf", blocks, weight_in, preferred_element_type=jnp.float32)
    hidden = gelu_exact(pre_act).astype(jnp.bfloat16)
    partial_value = jnp.einsum(
        "rkf,kfd->rkd", hidden, weight_out, preferred_element_type=jnp.float32
    )
    blocks, pre_act, hidden, partial_value = (
        blocks,
        pre_act,
        hidden,
        partial_value.astype(jnp.bfloat16).reshape(slot_rows.shape),
    )
    expert_outs = from_owners(partial_value)
    grad_rows = to_owners(grad_slots)
    grad_blocks = grad_rows.reshape(blocks.shape)
    grad_hidden = jnp.einsum(
        "rkd,kfd->rkf", grad_blocks, weight_out, preferred_element_type=jnp.float32
    )
    _, gelu_back = jax.vjp(gelu_exact, pre_act)
    grad_pre = gelu_back(grad_hidden)[0].astype(jnp.bfloat16)
    grad_second = jnp.einsum(
        "rkf,rkd->kfd", hidden, grad_blocks, preferred_element_type=jnp.float32
    ).astype(jnp.bfloat16)
    grad_first = jnp.einsum(
        "rkd,rkf->kdf", blocks, grad_pre, preferred_element_type=jnp.float32
    ).astype(jnp.bfloat16)
    partial_back = jnp.einsum(
        "rkf,kdf->rkd", grad_pre, weight_in, preferred_element_type=jnp.float32
    )
    grad_first, grad_second, partial_back = (
        grad_first,
        grad_second,
        partial_back.astype(jnp.bfloat16).reshape(grad_rows.shape),
    )
    grad_slot_all = from_owners(partial_back)
    mixed = jnp.einsum(
        "ise,ied->isd", combine, expert_outs, preferred_element_type=jnp.float32
    ).astype(jnp.bfloat16)
    grad_comb = jnp.einsum(
        "isd,ied->ise", cotangent, expert_outs, preferred_element_type=jnp.float32
    )
    grad_disp = jnp.einsum(
        "isd,ied->ise", tokens, grad_slot_all, preferred_element_type=jnp.float32
    )
    part_disp = dispatch_prob * (
        grad_disp - jnp.sum(dispatch_prob * grad_disp, axis=1, keepdims=True)
    )
    part_comb = combine_prob * (
        grad_comb - jnp.sum(combine_prob * grad_comb, axis=2, keepdims=True)
    )
    grad_logits = (part_disp + part_comb).astype(jnp.bfloat16)
    grad_tokens = (
        jnp.einsum("ise,ied->isd", dispatch, grad_slot_all, preferred_element_type=jnp.float32)
        + jnp.einsum("ise,de->isd", grad_logits, router, preferred_element_type=jnp.float32)
    ).astype(jnp.bfloat16)
    router_term = jnp.einsum("isd,ise->de", tokens, grad_logits, preferred_element_type=jnp.float32)
    grad_router = all_sum(router_term, n_dp, n_expert)
    return (mixed, grad_tokens, grad_router, grad_first, grad_second)


def solution(mesh):
    return jax.shard_map(
        functools.partial(local, mesh.shape["dp"], mesh.shape["expert"]),
        mesh=mesh,
        in_specs=(
            P(("dp", "expert"), None, None),
            P(),
            P("expert", None, "dp"),
            P("expert", "dp", None),
            P(("dp", "expert"), None, None),
        ),
        out_specs=(
            P(("dp", "expert"), None, None),
            P(("dp", "expert"), None, None),
            P(),
            P("expert", None, "dp"),
            P("expert", "dp", None),
        ),
        check_vma=False,
    )
```

```python
import functools

import jax
import jax.numpy as jnp
from jax import lax
from jax.experimental import pallas as pl
from jax.experimental.pallas import tpu as pltpu
from jax.sharding import PartitionSpec as P


def _exchange_kernel(axis, other, n, gather, x_ref, o_ref, land, send_sem, recv_sem):
    me = lax.axis_index(axis)
    fixed = lax.axis_index(other)

    def peer(j):
        if axis == "dp":
            return (j, fixed)
        return (fixed, j)

    barrier = pltpu.get_barrier_semaphore()

    @pl.loop(0, n)
    def _(j):
        @pl.when(j != me)
        def _():
            pl.semaphore_signal(barrier, inc=1, device_id=peer(j), device_id_type=pl.DeviceIdType.MESH)

    pl.semaphore_wait(barrier, n - 1)

    def copy_to(j):
        src = x_ref if gather else x_ref.at[j]
        return pltpu.make_async_remote_copy(
            src_ref=src,
            dst_ref=land.at[me],
            send_sem=send_sem.at[j],
            recv_sem=recv_sem.at[me],
            device_id=peer(j),
            device_id_type=pl.DeviceIdType.MESH,
        )

    @pl.loop(0, n)
    def _(j):
        @pl.when(j != me)
        def _():
            copy_to(j).start()

    own = x_ref[...] if gather else x_ref[me]
    o_ref[me] = own

    def arrived(j):
        src = x_ref if gather else x_ref.at[j]
        return pltpu.make_async_remote_copy(
            src_ref=src,
            dst_ref=land.at[j],
            send_sem=send_sem.at[j],
            recv_sem=recv_sem.at[j],
            device_id=peer(j),
            device_id_type=pl.DeviceIdType.MESH,
        )

    @pl.loop(0, n)
    def _(j):
        @pl.when(j != me)
        def _():
            arrived(j).wait_recv()
            o_ref[j] = land[j]
            copy_to(j).wait_send()


def exchange(x, axis, n, collective_id, gather=False):
    other = "expert" if axis == "dp" else "dp"
    block = x.shape if gather else x.shape[1:]
    out_shape = jax.ShapeDtypeStruct((n,) + tuple(block), x.dtype)
    return pl.pallas_call(
        functools.partial(_exchange_kernel, axis, other, n, gather),
        out_shape=out_shape,
        in_specs=[pl.BlockSpec(memory_space=pltpu.VMEM)],
        out_specs=pl.BlockSpec(memory_space=pltpu.VMEM),
        scratch_shapes=[
            pltpu.VMEM(out_shape.shape, x.dtype),
            pltpu.SemaphoreType.DMA((n,)),
            pltpu.SemaphoreType.DMA((n,)),
        ],
        compiler_params=pltpu.CompilerParams(collective_id=collective_id, has_side_effects=True),
    )(x)


def gelu_exact(values):
    return jax.nn.gelu(values, approximate=False)


def all_sum(value, n_dp, n_expert):
    rows, cols = value.shape
    part = value.reshape(n_expert, rows // n_expert, cols)
    part = exchange(part, "expert", n_expert, 4).sum(0)
    part = part.reshape(n_dp, rows // (n_expert * n_dp), cols)
    part = exchange(part, "dp", n_dp, 5).sum(0)
    whole = exchange(part, "dp", n_dp, 6, gather=True).reshape(rows // n_expert, cols)
    whole = exchange(whole, "expert", n_expert, 7, gather=True)
    return whole.reshape(rows, cols)


def local(n_dp, n_expert, tokens, router, weight_in, weight_out, cotangent):
    experts_dev = weight_in.shape[0]
    width = tokens.shape[2]
    logits = jnp.einsum("isd,de->ise", tokens, router, preferred_element_type=jnp.float32)
    dispatch_prob = jax.nn.softmax(logits, axis=1)
    combine_prob = jax.nn.softmax(logits, axis=2)
    dispatch = dispatch_prob.astype(jnp.bfloat16)
    combine = combine_prob.astype(jnp.bfloat16)
    slots = jnp.einsum("ise,isd->ied", dispatch, tokens, preferred_element_type=jnp.float32).astype(
        jnp.bfloat16
    )
    grad_slots = jnp.einsum(
        "ise,isd->ied", combine, cotangent, preferred_element_type=jnp.float32
    ).astype(jnp.bfloat16)

    def to_owners(local_rows, cid):
        chunks = local_rows.reshape(n_expert, experts_dev, width)
        arrived = exchange(chunks, "expert", n_expert, cid).reshape(local_rows.shape)
        return lax.all_gather(arrived, "dp", axis=0, tiled=True)

    def from_owners(partial_value, cid):
        summed = lax.psum_scatter(partial_value, "dp", scatter_dimension=0, tiled=True)
        chunks = summed.reshape(n_expert, experts_dev, width)
        return exchange(chunks, "expert", n_expert, cid).reshape(summed.shape)

    slot_rows = to_owners(slots, 0)
    blocks = slot_rows.reshape(-1, experts_dev, width)
    pre_act = jnp.einsum("rkd,kdf->rkf", blocks, weight_in, preferred_element_type=jnp.float32)
    hidden = gelu_exact(pre_act).astype(jnp.bfloat16)
    partial_value = jnp.einsum(
        "rkf,kfd->rkd", hidden, weight_out, preferred_element_type=jnp.float32
    )
    blocks, pre_act, hidden, partial_value = (
        blocks,
        pre_act,
        hidden,
        partial_value.astype(jnp.bfloat16).reshape(slot_rows.shape),
    )
    expert_outs = from_owners(partial_value, 2)
    grad_rows = to_owners(grad_slots, 1)
    grad_blocks = grad_rows.reshape(blocks.shape)
    grad_hidden = jnp.einsum(
        "rkd,kfd->rkf", grad_blocks, weight_out, preferred_element_type=jnp.float32
    )
    _, gelu_back = jax.vjp(gelu_exact, pre_act)
    grad_pre = gelu_back(grad_hidden)[0].astype(jnp.bfloat16)
    grad_second = jnp.einsum(
        "rkf,rkd->kfd", hidden, grad_blocks, preferred_element_type=jnp.float32
    ).astype(jnp.bfloat16)
    grad_first = jnp.einsum(
        "rkd,rkf->kdf", blocks, grad_pre, preferred_element_type=jnp.float32
    ).astype(jnp.bfloat16)
    partial_back = jnp.einsum(
        "rkf,kdf->rkd", grad_pre, weight_in, preferred_element_type=jnp.float32
    )
    grad_first, grad_second, partial_back = (
        grad_first,
        grad_second,
        partial_back.astype(jnp.bfloat16).reshape(grad_rows.shape),
    )
    grad_slot_all = from_owners(partial_back, 3)
    mixed = jnp.einsum(
        "ise,ied->isd", combine, expert_outs, preferred_element_type=jnp.float32
    ).astype(jnp.bfloat16)
    grad_comb = jnp.einsum(
        "isd,ied->ise", cotangent, expert_outs, preferred_element_type=jnp.float32
    )
    grad_disp = jnp.einsum(
        "isd,ied->ise", tokens, grad_slot_all, preferred_element_type=jnp.float32
    )
    part_disp = dispatch_prob * (
        grad_disp - jnp.sum(dispatch_prob * grad_disp, axis=1, keepdims=True)
    )
    part_comb = combine_prob * (
        grad_comb - jnp.sum(combine_prob * grad_comb, axis=2, keepdims=True)
    )
    grad_logits = (part_disp + part_comb).astype(jnp.bfloat16)
    grad_tokens = (
        jnp.einsum("ise,ied->isd", dispatch, grad_slot_all, preferred_element_type=jnp.float32)
        + jnp.einsum("ise,de->isd", grad_logits, router, preferred_element_type=jnp.float32)
    ).astype(jnp.bfloat16)
    router_term = jnp.einsum("isd,ise->de", tokens, grad_logits, preferred_element_type=jnp.float32)
    grad_router = all_sum(router_term, n_dp, n_expert)
    return (mixed, grad_tokens, grad_router, grad_first, grad_second)


def solution(mesh):
    return jax.shard_map(
        functools.partial(local, mesh.shape["dp"], mesh.shape["expert"]),
        mesh=mesh,
        in_specs=(
            P(("dp", "expert"), None, None),
            P(),
            P("expert", None, "dp"),
            P("expert", "dp", None),
            P(("dp", "expert"), None, None),
        ),
        out_specs=(
            P(("dp", "expert"), None, None),
            P(("dp", "expert"), None, None),
            P(),
            P("expert", None, "dp"),
            P("expert", "dp", None),
        ),
        check_vma=False,
    )
```

```python
import functools

import jax
import jax.numpy as jnp
from jax import lax
from jax.experimental import pallas as pl
from jax.experimental.pallas import tpu as pltpu
from jax.sharding import PartitionSpec as P


def _exchange_kernel(axis, other, n, gather, x_ref, o_ref, land, send_sem, recv_sem):
    me = lax.axis_index(axis)
    fixed = lax.axis_index(other)

    def peer(j):
        if axis == "dp":
            return (j, fixed)
        return (fixed, j)

    barrier = pltpu.get_barrier_semaphore()

    @pl.loop(0, n)
    def _(j):
        @pl.when(j != me)
        def _():
            pl.semaphore_signal(barrier, inc=1, device_id=peer(j), device_id_type=pl.DeviceIdType.MESH)

    pl.semaphore_wait(barrier, n - 1)

    def copy_to(j):
        src = x_ref if gather else x_ref.at[j]
        return pltpu.make_async_remote_copy(
            src_ref=src,
            dst_ref=land.at[me],
            send_sem=send_sem.at[j],
            recv_sem=recv_sem.at[me],
            device_id=peer(j),
            device_id_type=pl.DeviceIdType.MESH,
        )

    @pl.loop(0, n)
    def _(j):
        @pl.when(j != me)
        def _():
            copy_to(j).start()

    own = x_ref[...] if gather else x_ref[me]
    o_ref[me] = own

    def arrived(j):
        src = x_ref if gather else x_ref.at[j]
        return pltpu.make_async_remote_copy(
            src_ref=src,
            dst_ref=land.at[j],
            send_sem=send_sem.at[j],
            recv_sem=recv_sem.at[j],
            device_id=peer(j),
            device_id_type=pl.DeviceIdType.MESH,
        )

    @pl.loop(0, n)
    def _(j):
        @pl.when(j != me)
        def _():
            arrived(j).wait_recv()
            o_ref[j] = land[j]
            copy_to(j).wait_send()


def exchange(x, axis, n, collective_id, gather=False):
    other = "expert" if axis == "dp" else "dp"
    block = x.shape if gather else x.shape[1:]
    out_shape = jax.ShapeDtypeStruct((n,) + tuple(block), x.dtype)
    return pl.pallas_call(
        functools.partial(_exchange_kernel, axis, other, n, gather),
        out_shape=out_shape,
        in_specs=[pl.BlockSpec(memory_space=pltpu.VMEM)],
        out_specs=pl.BlockSpec(memory_space=pltpu.VMEM),
        scratch_shapes=[
            pltpu.VMEM(out_shape.shape, x.dtype),
            pltpu.SemaphoreType.DMA((n,)),
            pltpu.SemaphoreType.DMA((n,)),
        ],
        compiler_params=pltpu.CompilerParams(collective_id=collective_id, has_side_effects=True),
    )(x)


def gelu_exact(values):
    return jax.nn.gelu(values, approximate=False)


def all_sum(value, n_dp, n_expert):
    rows, cols = value.shape
    part = value.reshape(n_expert, rows // n_expert, cols)
    part = exchange(part, "expert", n_expert, 4).sum(0)
    part = exchange(part, "dp", n_dp, 5, gather=True).sum(0)
    whole = exchange(part, "expert", n_expert, 7, gather=True)
    return whole.reshape(rows, cols)


def local(n_dp, n_expert, tokens, router, weight_in, weight_out, cotangent):
    experts_dev = weight_in.shape[0]
    width = tokens.shape[2]
    logits = jnp.einsum("isd,de->ise", tokens, router, preferred_element_type=jnp.float32)
    dispatch_prob = jax.nn.softmax(logits, axis=1)
    combine_prob = jax.nn.softmax(logits, axis=2)
    dispatch = dispatch_prob.astype(jnp.bfloat16)
    combine = combine_prob.astype(jnp.bfloat16)
    slots = jnp.einsum("ise,isd->ied", dispatch, tokens, preferred_element_type=jnp.float32).astype(
        jnp.bfloat16
    )
    grad_slots = jnp.einsum(
        "ise,isd->ied", combine, cotangent, preferred_element_type=jnp.float32
    ).astype(jnp.bfloat16)

    def to_owners(local_rows, cid):
        chunks = local_rows.reshape(n_expert, experts_dev, width)
        arrived = exchange(chunks, "expert", n_expert, cid).reshape(local_rows.shape)
        return lax.all_gather(arrived, "dp", axis=0, tiled=True)

    def from_owners(partial_value, cid):
        pieces = exchange(partial_value, "dp", n_dp, cid + 8)
        summed = pieces.astype(jnp.float32).sum(0).astype(jnp.bfloat16)
        chunks = summed.reshape(n_expert, experts_dev, width)
        return exchange(chunks, "expert", n_expert, cid).reshape(1, *summed.shape)

    slot_rows = to_owners(slots, 0)
    blocks = slot_rows.reshape(-1, experts_dev, width)
    pre_act = jnp.einsum("rkd,kdf->rkf", blocks, weight_in, preferred_element_type=jnp.float32)
    hidden = gelu_exact(pre_act).astype(jnp.bfloat16)
    partial_value = jnp.einsum(
        "rkf,kfd->rkd", hidden, weight_out, preferred_element_type=jnp.float32
    )
    blocks, pre_act, hidden, partial_value = (
        blocks,
        pre_act,
        hidden,
        partial_value.astype(jnp.bfloat16).reshape(slot_rows.shape),
    )
    expert_outs = from_owners(partial_value, 2)
    grad_rows = to_owners(grad_slots, 1)
    grad_blocks = grad_rows.reshape(blocks.shape)
    grad_hidden = jnp.einsum(
        "rkd,kfd->rkf", grad_blocks, weight_out, preferred_element_type=jnp.float32
    )
    _, gelu_back = jax.vjp(gelu_exact, pre_act)
    grad_pre = gelu_back(grad_hidden)[0].astype(jnp.bfloat16)
    grad_second = jnp.einsum(
        "rkf,rkd->kfd", hidden, grad_blocks, preferred_element_type=jnp.float32
    ).astype(jnp.bfloat16)
    grad_first = jnp.einsum(
        "rkd,rkf->kdf", blocks, grad_pre, preferred_element_type=jnp.float32
    ).astype(jnp.bfloat16)
    partial_back = jnp.einsum(
        "rkf,kdf->rkd", grad_pre, weight_in, preferred_element_type=jnp.float32
    )
    grad_first, grad_second, partial_back = (
        grad_first,
        grad_second,
        partial_back.astype(jnp.bfloat16).reshape(grad_rows.shape),
    )
    grad_slot_all = from_owners(partial_back, 3)
    mixed = jnp.einsum(
        "ise,ied->isd", combine, expert_outs, preferred_element_type=jnp.float32
    ).astype(jnp.bfloat16)
    grad_comb = jnp.einsum(
        "isd,ied->ise", cotangent, expert_outs, preferred_element_type=jnp.float32
    )
    grad_disp = jnp.einsum(
        "isd,ied->ise", tokens, grad_slot_all, preferred_element_type=jnp.float32
    )
    part_disp = dispatch_prob * (
        grad_disp - jnp.sum(dispatch_prob * grad_disp, axis=1, keepdims=True)
    )
    part_comb = combine_prob * (
        grad_comb - jnp.sum(combine_prob * grad_comb, axis=2, keepdims=True)
    )
    grad_logits = (part_disp + part_comb).astype(jnp.bfloat16)
    grad_tokens = (
        jnp.einsum("ise,ied->isd", dispatch, grad_slot_all, preferred_element_type=jnp.float32)
        + jnp.einsum("ise,de->isd", grad_logits, router, preferred_element_type=jnp.float32)
    ).astype(jnp.bfloat16)
    router_term = jnp.einsum("isd,ise->de", tokens, grad_logits, preferred_element_type=jnp.float32)
    grad_router = all_sum(router_term, n_dp, n_expert)
    return (mixed, grad_tokens, grad_router, grad_first, grad_second)


def solution(mesh):
    return jax.shard_map(
        functools.partial(local, mesh.shape["dp"], mesh.shape["expert"]),
        mesh=mesh,
        in_specs=(
            P(("dp", "expert"), None, None),
            P(),
            P("expert", None, "dp"),
            P("expert", "dp", None),
            P(("dp", "expert"), None, None),
        ),
        out_specs=(
            P(("dp", "expert"), None, None),
            P(("dp", "expert"), None, None),
            P(),
            P("expert", None, "dp"),
            P("expert", "dp", None),
        ),
        check_vma=False,
    )
```

```python
import functools

import jax
import jax.numpy as jnp
from jax import lax
from jax.experimental import pallas as pl
from jax.experimental.pallas import tpu as pltpu
from jax.sharding import PartitionSpec as P


def _exchange_kernel(axis, other, n, gather, x_ref, o_ref, land, send_sem, recv_sem):
    me = lax.axis_index(axis)
    fixed = lax.axis_index(other)

    def peer(j):
        if axis == "dp":
            return (j, fixed)
        return (fixed, j)

    barrier = pltpu.get_barrier_semaphore()

    @pl.loop(0, n)
    def _(j):
        @pl.when(j != me)
        def _():
            pl.semaphore_signal(barrier, inc=1, device_id=peer(j), device_id_type=pl.DeviceIdType.MESH)

    pl.semaphore_wait(barrier, n - 1)

    def copy_to(j):
        src = x_ref if gather else x_ref.at[j]
        return pltpu.make_async_remote_copy(
            src_ref=src,
            dst_ref=land.at[me],
            send_sem=send_sem.at[j],
            recv_sem=recv_sem.at[me],
            device_id=peer(j),
            device_id_type=pl.DeviceIdType.MESH,
        )

    @pl.loop(0, n)
    def _(j):
        @pl.when(j != me)
        def _():
            copy_to(j).start()

    own = x_ref[...] if gather else x_ref[me]
    o_ref[me] = own

    def arrived(j):
        src = x_ref if gather else x_ref.at[j]
        return pltpu.make_async_remote_copy(
            src_ref=src,
            dst_ref=land.at[j],
            send_sem=send_sem.at[j],
            recv_sem=recv_sem.at[j],
            device_id=peer(j),
            device_id_type=pl.DeviceIdType.MESH,
        )

    @pl.loop(0, n)
    def _(j):
        @pl.when(j != me)
        def _():
            arrived(j).wait_recv()
            o_ref[j] = land[j]
            copy_to(j).wait_send()


def exchange(x, axis, n, collective_id, gather=False):
    other = "expert" if axis == "dp" else "dp"
    block = x.shape if gather else x.shape[1:]
    out_shape = jax.ShapeDtypeStruct((n,) + tuple(block), x.dtype)
    return pl.pallas_call(
        functools.partial(_exchange_kernel, axis, other, n, gather),
        out_shape=out_shape,
        in_specs=[pl.BlockSpec(memory_space=pltpu.VMEM)],
        out_specs=pl.BlockSpec(memory_space=pltpu.VMEM),
        scratch_shapes=[
            pltpu.VMEM(out_shape.shape, x.dtype),
            pltpu.SemaphoreType.DMA((n,)),
            pltpu.SemaphoreType.DMA((n,)),
        ],
        compiler_params=pltpu.CompilerParams(collective_id=collective_id, has_side_effects=True),
    )(x)


def gelu_exact(values):
    return jax.nn.gelu(values, approximate=False)


def _allsum_kernel(n_dp, n_ex, x_ref, o_ref, land1, land2, land3, red1, red2, s1, r1, s2, r2, s3, r3):
    me_d = lax.axis_index("dp")
    me_e = lax.axis_index("expert")
    mesh_id = pl.DeviceIdType.MESH
    barrier = pltpu.get_barrier_semaphore()

    @pl.loop(0, n_ex)
    def _(j):
        @pl.when(j != me_e)
        def _():
            pl.semaphore_signal(barrier, inc=1, device_id=(me_d, j), device_id_type=mesh_id)

    @pl.loop(0, n_dp)
    def _(k):
        @pl.when(k != me_d)
        def _():
            pl.semaphore_signal(barrier, inc=1, device_id=(k, me_e), device_id_type=mesh_id)

    pl.semaphore_wait(barrier, n_ex - 1 + n_dp - 1)

    def ex_copy(src, land, send, recv, j, slot):
        return pltpu.make_async_remote_copy(
            src_ref=src, dst_ref=land.at[slot], send_sem=send.at[j], recv_sem=recv.at[slot],
            device_id=(me_d, j), device_id_type=mesh_id)

    def dp_copy(src, land, send, recv, k, slot):
        return pltpu.make_async_remote_copy(
            src_ref=src, dst_ref=land.at[slot], send_sem=send.at[k], recv_sem=recv.at[slot],
            device_id=(k, me_e), device_id_type=mesh_id)

    @pl.loop(0, n_ex)
    def _(j):
        @pl.when(j != me_e)
        def _():
            ex_copy(x_ref.at[j], land1, s1, r1, j, me_e).start()

    land1[me_e] = x_ref[me_e]

    @pl.loop(0, n_ex)
    def _(j):
        @pl.when(j != me_e)
        def _():
            ex_copy(x_ref.at[j], land1, s1, r1, j, j).wait_recv()
            ex_copy(x_ref.at[j], land1, s1, r1, j, me_e).wait_send()

    red1[...] = jnp.sum(land1[...], axis=0)

    @pl.loop(0, n_dp)
    def _(k):
        @pl.when(k != me_d)
        def _():
            dp_copy(red1, land2, s2, r2, k, me_d).start()

    land2[me_d] = red1[...]

    @pl.loop(0, n_dp)
    def _(k):
        @pl.when(k != me_d)
        def _():
            dp_copy(red1, land2, s2, r2, k, k).wait_recv()
            dp_copy(red1, land2, s2, r2, k, me_d).wait_send()

    total = land2[0]
    for k in range(1, n_dp):
        total = total + land2[k]
    red2[...] = total

    @pl.loop(0, n_ex)
    def _(j):
        @pl.when(j != me_e)
        def _():
            ex_copy(red2, land3, s3, r3, j, me_e).start()

    o_ref[me_e] = red2[...]

    @pl.loop(0, n_ex)
    def _(j):
        @pl.when(j != me_e)
        def _():
            ex_copy(red2, land3, s3, r3, j, j).wait_recv()
            o_ref[j] = land3[j]
            ex_copy(red2, land3, s3, r3, j, me_e).wait_send()


def all_sum(value, n_dp, n_expert):
    rows, cols = value.shape
    block = (rows // n_expert, cols)
    chunks = value.reshape(n_expert, *block)
    out = pl.pallas_call(
        functools.partial(_allsum_kernel, n_dp, n_expert),
        out_shape=jax.ShapeDtypeStruct(chunks.shape, value.dtype),
        in_specs=[pl.BlockSpec(memory_space=pltpu.VMEM)],
        out_specs=pl.BlockSpec(memory_space=pltpu.VMEM),
        scratch_shapes=[
            pltpu.VMEM(chunks.shape, value.dtype),
            pltpu.VMEM((n_dp,) + block, value.dtype),
            pltpu.VMEM(chunks.shape, value.dtype),
            pltpu.VMEM(block, value.dtype),
            pltpu.VMEM(block, value.dtype),
            pltpu.SemaphoreType.DMA((n_expert,)),
            pltpu.SemaphoreType.DMA((n_expert,)),
            pltpu.SemaphoreType.DMA((n_dp,)),
            pltpu.SemaphoreType.DMA((n_dp,)),
            pltpu.SemaphoreType.DMA((n_expert,)),
            pltpu.SemaphoreType.DMA((n_expert,)),
        ],
        compiler_params=pltpu.CompilerParams(collective_id=4, has_side_effects=True),
    )(chunks)
    return out.reshape(rows, cols)


def local(n_dp, n_expert, tokens, router, weight_in, weight_out, cotangent):
    experts_dev = weight_in.shape[0]
    width = tokens.shape[2]
    logits = jnp.einsum("isd,de->ise", tokens, router, preferred_element_type=jnp.float32)
    dispatch_prob = jax.nn.softmax(logits, axis=1)
    combine_prob = jax.nn.softmax(logits, axis=2)
    dispatch = dispatch_prob.astype(jnp.bfloat16)
    combine = combine_prob.astype(jnp.bfloat16)
    slots = jnp.einsum("ise,isd->ied", dispatch, tokens, preferred_element_type=jnp.float32).astype(
        jnp.bfloat16
    )
    grad_slots = jnp.einsum(
        "ise,isd->ied", combine, cotangent, preferred_element_type=jnp.float32
    ).astype(jnp.bfloat16)

    def to_owners(local_rows, cid):
        chunks = local_rows.reshape(n_expert, experts_dev, width)
        arrived = exchange(chunks, "expert", n_expert, cid).reshape(local_rows.shape)
        return lax.all_gather(arrived, "dp", axis=0, tiled=True)

    def from_owners(partial_value, cid):
        summed = lax.psum_scatter(partial_value, "dp", scatter_dimension=0, tiled=True)
        chunks = summed.reshape(n_expert, experts_dev, width)
        return exchange(chunks, "expert", n_expert, cid).reshape(summed.shape)

    slot_rows = to_owners(slots, 0)
    blocks = slot_rows.reshape(-1, experts_dev, width)
    pre_act = jnp.einsum("rkd,kdf->rkf", blocks, weight_in, preferred_element_type=jnp.float32)
    hidden = gelu_exact(pre_act).astype(jnp.bfloat16)
    partial_value = jnp.einsum(
        "rkf,kfd->rkd", hidden, weight_out, preferred_element_type=jnp.float32
    )
    blocks, pre_act, hidden, partial_value = (
        blocks,
        pre_act,
        hidden,
        partial_value.astype(jnp.bfloat16).reshape(slot_rows.shape),
    )
    expert_outs = from_owners(partial_value, 2)
    grad_rows = to_owners(grad_slots, 1)
    grad_blocks = grad_rows.reshape(blocks.shape)
    grad_hidden = jnp.einsum(
        "rkd,kfd->rkf", grad_blocks, weight_out, preferred_element_type=jnp.float32
    )
    _, gelu_back = jax.vjp(gelu_exact, pre_act)
    grad_pre = gelu_back(grad_hidden)[0].astype(jnp.bfloat16)
    grad_second = jnp.einsum(
        "rkf,rkd->kfd", hidden, grad_blocks, preferred_element_type=jnp.float32
    ).astype(jnp.bfloat16)
    grad_first = jnp.einsum(
        "rkd,rkf->kdf", blocks, grad_pre, preferred_element_type=jnp.float32
    ).astype(jnp.bfloat16)
    partial_back = jnp.einsum(
        "rkf,kdf->rkd", grad_pre, weight_in, preferred_element_type=jnp.float32
    )
    grad_first, grad_second, partial_back = (
        grad_first,
        grad_second,
        partial_back.astype(jnp.bfloat16).reshape(grad_rows.shape),
    )
    grad_slot_all = from_owners(partial_back, 3)
    mixed = jnp.einsum(
        "ise,ied->isd", combine, expert_outs, preferred_element_type=jnp.float32
    ).astype(jnp.bfloat16)
    grad_comb = jnp.einsum(
        "isd,ied->ise", cotangent, expert_outs, preferred_element_type=jnp.float32
    )
    grad_disp = jnp.einsum(
        "isd,ied->ise", tokens, grad_slot_all, preferred_element_type=jnp.float32
    )
    part_disp = dispatch_prob * (
        grad_disp - jnp.sum(dispatch_prob * grad_disp, axis=1, keepdims=True)
    )
    part_comb = combine_prob * (
        grad_comb - jnp.sum(combine_prob * grad_comb, axis=2, keepdims=True)
    )
    grad_logits = (part_disp + part_comb).astype(jnp.bfloat16)
    grad_tokens = (
        jnp.einsum("ise,ied->isd", dispatch, grad_slot_all, preferred_element_type=jnp.float32)
        + jnp.einsum("ise,de->isd", grad_logits, router, preferred_element_type=jnp.float32)
    ).astype(jnp.bfloat16)
    router_term = jnp.einsum("isd,ise->de", tokens, grad_logits, preferred_element_type=jnp.float32)
    grad_router = all_sum(router_term, n_dp, n_expert)
    return (mixed, grad_tokens, grad_router, grad_first, grad_second)


def solution(mesh):
    return jax.shard_map(
        functools.partial(local, mesh.shape["dp"], mesh.shape["expert"]),
        mesh=mesh,
        in_specs=(
            P(("dp", "expert"), None, None),
            P(),
            P("expert", None, "dp"),
            P("expert", "dp", None),
            P(("dp", "expert"), None, None),
        ),
        out_specs=(
            P(("dp", "expert"), None, None),
            P(("dp", "expert"), None, None),
            P(),
            P("expert", None, "dp"),
            P("expert", "dp", None),
        ),
        check_vma=False,
    )
```

```python
import functools

import jax
import jax.numpy as jnp
from jax import lax
from jax.experimental import pallas as pl
from jax.experimental.pallas import tpu as pltpu
from jax.sharding import PartitionSpec as P


def _exchange_kernel(axis, other, n, gather, x_ref, o_ref, land, send_sem, recv_sem):
    me = lax.axis_index(axis)
    fixed = lax.axis_index(other)

    def peer(j):
        if axis == "dp":
            return (j, fixed)
        return (fixed, j)

    barrier = pltpu.get_barrier_semaphore()

    @pl.loop(0, n)
    def _(j):
        @pl.when(j != me)
        def _():
            pl.semaphore_signal(barrier, inc=1, device_id=peer(j), device_id_type=pl.DeviceIdType.MESH)

    pl.semaphore_wait(barrier, n - 1)

    def copy_to(j):
        src = x_ref if gather else x_ref.at[j]
        return pltpu.make_async_remote_copy(
            src_ref=src,
            dst_ref=land.at[me],
            send_sem=send_sem.at[j],
            recv_sem=recv_sem.at[me],
            device_id=peer(j),
            device_id_type=pl.DeviceIdType.MESH,
        )

    @pl.loop(0, n)
    def _(j):
        @pl.when(j != me)
        def _():
            copy_to(j).start()

    own = x_ref[...] if gather else x_ref[me]
    o_ref[me] = own

    def arrived(j):
        src = x_ref if gather else x_ref.at[j]
        return pltpu.make_async_remote_copy(
            src_ref=src,
            dst_ref=land.at[j],
            send_sem=send_sem.at[j],
            recv_sem=recv_sem.at[j],
            device_id=peer(j),
            device_id_type=pl.DeviceIdType.MESH,
        )

    @pl.loop(0, n)
    def _(j):
        @pl.when(j != me)
        def _():
            arrived(j).wait_recv()
            o_ref[j] = land[j]
            copy_to(j).wait_send()


def exchange(x, axis, n, collective_id, gather=False):
    other = "expert" if axis == "dp" else "dp"
    block = x.shape if gather else x.shape[1:]
    out_shape = jax.ShapeDtypeStruct((n,) + tuple(block), x.dtype)
    return pl.pallas_call(
        functools.partial(_exchange_kernel, axis, other, n, gather),
        out_shape=out_shape,
        in_specs=[pl.BlockSpec(memory_space=pltpu.VMEM)],
        out_specs=pl.BlockSpec(memory_space=pltpu.VMEM),
        scratch_shapes=[
            pltpu.VMEM(out_shape.shape, x.dtype),
            pltpu.SemaphoreType.DMA((n,)),
            pltpu.SemaphoreType.DMA((n,)),
        ],
        compiler_params=pltpu.CompilerParams(collective_id=collective_id, has_side_effects=True),
    )(x)


def gelu_exact(values):
    return jax.nn.gelu(values, approximate=False)


def _relay_sum_kernel(n_chip, x_ref, o_ref, land1, pair, land2, s1, r1, s2, r2):
    me = lax.axis_index("dp")
    fixed = lax.axis_index("expert")
    core = me % 2
    chip = me // 2
    partner = me + 1 - 2 * core
    mesh_id = pl.DeviceIdType.MESH
    barrier = pltpu.get_barrier_semaphore()
    pl.semaphore_signal(barrier, inc=1, device_id=(partner, fixed), device_id_type=mesh_id)
    for h in range(n_chip):
        @pl.when(h != chip)
        def _():
            pl.semaphore_signal(barrier, inc=1, device_id=(2 * h + core, fixed), device_id_type=mesh_id)
    pl.semaphore_wait(barrier, n_chip)

    def to_partner(h):
        return pltpu.make_async_remote_copy(
            src_ref=x_ref.at[2 * h + 1 - core], dst_ref=land1.at[h], send_sem=s1.at[h], recv_sem=r1.at[h],
            device_id=(partner, fixed), device_id_type=mesh_id)

    for h in range(n_chip):
        to_partner(h).start()
    for h in range(n_chip):
        to_partner(h).wait_recv()
        pair[h] = (x_ref[2 * h + core].astype(jnp.float32) + land1[h].astype(jnp.float32)).astype(pair.dtype)
        to_partner(h).wait_send()

    def to_chip(h, slot):
        return pltpu.make_async_remote_copy(
            src_ref=pair.at[h], dst_ref=land2.at[slot], send_sem=s2.at[h], recv_sem=r2.at[slot],
            device_id=(2 * h + core, fixed), device_id_type=mesh_id)

    for h in range(n_chip):
        @pl.when(h != chip)
        def _():
            to_chip(h, chip).start()
    land2[chip] = pair[chip]
    for h in range(n_chip):
        @pl.when(h != chip)
        def _():
            to_chip(h, h).wait_recv()
            to_chip(h, chip).wait_send()
    total = land2[0].astype(jnp.float32)
    for h in range(1, n_chip):
        total = total + land2[h].astype(jnp.float32)
    o_ref[...] = total.astype(o_ref.dtype)


def relay_sum(x, collective_id):
    n_dp = x.shape[0]
    n_chip = n_dp // 2
    block = x.shape[1:]
    return pl.pallas_call(
        functools.partial(_relay_sum_kernel, n_chip),
        out_shape=jax.ShapeDtypeStruct(block, x.dtype),
        in_specs=[pl.BlockSpec(memory_space=pltpu.VMEM)],
        out_specs=pl.BlockSpec(memory_space=pltpu.VMEM),
        scratch_shapes=[
            pltpu.VMEM((n_chip,) + block, x.dtype),
            pltpu.VMEM((n_chip,) + block, x.dtype),
            pltpu.VMEM((n_chip,) + block, x.dtype),
            pltpu.SemaphoreType.DMA((n_chip,)),
            pltpu.SemaphoreType.DMA((n_chip,)),
            pltpu.SemaphoreType.DMA((n_chip,)),
            pltpu.SemaphoreType.DMA((n_chip,)),
        ],
        compiler_params=pltpu.CompilerParams(collective_id=collective_id, has_side_effects=True),
    )(x)


def _allsum_kernel(n_dp, n_ex, x_ref, o_ref, land1, land2, land3, red1, red2, s1, r1, s2, r2, s3, r3):
    me_d = lax.axis_index("dp")
    me_e = lax.axis_index("expert")
    mesh_id = pl.DeviceIdType.MESH
    barrier = pltpu.get_barrier_semaphore()

    @pl.loop(0, n_ex)
    def _(j):
        @pl.when(j != me_e)
        def _():
            pl.semaphore_signal(barrier, inc=1, device_id=(me_d, j), device_id_type=mesh_id)

    @pl.loop(0, n_dp)
    def _(k):
        @pl.when(k != me_d)
        def _():
            pl.semaphore_signal(barrier, inc=1, device_id=(k, me_e), device_id_type=mesh_id)

    pl.semaphore_wait(barrier, n_ex - 1 + n_dp - 1)

    def ex_copy(src, land, send, recv, j, slot):
        return pltpu.make_async_remote_copy(
            src_ref=src, dst_ref=land.at[slot], send_sem=send.at[j], recv_sem=recv.at[slot],
            device_id=(me_d, j), device_id_type=mesh_id)

    def dp_copy(src, land, send, recv, k, slot):
        return pltpu.make_async_remote_copy(
            src_ref=src, dst_ref=land.at[slot], send_sem=send.at[k], recv_sem=recv.at[slot],
            device_id=(k, me_e), device_id_type=mesh_id)

    @pl.loop(0, n_ex)
    def _(j):
        @pl.when(j != me_e)
        def _():
            ex_copy(x_ref.at[j], land1, s1, r1, j, me_e).start()

    land1[me_e] = x_ref[me_e]

    @pl.loop(0, n_ex)
    def _(j):
        @pl.when(j != me_e)
        def _():
            ex_copy(x_ref.at[j], land1, s1, r1, j, j).wait_recv()
            ex_copy(x_ref.at[j], land1, s1, r1, j, me_e).wait_send()

    red1[...] = jnp.sum(land1[...], axis=0)

    @pl.loop(0, n_dp)
    def _(k):
        @pl.when(k != me_d)
        def _():
            dp_copy(red1, land2, s2, r2, k, me_d).start()

    land2[me_d] = red1[...]

    @pl.loop(0, n_dp)
    def _(k):
        @pl.when(k != me_d)
        def _():
            dp_copy(red1, land2, s2, r2, k, k).wait_recv()
            dp_copy(red1, land2, s2, r2, k, me_d).wait_send()

    total = land2[0]
    for k in range(1, n_dp):
        total = total + land2[k]
    red2[...] = total

    @pl.loop(0, n_ex)
    def _(j):
        @pl.when(j != me_e)
        def _():
            ex_copy(red2, land3, s3, r3, j, me_e).start()

    o_ref[me_e] = red2[...]

    @pl.loop(0, n_ex)
    def _(j):
        @pl.when(j != me_e)
        def _():
            ex_copy(red2, land3, s3, r3, j, j).wait_recv()
            o_ref[j] = land3[j]
            ex_copy(red2, land3, s3, r3, j, me_e).wait_send()


def all_sum(value, n_dp, n_expert):
    rows, cols = value.shape
    block = (rows // n_expert, cols)
    chunks = value.reshape(n_expert, *block)
    out = pl.pallas_call(
        functools.partial(_allsum_kernel, n_dp, n_expert),
        out_shape=jax.ShapeDtypeStruct(chunks.shape, value.dtype),
        in_specs=[pl.BlockSpec(memory_space=pltpu.VMEM)],
        out_specs=pl.BlockSpec(memory_space=pltpu.VMEM),
        scratch_shapes=[
            pltpu.VMEM(chunks.shape, value.dtype),
            pltpu.VMEM((n_dp,) + block, value.dtype),
            pltpu.VMEM(chunks.shape, value.dtype),
            pltpu.VMEM(block, value.dtype),
            pltpu.VMEM(block, value.dtype),
            pltpu.SemaphoreType.DMA((n_expert,)),
            pltpu.SemaphoreType.DMA((n_expert,)),
            pltpu.SemaphoreType.DMA((n_dp,)),
            pltpu.SemaphoreType.DMA((n_dp,)),
            pltpu.SemaphoreType.DMA((n_expert,)),
            pltpu.SemaphoreType.DMA((n_expert,)),
        ],
        compiler_params=pltpu.CompilerParams(collective_id=4, has_side_effects=True),
    )(chunks)
    return out.reshape(rows, cols)


def local(n_dp, n_expert, tokens, router, weight_in, weight_out, cotangent):
    experts_dev = weight_in.shape[0]
    width = tokens.shape[2]
    logits = jnp.einsum("isd,de->ise", tokens, router, preferred_element_type=jnp.float32)
    dispatch_prob = jax.nn.softmax(logits, axis=1)
    combine_prob = jax.nn.softmax(logits, axis=2)
    dispatch = dispatch_prob.astype(jnp.bfloat16)
    combine = combine_prob.astype(jnp.bfloat16)
    slots = jnp.einsum("ise,isd->ied", dispatch, tokens, preferred_element_type=jnp.float32).astype(
        jnp.bfloat16
    )
    grad_slots = jnp.einsum(
        "ise,isd->ied", combine, cotangent, preferred_element_type=jnp.float32
    ).astype(jnp.bfloat16)

    def to_owners(local_rows, cid):
        chunks = local_rows.reshape(n_expert, experts_dev, width)
        arrived = exchange(chunks, "expert", n_expert, cid).reshape(local_rows.shape)
        return lax.all_gather(arrived, "dp", axis=0, tiled=True)

    def from_owners(partial_value, cid):
        summed = relay_sum(partial_value, cid + 8)
        chunks = summed.reshape(n_expert, experts_dev, width)
        return exchange(chunks, "expert", n_expert, cid).reshape(1, *summed.shape)

    slot_rows = to_owners(slots, 0)
    blocks = slot_rows.reshape(-1, experts_dev, width)
    pre_act = jnp.einsum("rkd,kdf->rkf", blocks, weight_in, preferred_element_type=jnp.float32)
    hidden = gelu_exact(pre_act).astype(jnp.bfloat16)
    partial_value = jnp.einsum(
        "rkf,kfd->rkd", hidden, weight_out, preferred_element_type=jnp.float32
    )
    blocks, pre_act, hidden, partial_value = (
        blocks,
        pre_act,
        hidden,
        partial_value.astype(jnp.bfloat16).reshape(slot_rows.shape),
    )
    expert_outs = from_owners(partial_value, 2)
    grad_rows = to_owners(grad_slots, 1)
    grad_blocks = grad_rows.reshape(blocks.shape)
    grad_hidden = jnp.einsum(
        "rkd,kfd->rkf", grad_blocks, weight_out, preferred_element_type=jnp.float32
    )
    _, gelu_back = jax.vjp(gelu_exact, pre_act)
    grad_pre = gelu_back(grad_hidden)[0].astype(jnp.bfloat16)
    grad_second = jnp.einsum(
        "rkf,rkd->kfd", hidden, grad_blocks, preferred_element_type=jnp.float32
    ).astype(jnp.bfloat16)
    grad_first = jnp.einsum(
        "rkd,rkf->kdf", blocks, grad_pre, preferred_element_type=jnp.float32
    ).astype(jnp.bfloat16)
    partial_back = jnp.einsum(
        "rkf,kdf->rkd", grad_pre, weight_in, preferred_element_type=jnp.float32
    )
    grad_first, grad_second, partial_back = (
        grad_first,
        grad_second,
        partial_back.astype(jnp.bfloat16).reshape(grad_rows.shape),
    )
    grad_slot_all = from_owners(partial_back, 3)
    mixed = jnp.einsum(
        "ise,ied->isd", combine, expert_outs, preferred_element_type=jnp.float32
    ).astype(jnp.bfloat16)
    grad_comb = jnp.einsum(
        "isd,ied->ise", cotangent, expert_outs, preferred_element_type=jnp.float32
    )
    grad_disp = jnp.einsum(
        "isd,ied->ise", tokens, grad_slot_all, preferred_element_type=jnp.float32
    )
    part_disp = dispatch_prob * (
        grad_disp - jnp.sum(dispatch_prob * grad_disp, axis=1, keepdims=True)
    )
    part_comb = combine_prob * (
        grad_comb - jnp.sum(combine_prob * grad_comb, axis=2, keepdims=True)
    )
    grad_logits = (part_disp + part_comb).astype(jnp.bfloat16)
    grad_tokens = (
        jnp.einsum("ise,ied->isd", dispatch, grad_slot_all, preferred_element_type=jnp.float32)
        + jnp.einsum("ise,de->isd", grad_logits, router, preferred_element_type=jnp.float32)
    ).astype(jnp.bfloat16)
    router_term = jnp.einsum("isd,ise->de", tokens, grad_logits, preferred_element_type=jnp.float32)
    grad_router = all_sum(router_term, n_dp, n_expert)
    return (mixed, grad_tokens, grad_router, grad_first, grad_second)


def solution(mesh):
    return jax.shard_map(
        functools.partial(local, mesh.shape["dp"], mesh.shape["expert"]),
        mesh=mesh,
        in_specs=(
            P(("dp", "expert"), None, None),
            P(),
            P("expert", None, "dp"),
            P("expert", "dp", None),
            P(("dp", "expert"), None, None),
        ),
        out_specs=(
            P(("dp", "expert"), None, None),
            P(("dp", "expert"), None, None),
            P(),
            P("expert", None, "dp"),
            P("expert", "dp", None),
        ),
        check_vma=False,
    )
```

```python
import functools

import jax
import jax.numpy as jnp
from jax import lax
from jax.experimental import pallas as pl
from jax.experimental.pallas import tpu as pltpu
from jax.sharding import PartitionSpec as P


def _exchange_kernel(axis, other, n, gather, x_ref, o_ref, land, send_sem, recv_sem):
    me = lax.axis_index(axis)
    fixed = lax.axis_index(other)

    def peer(j):
        if axis == "dp":
            return (j, fixed)
        return (fixed, j)

    barrier = pltpu.get_barrier_semaphore()

    @pl.loop(0, n)
    def _(j):
        @pl.when(j != me)
        def _():
            pl.semaphore_signal(barrier, inc=1, device_id=peer(j), device_id_type=pl.DeviceIdType.MESH)

    pl.semaphore_wait(barrier, n - 1)

    def copy_to(j):
        src = x_ref if gather else x_ref.at[j]
        return pltpu.make_async_remote_copy(
            src_ref=src,
            dst_ref=land.at[me],
            send_sem=send_sem.at[j],
            recv_sem=recv_sem.at[me],
            device_id=peer(j),
            device_id_type=pl.DeviceIdType.MESH,
        )

    @pl.loop(0, n)
    def _(j):
        @pl.when(j != me)
        def _():
            copy_to(j).start()

    own = x_ref[...] if gather else x_ref[me]
    o_ref[me] = own

    def arrived(j):
        src = x_ref if gather else x_ref.at[j]
        return pltpu.make_async_remote_copy(
            src_ref=src,
            dst_ref=land.at[j],
            send_sem=send_sem.at[j],
            recv_sem=recv_sem.at[j],
            device_id=peer(j),
            device_id_type=pl.DeviceIdType.MESH,
        )

    @pl.loop(0, n)
    def _(j):
        @pl.when(j != me)
        def _():
            arrived(j).wait_recv()
            o_ref[j] = land[j]
            copy_to(j).wait_send()


def exchange(x, axis, n, collective_id, gather=False):
    other = "expert" if axis == "dp" else "dp"
    block = x.shape if gather else x.shape[1:]
    out_shape = jax.ShapeDtypeStruct((n,) + tuple(block), x.dtype)
    return pl.pallas_call(
        functools.partial(_exchange_kernel, axis, other, n, gather),
        out_shape=out_shape,
        in_specs=[pl.BlockSpec(memory_space=pltpu.VMEM)],
        out_specs=pl.BlockSpec(memory_space=pltpu.VMEM),
        scratch_shapes=[
            pltpu.VMEM(out_shape.shape, x.dtype),
            pltpu.SemaphoreType.DMA((n,)),
            pltpu.SemaphoreType.DMA((n,)),
        ],
        compiler_params=pltpu.CompilerParams(collective_id=collective_id, has_side_effects=True),
    )(x)


def gelu_exact(values):
    return jax.nn.gelu(values, approximate=False)


def _relay_sum_kernel(n_chip, x_ref, o_ref, land1, pair, land2, s1, r1, s2, r2):
    me = lax.axis_index("dp")
    fixed = lax.axis_index("expert")
    core = me % 2
    chip = me // 2
    partner = me + 1 - 2 * core
    mesh_id = pl.DeviceIdType.MESH
    barrier = pltpu.get_barrier_semaphore()
    pl.semaphore_signal(barrier, inc=1, device_id=(partner, fixed), device_id_type=mesh_id)
    for h in range(n_chip):
        @pl.when(h != chip)
        def _():
            pl.semaphore_signal(barrier, inc=1, device_id=(2 * h + core, fixed), device_id_type=mesh_id)
    pl.semaphore_wait(barrier, n_chip)

    def to_partner(h):
        return pltpu.make_async_remote_copy(
            src_ref=x_ref.at[2 * h + 1 - core], dst_ref=land1.at[h], send_sem=s1.at[h], recv_sem=r1.at[h],
            device_id=(partner, fixed), device_id_type=mesh_id)

    for h in range(n_chip):
        to_partner(h).start()
    for h in range(n_chip):
        to_partner(h).wait_recv()
        pair[h] = (x_ref[2 * h + core].astype(jnp.float32) + land1[h].astype(jnp.float32)).astype(pair.dtype)
        to_partner(h).wait_send()

    def to_chip(h, slot):
        return pltpu.make_async_remote_copy(
            src_ref=pair.at[h], dst_ref=land2.at[slot], send_sem=s2.at[h], recv_sem=r2.at[slot],
            device_id=(2 * h + core, fixed), device_id_type=mesh_id)

    for h in range(n_chip):
        @pl.when(h != chip)
        def _():
            to_chip(h, chip).start()
    land2[chip] = pair[chip]
    for h in range(n_chip):
        @pl.when(h != chip)
        def _():
            to_chip(h, h).wait_recv()
            to_chip(h, chip).wait_send()
    total = land2[0].astype(jnp.float32)
    for h in range(1, n_chip):
        total = total + land2[h].astype(jnp.float32)
    o_ref[...] = total.astype(o_ref.dtype)


def relay_sum(x, collective_id):
    n_dp = x.shape[0]
    n_chip = n_dp // 2
    block = x.shape[1:]
    return pl.pallas_call(
        functools.partial(_relay_sum_kernel, n_chip),
        out_shape=jax.ShapeDtypeStruct(block, x.dtype),
        in_specs=[pl.BlockSpec(memory_space=pltpu.VMEM)],
        out_specs=pl.BlockSpec(memory_space=pltpu.VMEM),
        scratch_shapes=[
            pltpu.VMEM((n_chip,) + block, x.dtype),
            pltpu.VMEM((n_chip,) + block, x.dtype),
            pltpu.VMEM((n_chip,) + block, x.dtype),
            pltpu.SemaphoreType.DMA((n_chip,)),
            pltpu.SemaphoreType.DMA((n_chip,)),
            pltpu.SemaphoreType.DMA((n_chip,)),
            pltpu.SemaphoreType.DMA((n_chip,)),
        ],
        compiler_params=pltpu.CompilerParams(collective_id=collective_id, has_side_effects=True),
    )(x)


def _relay_gather_kernel(n_chip, x_ref, o_ref, land, s_off, s_fwd, recv):
    me = lax.axis_index("dp")
    fixed = lax.axis_index("expert")
    core = me % 2
    chip = me // 2
    partner = me + 1 - 2 * core
    mesh_id = pl.DeviceIdType.MESH
    barrier = pltpu.get_barrier_semaphore()
    pl.semaphore_signal(barrier, inc=1, device_id=(partner, fixed), device_id_type=mesh_id)
    for h in range(n_chip):
        @pl.when(h != chip)
        def _():
            pl.semaphore_signal(barrier, inc=1, device_id=(2 * h + core, fixed), device_id_type=mesh_id)
    pl.semaphore_wait(barrier, n_chip)

    def off_chip(h, slot):
        return pltpu.make_async_remote_copy(
            src_ref=x_ref, dst_ref=land.at[slot], send_sem=s_off.at[h], recv_sem=recv.at[slot],
            device_id=(2 * h + core, fixed), device_id_type=mesh_id)

    def on_chip(h, slot):
        src = x_ref if h is None else land.at[slot]
        return pltpu.make_async_remote_copy(
            src_ref=src, dst_ref=land.at[slot], send_sem=s_fwd.at[slot], recv_sem=recv.at[slot],
            device_id=(partner, fixed), device_id_type=mesh_id)

    for h in range(n_chip):
        @pl.when(h != chip)
        def _():
            off_chip(h, me).start()
    on_chip(None, me).start()
    o_ref[me] = x_ref[...]
    for h in range(n_chip):
        @pl.when(h != chip)
        def _():
            slot = 2 * h + core
            off_chip(h, slot).wait_recv()
            on_chip(h, slot).start()
            o_ref[slot] = land[slot]
    for h in range(n_chip):
        slot = 2 * h + 1 - core
        on_chip(h, slot).wait_recv()
        o_ref[slot] = land[slot]
    for h in range(n_chip):
        @pl.when(h != chip)
        def _():
            off_chip(h, me).wait_send()
            on_chip(h, 2 * h + core).wait_send()
    on_chip(None, me).wait_send()


def relay_gather(x, n_dp, collective_id):
    n_chip = n_dp // 2
    return pl.pallas_call(
        functools.partial(_relay_gather_kernel, n_chip),
        out_shape=jax.ShapeDtypeStruct((n_dp,) + x.shape, x.dtype),
        in_specs=[pl.BlockSpec(memory_space=pltpu.VMEM)],
        out_specs=pl.BlockSpec(memory_space=pltpu.VMEM),
        scratch_shapes=[
            pltpu.VMEM((n_dp,) + x.shape, x.dtype),
            pltpu.SemaphoreType.DMA((n_chip,)),
            pltpu.SemaphoreType.DMA((n_dp,)),
            pltpu.SemaphoreType.DMA((n_dp,)),
        ],
        compiler_params=pltpu.CompilerParams(collective_id=collective_id, has_side_effects=True),
    )(x)


def _allsum_kernel(n_dp, n_ex, x_ref, o_ref, land1, land2, land3, red1, red2, s1, r1, s2, r2, s3, r3):
    me_d = lax.axis_index("dp")
    me_e = lax.axis_index("expert")
    mesh_id = pl.DeviceIdType.MESH
    barrier = pltpu.get_barrier_semaphore()

    @pl.loop(0, n_ex)
    def _(j):
        @pl.when(j != me_e)
        def _():
            pl.semaphore_signal(barrier, inc=1, device_id=(me_d, j), device_id_type=mesh_id)

    @pl.loop(0, n_dp)
    def _(k):
        @pl.when(k != me_d)
        def _():
            pl.semaphore_signal(barrier, inc=1, device_id=(k, me_e), device_id_type=mesh_id)

    pl.semaphore_wait(barrier, n_ex - 1 + n_dp - 1)

    def ex_copy(src, land, send, recv, j, slot):
        return pltpu.make_async_remote_copy(
            src_ref=src, dst_ref=land.at[slot], send_sem=send.at[j], recv_sem=recv.at[slot],
            device_id=(me_d, j), device_id_type=mesh_id)

    def dp_copy(src, land, send, recv, k, slot):
        return pltpu.make_async_remote_copy(
            src_ref=src, dst_ref=land.at[slot], send_sem=send.at[k], recv_sem=recv.at[slot],
            device_id=(k, me_e), device_id_type=mesh_id)

    @pl.loop(0, n_ex)
    def _(j):
        @pl.when(j != me_e)
        def _():
            ex_copy(x_ref.at[j], land1, s1, r1, j, me_e).start()

    land1[me_e] = x_ref[me_e]

    @pl.loop(0, n_ex)
    def _(j):
        @pl.when(j != me_e)
        def _():
            ex_copy(x_ref.at[j], land1, s1, r1, j, j).wait_recv()
            ex_copy(x_ref.at[j], land1, s1, r1, j, me_e).wait_send()

    red1[...] = jnp.sum(land1[...], axis=0)

    @pl.loop(0, n_dp)
    def _(k):
        @pl.when(k != me_d)
        def _():
            dp_copy(red1, land2, s2, r2, k, me_d).start()

    land2[me_d] = red1[...]

    @pl.loop(0, n_dp)
    def _(k):
        @pl.when(k != me_d)
        def _():
            dp_copy(red1, land2, s2, r2, k, k).wait_recv()
            dp_copy(red1, land2, s2, r2, k, me_d).wait_send()

    total = land2[0]
    for k in range(1, n_dp):
        total = total + land2[k]
    red2[...] = total

    @pl.loop(0, n_ex)
    def _(j):
        @pl.when(j != me_e)
        def _():
            ex_copy(red2, land3, s3, r3, j, me_e).start()

    o_ref[me_e] = red2[...]

    @pl.loop(0, n_ex)
    def _(j):
        @pl.when(j != me_e)
        def _():
            ex_copy(red2, land3, s3, r3, j, j).wait_recv()
            o_ref[j] = land3[j]
            ex_copy(red2, land3, s3, r3, j, me_e).wait_send()


def all_sum(value, n_dp, n_expert):
    rows, cols = value.shape
    block = (rows // n_expert, cols)
    chunks = value.reshape(n_expert, *block)
    out = pl.pallas_call(
        functools.partial(_allsum_kernel, n_dp, n_expert),
        out_shape=jax.ShapeDtypeStruct(chunks.shape, value.dtype),
        in_specs=[pl.BlockSpec(memory_space=pltpu.VMEM)],
        out_specs=pl.BlockSpec(memory_space=pltpu.VMEM),
        scratch_shapes=[
            pltpu.VMEM(chunks.shape, value.dtype),
            pltpu.VMEM((n_dp,) + block, value.dtype),
            pltpu.VMEM(chunks.shape, value.dtype),
            pltpu.VMEM(block, value.dtype),
            pltpu.VMEM(block, value.dtype),
            pltpu.SemaphoreType.DMA((n_expert,)),
            pltpu.SemaphoreType.DMA((n_expert,)),
            pltpu.SemaphoreType.DMA((n_dp,)),
            pltpu.SemaphoreType.DMA((n_dp,)),
            pltpu.SemaphoreType.DMA((n_expert,)),
            pltpu.SemaphoreType.DMA((n_expert,)),
        ],
        compiler_params=pltpu.CompilerParams(collective_id=4, has_side_effects=True),
    )(chunks)
    return out.reshape(rows, cols)


def local(n_dp, n_expert, tokens, router, weight_in, weight_out, cotangent):
    experts_dev = weight_in.shape[0]
    width = tokens.shape[2]
    logits = jnp.einsum("isd,de->ise", tokens, router, preferred_element_type=jnp.float32)
    dispatch_prob = jax.nn.softmax(logits, axis=1)
    combine_prob = jax.nn.softmax(logits, axis=2)
    dispatch = dispatch_prob.astype(jnp.bfloat16)
    combine = combine_prob.astype(jnp.bfloat16)
    slots = jnp.einsum("ise,isd->ied", dispatch, tokens, preferred_element_type=jnp.float32).astype(
        jnp.bfloat16
    )
    grad_slots = jnp.einsum(
        "ise,isd->ied", combine, cotangent, preferred_element_type=jnp.float32
    ).astype(jnp.bfloat16)

    def to_owners(local_rows, cid):
        chunks = local_rows.reshape(n_expert, experts_dev, width)
        arrived = exchange(chunks, "expert", n_expert, cid).reshape(local_rows.shape)
        return relay_gather(arrived[0], n_dp, cid + 12)

    def from_owners(partial_value, cid):
        summed = relay_sum(partial_value, cid + 8)
        chunks = summed.reshape(n_expert, experts_dev, width)
        return exchange(chunks, "expert", n_expert, cid).reshape(1, *summed.shape)

    slot_rows = to_owners(slots, 0)
    blocks = slot_rows.reshape(-1, experts_dev, width)
    pre_act = jnp.einsum("rkd,kdf->rkf", blocks, weight_in, preferred_element_type=jnp.float32)
    hidden = gelu_exact(pre_act).astype(jnp.bfloat16)
    partial_value = jnp.einsum(
        "rkf,kfd->rkd", hidden, weight_out, preferred_element_type=jnp.float32
    )
    blocks, pre_act, hidden, partial_value = (
        blocks,
        pre_act,
        hidden,
        partial_value.astype(jnp.bfloat16).reshape(slot_rows.shape),
    )
    expert_outs = from_owners(partial_value, 2)
    grad_rows = to_owners(grad_slots, 1)
    grad_blocks = grad_rows.reshape(blocks.shape)
    grad_hidden = jnp.einsum(
        "rkd,kfd->rkf", grad_blocks, weight_out, preferred_element_type=jnp.float32
    )
    _, gelu_back = jax.vjp(gelu_exact, pre_act)
    grad_pre = gelu_back(grad_hidden)[0].astype(jnp.bfloat16)
    grad_second = jnp.einsum(
        "rkf,rkd->kfd", hidden, grad_blocks, preferred_element_type=jnp.float32
    ).astype(jnp.bfloat16)
    grad_first = jnp.einsum(
        "rkd,rkf->kdf", blocks, grad_pre, preferred_element_type=jnp.float32
    ).astype(jnp.bfloat16)
    partial_back = jnp.einsum(
        "rkf,kdf->rkd", grad_pre, weight_in, preferred_element_type=jnp.float32
    )
    grad_first, grad_second, partial_back = (
        grad_first,
        grad_second,
        partial_back.astype(jnp.bfloat16).reshape(grad_rows.shape),
    )
    grad_slot_all = from_owners(partial_back, 3)
    mixed = jnp.einsum(
        "ise,ied->isd", combine, expert_outs, preferred_element_type=jnp.float32
    ).astype(jnp.bfloat16)
    grad_comb = jnp.einsum(
        "isd,ied->ise", cotangent, expert_outs, preferred_element_type=jnp.float32
    )
    grad_disp = jnp.einsum(
        "isd,ied->ise", tokens, grad_slot_all, preferred_element_type=jnp.float32
    )
    part_disp = dispatch_prob * (
        grad_disp - jnp.sum(dispatch_prob * grad_disp, axis=1, keepdims=True)
    )
    part_comb = combine_prob * (
        grad_comb - jnp.sum(combine_prob * grad_comb, axis=2, keepdims=True)
    )
    grad_logits = (part_disp + part_comb).astype(jnp.bfloat16)
    grad_tokens = (
        jnp.einsum("ise,ied->isd", dispatch, grad_slot_all, preferred_element_type=jnp.float32)
        + jnp.einsum("ise,de->isd", grad_logits, router, preferred_element_type=jnp.float32)
    ).astype(jnp.bfloat16)
    router_term = jnp.einsum("isd,ise->de", tokens, grad_logits, preferred_element_type=jnp.float32)
    grad_router = all_sum(router_term, n_dp, n_expert)
    return (mixed, grad_tokens, grad_router, grad_first, grad_second)


def solution(mesh):
    return jax.shard_map(
        functools.partial(local, mesh.shape["dp"], mesh.shape["expert"]),
        mesh=mesh,
        in_specs=(
            P(("dp", "expert"), None, None),
            P(),
            P("expert", None, "dp"),
            P("expert", "dp", None),
            P(("dp", "expert"), None, None),
        ),
        out_specs=(
            P(("dp", "expert"), None, None),
            P(("dp", "expert"), None, None),
            P(),
            P("expert", None, "dp"),
            P("expert", "dp", None),
        ),
        check_vma=False,
    )
```

```python
import functools

import jax
import jax.numpy as jnp
from jax import lax
from jax.experimental import pallas as pl
from jax.experimental.pallas import tpu as pltpu
from jax.sharding import PartitionSpec as P


def _exchange_kernel(axis, other, n, gather, x_ref, o_ref, land, send_sem, recv_sem):
    me = lax.axis_index(axis)
    fixed = lax.axis_index(other)

    def peer(j):
        if axis == "dp":
            return (j, fixed)
        return (fixed, j)

    barrier = pltpu.get_barrier_semaphore()

    @pl.loop(0, n)
    def _(j):
        @pl.when(j != me)
        def _():
            pl.semaphore_signal(barrier, inc=1, device_id=peer(j), device_id_type=pl.DeviceIdType.MESH)

    pl.semaphore_wait(barrier, n - 1)

    def copy_to(j):
        src = x_ref if gather else x_ref.at[j]
        return pltpu.make_async_remote_copy(
            src_ref=src,
            dst_ref=land.at[me],
            send_sem=send_sem.at[j],
            recv_sem=recv_sem.at[me],
            device_id=peer(j),
            device_id_type=pl.DeviceIdType.MESH,
        )

    @pl.loop(0, n)
    def _(j):
        @pl.when(j != me)
        def _():
            copy_to(j).start()

    own = x_ref[...] if gather else x_ref[me]
    o_ref[me] = own

    def arrived(j):
        src = x_ref if gather else x_ref.at[j]
        return pltpu.make_async_remote_copy(
            src_ref=src,
            dst_ref=land.at[j],
            send_sem=send_sem.at[j],
            recv_sem=recv_sem.at[j],
            device_id=peer(j),
            device_id_type=pl.DeviceIdType.MESH,
        )

    @pl.loop(0, n)
    def _(j):
        @pl.when(j != me)
        def _():
            arrived(j).wait_recv()
            o_ref[j] = land[j]
            copy_to(j).wait_send()


def exchange(x, axis, n, collective_id, gather=False):
    other = "expert" if axis == "dp" else "dp"
    block = x.shape if gather else x.shape[1:]
    out_shape = jax.ShapeDtypeStruct((n,) + tuple(block), x.dtype)
    return pl.pallas_call(
        functools.partial(_exchange_kernel, axis, other, n, gather),
        out_shape=out_shape,
        in_specs=[pl.BlockSpec(memory_space=pltpu.VMEM)],
        out_specs=pl.BlockSpec(memory_space=pltpu.VMEM),
        scratch_shapes=[
            pltpu.VMEM(out_shape.shape, x.dtype),
            pltpu.SemaphoreType.DMA((n,)),
            pltpu.SemaphoreType.DMA((n,)),
        ],
        compiler_params=pltpu.CompilerParams(collective_id=collective_id, has_side_effects=True),
    )(x)


def gelu_exact(values):
    return jax.nn.gelu(values, approximate=False)


def _relay_gather_kernel(n_chip, x_ref, o_ref, land, s_off, s_fwd, recv):
    me = lax.axis_index("dp")
    fixed = lax.axis_index("expert")
    core = me % 2
    chip = me // 2
    partner = me + 1 - 2 * core
    mesh_id = pl.DeviceIdType.MESH
    barrier = pltpu.get_barrier_semaphore()
    pl.semaphore_signal(barrier, inc=1, device_id=(partner, fixed), device_id_type=mesh_id)
    for h in range(n_chip):
        @pl.when(h != chip)
        def _():
            pl.semaphore_signal(barrier, inc=1, device_id=(2 * h + core, fixed), device_id_type=mesh_id)
    pl.semaphore_wait(barrier, n_chip)

    def off_chip(h, slot):
        return pltpu.make_async_remote_copy(
            src_ref=x_ref, dst_ref=land.at[slot], send_sem=s_off.at[h], recv_sem=recv.at[slot],
            device_id=(2 * h + core, fixed), device_id_type=mesh_id)

    def on_chip(h, slot):
        src = x_ref if h is None else land.at[slot]
        return pltpu.make_async_remote_copy(
            src_ref=src, dst_ref=land.at[slot], send_sem=s_fwd.at[slot], recv_sem=recv.at[slot],
            device_id=(partner, fixed), device_id_type=mesh_id)

    for h in range(n_chip):
        @pl.when(h != chip)
        def _():
            off_chip(h, me).start()
    on_chip(None, me).start()
    o_ref[me] = x_ref[...]
    for h in range(n_chip):
        @pl.when(h != chip)
        def _():
            slot = 2 * h + core
            off_chip(h, slot).wait_recv()
            on_chip(h, slot).start()
            o_ref[slot] = land[slot]
    for h in range(n_chip):
        slot = 2 * h + 1 - core
        on_chip(h, slot).wait_recv()
        o_ref[slot] = land[slot]
    for h in range(n_chip):
        @pl.when(h != chip)
        def _():
            off_chip(h, me).wait_send()
            on_chip(h, 2 * h + core).wait_send()
    on_chip(None, me).wait_send()


def relay_gather(x, n_dp, collective_id):
    n_chip = n_dp // 2
    return pl.pallas_call(
        functools.partial(_relay_gather_kernel, n_chip),
        out_shape=jax.ShapeDtypeStruct((n_dp,) + x.shape, x.dtype),
        in_specs=[pl.BlockSpec(memory_space=pltpu.VMEM)],
        out_specs=pl.BlockSpec(memory_space=pltpu.VMEM),
        scratch_shapes=[
            pltpu.VMEM((n_dp,) + x.shape, x.dtype),
            pltpu.SemaphoreType.DMA((n_chip,)),
            pltpu.SemaphoreType.DMA((n_dp,)),
            pltpu.SemaphoreType.DMA((n_dp,)),
        ],
        compiler_params=pltpu.CompilerParams(collective_id=collective_id, has_side_effects=True),
    )(x)


def _allsum_kernel(n_dp, n_ex, x_ref, o_ref, land1, land2, land3, red1, red2, s1, r1, s2, r2, s3, r3):
    me_d = lax.axis_index("dp")
    me_e = lax.axis_index("expert")
    mesh_id = pl.DeviceIdType.MESH
    barrier = pltpu.get_barrier_semaphore()

    @pl.loop(0, n_ex)
    def _(j):
        @pl.when(j != me_e)
        def _():
            pl.semaphore_signal(barrier, inc=1, device_id=(me_d, j), device_id_type=mesh_id)

    @pl.loop(0, n_dp)
    def _(k):
        @pl.when(k != me_d)
        def _():
            pl.semaphore_signal(barrier, inc=1, device_id=(k, me_e), device_id_type=mesh_id)

    pl.semaphore_wait(barrier, n_ex - 1 + n_dp - 1)

    def ex_copy(src, land, send, recv, j, slot):
        return pltpu.make_async_remote_copy(
            src_ref=src, dst_ref=land.at[slot], send_sem=send.at[j], recv_sem=recv.at[slot],
            device_id=(me_d, j), device_id_type=mesh_id)

    def dp_copy(src, land, send, recv, k, slot):
        return pltpu.make_async_remote_copy(
            src_ref=src, dst_ref=land.at[slot], send_sem=send.at[k], recv_sem=recv.at[slot],
            device_id=(k, me_e), device_id_type=mesh_id)

    @pl.loop(0, n_ex)
    def _(j):
        @pl.when(j != me_e)
        def _():
            ex_copy(x_ref.at[j], land1, s1, r1, j, me_e).start()

    land1[me_e] = x_ref[me_e]

    @pl.loop(0, n_ex)
    def _(j):
        @pl.when(j != me_e)
        def _():
            ex_copy(x_ref.at[j], land1, s1, r1, j, j).wait_recv()
            ex_copy(x_ref.at[j], land1, s1, r1, j, me_e).wait_send()

    red1[...] = jnp.sum(land1[...], axis=0)

    @pl.loop(0, n_dp)
    def _(k):
        @pl.when(k != me_d)
        def _():
            dp_copy(red1, land2, s2, r2, k, me_d).start()

    land2[me_d] = red1[...]

    @pl.loop(0, n_dp)
    def _(k):
        @pl.when(k != me_d)
        def _():
            dp_copy(red1, land2, s2, r2, k, k).wait_recv()
            dp_copy(red1, land2, s2, r2, k, me_d).wait_send()

    total = land2[0]
    for k in range(1, n_dp):
        total = total + land2[k]
    red2[...] = total

    @pl.loop(0, n_ex)
    def _(j):
        @pl.when(j != me_e)
        def _():
            ex_copy(red2, land3, s3, r3, j, me_e).start()

    o_ref[me_e] = red2[...]

    @pl.loop(0, n_ex)
    def _(j):
        @pl.when(j != me_e)
        def _():
            ex_copy(red2, land3, s3, r3, j, j).wait_recv()
            o_ref[j] = land3[j]
            ex_copy(red2, land3, s3, r3, j, me_e).wait_send()


def all_sum(value, n_dp, n_expert):
    rows, cols = value.shape
    block = (rows // n_expert, cols)
    chunks = value.reshape(n_expert, *block)
    out = pl.pallas_call(
        functools.partial(_allsum_kernel, n_dp, n_expert),
        out_shape=jax.ShapeDtypeStruct(chunks.shape, value.dtype),
        in_specs=[pl.BlockSpec(memory_space=pltpu.VMEM)],
        out_specs=pl.BlockSpec(memory_space=pltpu.VMEM),
        scratch_shapes=[
            pltpu.VMEM(chunks.shape, value.dtype),
            pltpu.VMEM((n_dp,) + block, value.dtype),
            pltpu.VMEM(chunks.shape, value.dtype),
            pltpu.VMEM(block, value.dtype),
            pltpu.VMEM(block, value.dtype),
            pltpu.SemaphoreType.DMA((n_expert,)),
            pltpu.SemaphoreType.DMA((n_expert,)),
            pltpu.SemaphoreType.DMA((n_dp,)),
            pltpu.SemaphoreType.DMA((n_dp,)),
            pltpu.SemaphoreType.DMA((n_expert,)),
            pltpu.SemaphoreType.DMA((n_expert,)),
        ],
        compiler_params=pltpu.CompilerParams(collective_id=4, has_side_effects=True),
    )(chunks)
    return out.reshape(rows, cols)


def local(n_dp, n_expert, tokens, router, weight_in, weight_out, cotangent):
    experts_dev = weight_in.shape[0]
    width = tokens.shape[2]
    logits = jnp.einsum("isd,de->ise", tokens, router, preferred_element_type=jnp.float32)
    dispatch_prob = jax.nn.softmax(logits, axis=1)
    combine_prob = jax.nn.softmax(logits, axis=2)
    dispatch = dispatch_prob.astype(jnp.bfloat16)
    combine = combine_prob.astype(jnp.bfloat16)
    slots = jnp.einsum("ise,isd->ied", dispatch, tokens, preferred_element_type=jnp.float32).astype(
        jnp.bfloat16
    )
    grad_slots = jnp.einsum(
        "ise,isd->ied", combine, cotangent, preferred_element_type=jnp.float32
    ).astype(jnp.bfloat16)

    def to_owners(local_rows, cid):
        chunks = local_rows.reshape(n_expert, experts_dev, width)
        arrived = exchange(chunks, "expert", n_expert, cid).reshape(local_rows.shape)
        if cid == 1:
            return relay_gather(arrived[0], n_dp, cid + 12)
        return lax.all_gather(arrived, "dp", axis=0, tiled=True)

    def from_owners(partial_value, cid):
        summed = lax.psum_scatter(partial_value, "dp", scatter_dimension=0, tiled=True)
        chunks = summed.reshape(n_expert, experts_dev, width)
        return exchange(chunks, "expert", n_expert, cid).reshape(summed.shape)

    slot_rows = to_owners(slots, 0)
    grad_rows = to_owners(grad_slots, 1)
    slot_rows, grad_rows = lax.optimization_barrier((slot_rows, grad_rows))
    blocks = slot_rows.reshape(-1, experts_dev, width)
    pre_act = jnp.einsum("rkd,kdf->rkf", blocks, weight_in, preferred_element_type=jnp.float32)
    hidden = gelu_exact(pre_act).astype(jnp.bfloat16)
    partial_value = jnp.einsum(
        "rkf,kfd->rkd", hidden, weight_out, preferred_element_type=jnp.float32
    )
    blocks, pre_act, hidden, partial_value = (
        blocks,
        pre_act,
        hidden,
        partial_value.astype(jnp.bfloat16).reshape(slot_rows.shape),
    )
    expert_outs = from_owners(partial_value, 2)
    grad_blocks = grad_rows.reshape(blocks.shape)
    grad_hidden = jnp.einsum(
        "rkd,kfd->rkf", grad_blocks, weight_out, preferred_element_type=jnp.float32
    )
    _, gelu_back = jax.vjp(gelu_exact, pre_act)
    grad_pre = gelu_back(grad_hidden)[0].astype(jnp.bfloat16)
    grad_second = jnp.einsum(
        "rkf,rkd->kfd", hidden, grad_blocks, preferred_element_type=jnp.float32
    ).astype(jnp.bfloat16)
    grad_first = jnp.einsum(
        "rkd,rkf->kdf", blocks, grad_pre, preferred_element_type=jnp.float32
    ).astype(jnp.bfloat16)
    partial_back = jnp.einsum(
        "rkf,kdf->rkd", grad_pre, weight_in, preferred_element_type=jnp.float32
    )
    grad_first, grad_second, partial_back = (
        grad_first,
        grad_second,
        partial_back.astype(jnp.bfloat16).reshape(grad_rows.shape),
    )
    grad_slot_all = from_owners(partial_back, 3)
    mixed = jnp.einsum(
        "ise,ied->isd", combine, expert_outs, preferred_element_type=jnp.float32
    ).astype(jnp.bfloat16)
    grad_comb = jnp.einsum(
        "isd,ied->ise", cotangent, expert_outs, preferred_element_type=jnp.float32
    )
    grad_disp = jnp.einsum(
        "isd,ied->ise", tokens, grad_slot_all, preferred_element_type=jnp.float32
    )
    part_disp = dispatch_prob * (
        grad_disp - jnp.sum(dispatch_prob * grad_disp, axis=1, keepdims=True)
    )
    part_comb = combine_prob * (
        grad_comb - jnp.sum(combine_prob * grad_comb, axis=2, keepdims=True)
    )
    grad_logits = (part_disp + part_comb).astype(jnp.bfloat16)
    grad_tokens = (
        jnp.einsum("ise,ied->isd", dispatch, grad_slot_all, preferred_element_type=jnp.float32)
        + jnp.einsum("ise,de->isd", grad_logits, router, preferred_element_type=jnp.float32)
    ).astype(jnp.bfloat16)
    router_term = jnp.einsum("isd,ise->de", tokens, grad_logits, preferred_element_type=jnp.float32)
    grad_router = all_sum(router_term, n_dp, n_expert)
    return (mixed, grad_tokens, grad_router, grad_first, grad_second)


def solution(mesh):
    return jax.shard_map(
        functools.partial(local, mesh.shape["dp"], mesh.shape["expert"]),
        mesh=mesh,
        in_specs=(
            P(("dp", "expert"), None, None),
            P(),
            P("expert", None, "dp"),
            P("expert", "dp", None),
            P(("dp", "expert"), None, None),
        ),
        out_specs=(
            P(("dp", "expert"), None, None),
            P(("dp", "expert"), None, None),
            P(),
            P("expert", None, "dp"),
            P("expert", "dp", None),
        ),
        check_vma=False,
    )
```

```python
import functools

import jax
import jax.numpy as jnp
from jax import lax
from jax.experimental import pallas as pl
from jax.experimental.pallas import tpu as pltpu
from jax.sharding import PartitionSpec as P


def _exchange_kernel(axis, other, n, gather, x_ref, o_ref, land, send_sem, recv_sem):
    me = lax.axis_index(axis)
    fixed = lax.axis_index(other)

    def peer(j):
        if axis == "dp":
            return (j, fixed)
        return (fixed, j)

    barrier = pltpu.get_barrier_semaphore()

    @pl.loop(0, n)
    def _(j):
        @pl.when(j != me)
        def _():
            pl.semaphore_signal(barrier, inc=1, device_id=peer(j), device_id_type=pl.DeviceIdType.MESH)

    pl.semaphore_wait(barrier, n - 1)

    def copy_to(j):
        src = x_ref if gather else x_ref.at[j]
        return pltpu.make_async_remote_copy(
            src_ref=src,
            dst_ref=land.at[me],
            send_sem=send_sem.at[j],
            recv_sem=recv_sem.at[me],
            device_id=peer(j),
            device_id_type=pl.DeviceIdType.MESH,
        )

    @pl.loop(0, n)
    def _(j):
        @pl.when(j != me)
        def _():
            copy_to(j).start()

    own = x_ref[...] if gather else x_ref[me]
    o_ref[me] = own

    def arrived(j):
        src = x_ref if gather else x_ref.at[j]
        return pltpu.make_async_remote_copy(
            src_ref=src,
            dst_ref=land.at[j],
            send_sem=send_sem.at[j],
            recv_sem=recv_sem.at[j],
            device_id=peer(j),
            device_id_type=pl.DeviceIdType.MESH,
        )

    @pl.loop(0, n)
    def _(j):
        @pl.when(j != me)
        def _():
            arrived(j).wait_recv()
            o_ref[j] = land[j]
            copy_to(j).wait_send()


def exchange(x, axis, n, collective_id, gather=False):
    other = "expert" if axis == "dp" else "dp"
    block = x.shape if gather else x.shape[1:]
    out_shape = jax.ShapeDtypeStruct((n,) + tuple(block), x.dtype)
    return pl.pallas_call(
        functools.partial(_exchange_kernel, axis, other, n, gather),
        out_shape=out_shape,
        in_specs=[pl.BlockSpec(memory_space=pltpu.VMEM)],
        out_specs=pl.BlockSpec(memory_space=pltpu.VMEM),
        scratch_shapes=[
            pltpu.VMEM(out_shape.shape, x.dtype),
            pltpu.SemaphoreType.DMA((n,)),
            pltpu.SemaphoreType.DMA((n,)),
        ],
        compiler_params=pltpu.CompilerParams(collective_id=collective_id, has_side_effects=True),
    )(x)


def _row_exchange_kernel(n, rows, x_ref, o_ref, land, send_sem, recv_sem, own_sem):
    me = lax.axis_index("expert")
    fixed = lax.axis_index("dp")
    mesh_id = pl.DeviceIdType.MESH
    barrier = pltpu.get_barrier_semaphore()

    @pl.loop(0, n)
    def _(j):
        @pl.when(j != me)
        def _():
            pl.semaphore_signal(barrier, inc=1, device_id=(fixed, j), device_id_type=mesh_id)

    pl.semaphore_wait(barrier, n - 1)

    def block(ref, j):
        return ref.at[pl.ds(j * rows, rows)]

    def copy_to(j, slot):
        return pltpu.make_async_remote_copy(
            src_ref=block(x_ref, j), dst_ref=block(land, slot), send_sem=send_sem.at[j],
            recv_sem=recv_sem.at[slot], device_id=(fixed, j), device_id_type=mesh_id)

    @pl.loop(0, n)
    def _(j):
        @pl.when(j != me)
        def _():
            copy_to(j, me).start()

    own = pltpu.make_async_copy(block(x_ref, me), block(land, me), own_sem)
    own.start()

    @pl.loop(0, n)
    def _(j):
        @pl.when(j != me)
        def _():
            copy_to(j, j).wait_recv()
            copy_to(j, me).wait_send()

    own.wait()
    o_ref[...] = land[...]


def row_exchange(x, n, collective_id):
    return pl.pallas_call(
        functools.partial(_row_exchange_kernel, n, x.shape[0] // n),
        out_shape=jax.ShapeDtypeStruct(x.shape, x.dtype),
        in_specs=[pl.BlockSpec(memory_space=pltpu.VMEM)],
        out_specs=pl.BlockSpec(memory_space=pltpu.VMEM),
        scratch_shapes=[
            pltpu.VMEM(x.shape, x.dtype),
            pltpu.SemaphoreType.DMA((n,)),
            pltpu.SemaphoreType.DMA((n,)),
            pltpu.SemaphoreType.DMA(()),
        ],
        compiler_params=pltpu.CompilerParams(collective_id=collective_id, has_side_effects=True),
    )(x)


def gelu_exact(values):
    return jax.nn.gelu(values, approximate=False)


def _allsum_kernel(n_dp, n_ex, x_ref, o_ref, land1, land2, land3, red1, red2, s1, r1, s2, r2, s3, r3):
    me_d = lax.axis_index("dp")
    me_e = lax.axis_index("expert")
    mesh_id = pl.DeviceIdType.MESH
    barrier = pltpu.get_barrier_semaphore()

    @pl.loop(0, n_ex)
    def _(j):
        @pl.when(j != me_e)
        def _():
            pl.semaphore_signal(barrier, inc=1, device_id=(me_d, j), device_id_type=mesh_id)

    @pl.loop(0, n_dp)
    def _(k):
        @pl.when(k != me_d)
        def _():
            pl.semaphore_signal(barrier, inc=1, device_id=(k, me_e), device_id_type=mesh_id)

    pl.semaphore_wait(barrier, n_ex - 1 + n_dp - 1)

    def ex_copy(src, land, send, recv, j, slot):
        return pltpu.make_async_remote_copy(
            src_ref=src, dst_ref=land.at[slot], send_sem=send.at[j], recv_sem=recv.at[slot],
            device_id=(me_d, j), device_id_type=mesh_id)

    def dp_copy(src, land, send, recv, k, slot):
        return pltpu.make_async_remote_copy(
            src_ref=src, dst_ref=land.at[slot], send_sem=send.at[k], recv_sem=recv.at[slot],
            device_id=(k, me_e), device_id_type=mesh_id)

    @pl.loop(0, n_ex)
    def _(j):
        @pl.when(j != me_e)
        def _():
            ex_copy(x_ref.at[j], land1, s1, r1, j, me_e).start()

    land1[me_e] = x_ref[me_e]

    @pl.loop(0, n_ex)
    def _(j):
        @pl.when(j != me_e)
        def _():
            ex_copy(x_ref.at[j], land1, s1, r1, j, j).wait_recv()
            ex_copy(x_ref.at[j], land1, s1, r1, j, me_e).wait_send()

    red1[...] = jnp.sum(land1[...], axis=0)

    @pl.loop(0, n_dp)
    def _(k):
        @pl.when(k != me_d)
        def _():
            dp_copy(red1, land2, s2, r2, k, me_d).start()

    land2[me_d] = red1[...]

    @pl.loop(0, n_dp)
    def _(k):
        @pl.when(k != me_d)
        def _():
            dp_copy(red1, land2, s2, r2, k, k).wait_recv()
            dp_copy(red1, land2, s2, r2, k, me_d).wait_send()

    total = land2[0]
    for k in range(1, n_dp):
        total = total + land2[k]
    red2[...] = total

    @pl.loop(0, n_ex)
    def _(j):
        @pl.when(j != me_e)
        def _():
            ex_copy(red2, land3, s3, r3, j, me_e).start()

    o_ref[me_e] = red2[...]

    @pl.loop(0, n_ex)
    def _(j):
        @pl.when(j != me_e)
        def _():
            ex_copy(red2, land3, s3, r3, j, j).wait_recv()
            o_ref[j] = land3[j]
            ex_copy(red2, land3, s3, r3, j, me_e).wait_send()


def all_sum(value, n_dp, n_expert):
    rows, cols = value.shape
    block = (rows // n_expert, cols)
    chunks = value.reshape(n_expert, *block)
    out = pl.pallas_call(
        functools.partial(_allsum_kernel, n_dp, n_expert),
        out_shape=jax.ShapeDtypeStruct(chunks.shape, value.dtype),
        in_specs=[pl.BlockSpec(memory_space=pltpu.VMEM)],
        out_specs=pl.BlockSpec(memory_space=pltpu.VMEM),
        scratch_shapes=[
            pltpu.VMEM(chunks.shape, value.dtype),
            pltpu.VMEM((n_dp,) + block, value.dtype),
            pltpu.VMEM(chunks.shape, value.dtype),
            pltpu.VMEM(block, value.dtype),
            pltpu.VMEM(block, value.dtype),
            pltpu.SemaphoreType.DMA((n_expert,)),
            pltpu.SemaphoreType.DMA((n_expert,)),
            pltpu.SemaphoreType.DMA((n_dp,)),
            pltpu.SemaphoreType.DMA((n_dp,)),
            pltpu.SemaphoreType.DMA((n_expert,)),
            pltpu.SemaphoreType.DMA((n_expert,)),
        ],
        compiler_params=pltpu.CompilerParams(collective_id=4, has_side_effects=True),
    )(chunks)
    return out.reshape(rows, cols)


def local(n_dp, n_expert, tokens, router, weight_in, weight_out, cotangent):
    experts_dev = weight_in.shape[0]
    width = tokens.shape[2]
    logits = jnp.einsum("isd,de->ise", tokens, router, preferred_element_type=jnp.float32)
    dispatch_prob = jax.nn.softmax(logits, axis=1)
    combine_prob = jax.nn.softmax(logits, axis=2)
    dispatch = dispatch_prob.astype(jnp.bfloat16)
    combine = combine_prob.astype(jnp.bfloat16)
    slots = jnp.einsum("ise,isd->ied", dispatch, tokens, preferred_element_type=jnp.float32).astype(
        jnp.bfloat16
    )
    grad_slots = jnp.einsum(
        "ise,isd->ied", combine, cotangent, preferred_element_type=jnp.float32
    ).astype(jnp.bfloat16)

    def to_owners(local_rows, cid):
        arrived = row_exchange(local_rows[0], n_expert, cid)[None]
        return lax.all_gather(arrived, "dp", axis=0, tiled=True)

    def from_owners(partial_value, cid):
        summed = lax.psum_scatter(partial_value, "dp", scatter_dimension=0, tiled=True)
        return row_exchange(summed[0], n_expert, cid)[None]

    slot_rows = to_owners(slots, 0)
    blocks = slot_rows.reshape(-1, experts_dev, width)
    pre_act = jnp.einsum("rkd,kdf->rkf", blocks, weight_in, preferred_element_type=jnp.float32)
    hidden = gelu_exact(pre_act).astype(jnp.bfloat16)
    partial_value = jnp.einsum(
        "rkf,kfd->rkd", hidden, weight_out, preferred_element_type=jnp.float32
    )
    blocks, pre_act, hidden, partial_value = (
        blocks,
        pre_act,
        hidden,
        partial_value.astype(jnp.bfloat16).reshape(slot_rows.shape),
    )
    expert_outs = from_owners(partial_value, 2)
    grad_rows = to_owners(grad_slots, 1)
    grad_blocks = grad_rows.reshape(blocks.shape)
    grad_hidden = jnp.einsum(
        "rkd,kfd->rkf", grad_blocks, weight_out, preferred_element_type=jnp.float32
    )
    _, gelu_back = jax.vjp(gelu_exact, pre_act)
    grad_pre = gelu_back(grad_hidden)[0].astype(jnp.bfloat16)
    grad_second = jnp.einsum(
        "rkf,rkd->kfd", hidden, grad_blocks, preferred_element_type=jnp.float32
    ).astype(jnp.bfloat16)
    grad_first = jnp.einsum(
        "rkd,rkf->kdf", blocks, grad_pre, preferred_element_type=jnp.float32
    ).astype(jnp.bfloat16)
    partial_back = jnp.einsum(
        "rkf,kdf->rkd", grad_pre, weight_in, preferred_element_type=jnp.float32
    )
    grad_first, grad_second, partial_back = (
        grad_first,
        grad_second,
        partial_back.astype(jnp.bfloat16).reshape(grad_rows.shape),
    )
    grad_slot_all = from_owners(partial_back, 3)
    mixed = jnp.einsum(
        "ise,ied->isd", combine, expert_outs, preferred_element_type=jnp.float32
    ).astype(jnp.bfloat16)
    grad_comb = jnp.einsum(
        "isd,ied->ise", cotangent, expert_outs, preferred_element_type=jnp.float32
    )
    grad_disp = jnp.einsum(
        "isd,ied->ise", tokens, grad_slot_all, preferred_element_type=jnp.float32
    )
    part_disp = dispatch_prob * (
        grad_disp - jnp.sum(dispatch_prob * grad_disp, axis=1, keepdims=True)
    )
    part_comb = combine_prob * (
        grad_comb - jnp.sum(combine_prob * grad_comb, axis=2, keepdims=True)
    )
    grad_logits = (part_disp + part_comb).astype(jnp.bfloat16)
    grad_tokens = (
        jnp.einsum("ise,ied->isd", dispatch, grad_slot_all, preferred_element_type=jnp.float32)
        + jnp.einsum("ise,de->isd", grad_logits, router, preferred_element_type=jnp.float32)
    ).astype(jnp.bfloat16)
    router_term = jnp.einsum("isd,ise->de", tokens, grad_logits, preferred_element_type=jnp.float32)
    grad_router = all_sum(router_term, n_dp, n_expert)
    return (mixed, grad_tokens, grad_router, grad_first, grad_second)


def solution(mesh):
    return jax.shard_map(
        functools.partial(local, mesh.shape["dp"], mesh.shape["expert"]),
        mesh=mesh,
        in_specs=(
            P(("dp", "expert"), None, None),
            P(),
            P("expert", None, "dp"),
            P("expert", "dp", None),
            P(("dp", "expert"), None, None),
        ),
        out_specs=(
            P(("dp", "expert"), None, None),
            P(("dp", "expert"), None, None),
            P(),
            P("expert", None, "dp"),
            P("expert", "dp", None),
        ),
        check_vma=False,
    )
```

```python
import functools

import jax
import jax.numpy as jnp
from jax import lax
from jax.experimental import pallas as pl
from jax.experimental.pallas import tpu as pltpu
from jax.sharding import PartitionSpec as P


def _exchange_kernel(axis, other, n, gather, x_ref, o_ref, land, send_sem, recv_sem):
    me = lax.axis_index(axis)
    fixed = lax.axis_index(other)

    def peer(j):
        if axis == "dp":
            return (j, fixed)
        return (fixed, j)

    barrier = pltpu.get_barrier_semaphore()

    @pl.loop(0, n)
    def _(j):
        @pl.when(j != me)
        def _():
            pl.semaphore_signal(barrier, inc=1, device_id=peer(j), device_id_type=pl.DeviceIdType.MESH)

    pl.semaphore_wait(barrier, n - 1)

    def copy_to(j):
        src = x_ref if gather else x_ref.at[j]
        return pltpu.make_async_remote_copy(
            src_ref=src,
            dst_ref=land.at[me],
            send_sem=send_sem.at[j],
            recv_sem=recv_sem.at[me],
            device_id=peer(j),
            device_id_type=pl.DeviceIdType.MESH,
        )

    @pl.loop(0, n)
    def _(j):
        @pl.when(j != me)
        def _():
            copy_to(j).start()

    own = x_ref[...] if gather else x_ref[me]
    o_ref[me] = own

    def arrived(j):
        src = x_ref if gather else x_ref.at[j]
        return pltpu.make_async_remote_copy(
            src_ref=src,
            dst_ref=land.at[j],
            send_sem=send_sem.at[j],
            recv_sem=recv_sem.at[j],
            device_id=peer(j),
            device_id_type=pl.DeviceIdType.MESH,
        )

    @pl.loop(0, n)
    def _(j):
        @pl.when(j != me)
        def _():
            arrived(j).wait_recv()
            o_ref[j] = land[j]
            copy_to(j).wait_send()


def exchange(x, axis, n, collective_id, gather=False):
    other = "expert" if axis == "dp" else "dp"
    block = x.shape if gather else x.shape[1:]
    out_shape = jax.ShapeDtypeStruct((n,) + tuple(block), x.dtype)
    return pl.pallas_call(
        functools.partial(_exchange_kernel, axis, other, n, gather),
        out_shape=out_shape,
        in_specs=[pl.BlockSpec(memory_space=pltpu.VMEM)],
        out_specs=pl.BlockSpec(memory_space=pltpu.VMEM),
        scratch_shapes=[
            pltpu.VMEM(out_shape.shape, x.dtype),
            pltpu.SemaphoreType.DMA((n,)),
            pltpu.SemaphoreType.DMA((n,)),
        ],
        compiler_params=pltpu.CompilerParams(collective_id=collective_id, has_side_effects=True),
    )(x)


def _row_exchange_kernel(n, rows, x_ref, o_ref, land, send_sem, recv_sem, own_sem):
    me = lax.axis_index("expert")
    fixed = lax.axis_index("dp")
    mesh_id = pl.DeviceIdType.MESH
    barrier = pltpu.get_barrier_semaphore()

    @pl.loop(0, n)
    def _(j):
        @pl.when(j != me)
        def _():
            pl.semaphore_signal(barrier, inc=1, device_id=(fixed, j), device_id_type=mesh_id)

    pl.semaphore_wait(barrier, n - 1)

    def block(ref, j):
        return ref.at[pl.ds(j * rows, rows)]

    def copy_to(j, slot):
        return pltpu.make_async_remote_copy(
            src_ref=block(x_ref, j), dst_ref=block(land, slot), send_sem=send_sem.at[j],
            recv_sem=recv_sem.at[slot], device_id=(fixed, j), device_id_type=mesh_id)

    @pl.loop(0, n)
    def _(j):
        @pl.when(j != me)
        def _():
            copy_to(j, me).start()

    own = pltpu.make_async_copy(block(x_ref, me), block(land, me), own_sem)
    own.start()

    @pl.loop(0, n)
    def _(j):
        @pl.when(j != me)
        def _():
            copy_to(j, j).wait_recv()
            copy_to(j, me).wait_send()

    own.wait()
    o_ref[...] = land[...]


def row_exchange(x, n, collective_id):
    return pl.pallas_call(
        functools.partial(_row_exchange_kernel, n, x.shape[0] // n),
        out_shape=jax.ShapeDtypeStruct(x.shape, x.dtype),
        in_specs=[pl.BlockSpec(memory_space=pltpu.VMEM)],
        out_specs=pl.BlockSpec(memory_space=pltpu.VMEM),
        scratch_shapes=[
            pltpu.VMEM(x.shape, x.dtype),
            pltpu.SemaphoreType.DMA((n,)),
            pltpu.SemaphoreType.DMA((n,)),
            pltpu.SemaphoreType.DMA(()),
        ],
        compiler_params=pltpu.CompilerParams(collective_id=collective_id, has_side_effects=True),
    )(x)


def gelu_exact(values):
    return jax.nn.gelu(values, approximate=False)


def _allsum_kernel(n_dp, n_ex, x_ref, o_ref, land1, land2, land3, red1, red2, s1, r1, s2, r2, s3, r3):
    me_d = lax.axis_index("dp")
    me_e = lax.axis_index("expert")
    mesh_id = pl.DeviceIdType.MESH
    barrier = pltpu.get_barrier_semaphore()

    @pl.loop(0, n_ex)
    def _(j):
        @pl.when(j != me_e)
        def _():
            pl.semaphore_signal(barrier, inc=1, device_id=(me_d, j), device_id_type=mesh_id)

    @pl.loop(0, n_dp)
    def _(k):
        @pl.when(k != me_d)
        def _():
            pl.semaphore_signal(barrier, inc=1, device_id=(k, me_e), device_id_type=mesh_id)

    pl.semaphore_wait(barrier, n_ex - 1 + n_dp - 1)

    def ex_copy(src, land, send, recv, j, slot):
        return pltpu.make_async_remote_copy(
            src_ref=src, dst_ref=land.at[slot], send_sem=send.at[j], recv_sem=recv.at[slot],
            device_id=(me_d, j), device_id_type=mesh_id)

    def dp_copy(src, land, send, recv, k, slot):
        return pltpu.make_async_remote_copy(
            src_ref=src, dst_ref=land.at[slot], send_sem=send.at[k], recv_sem=recv.at[slot],
            device_id=(k, me_e), device_id_type=mesh_id)

    @pl.loop(0, n_ex)
    def _(j):
        @pl.when(j != me_e)
        def _():
            ex_copy(x_ref.at[j], land1, s1, r1, j, me_e).start()

    land1[me_e] = x_ref[me_e]

    @pl.loop(0, n_ex)
    def _(j):
        @pl.when(j != me_e)
        def _():
            ex_copy(x_ref.at[j], land1, s1, r1, j, j).wait_recv()
            ex_copy(x_ref.at[j], land1, s1, r1, j, me_e).wait_send()

    red1[...] = jnp.sum(land1[...].astype(jnp.float32), axis=0).astype(red1.dtype)

    @pl.loop(0, n_dp)
    def _(k):
        @pl.when(k != me_d)
        def _():
            dp_copy(red1, land2, s2, r2, k, me_d).start()

    land2[me_d] = red1[...]

    @pl.loop(0, n_dp)
    def _(k):
        @pl.when(k != me_d)
        def _():
            dp_copy(red1, land2, s2, r2, k, k).wait_recv()
            dp_copy(red1, land2, s2, r2, k, me_d).wait_send()

    total = land2[0].astype(jnp.float32)
    for k in range(1, n_dp):
        total = total + land2[k].astype(jnp.float32)
    red2[...] = total.astype(red2.dtype)

    @pl.loop(0, n_ex)
    def _(j):
        @pl.when(j != me_e)
        def _():
            ex_copy(red2, land3, s3, r3, j, me_e).start()

    o_ref[me_e] = red2[...].astype(o_ref.dtype)

    @pl.loop(0, n_ex)
    def _(j):
        @pl.when(j != me_e)
        def _():
            ex_copy(red2, land3, s3, r3, j, j).wait_recv()
            o_ref[j] = land3[j].astype(o_ref.dtype)
            ex_copy(red2, land3, s3, r3, j, me_e).wait_send()


def all_sum(value, n_dp, n_expert):
    rows, cols = value.shape
    block = (rows // n_expert, cols)
    chunks = value.astype(jnp.bfloat16).reshape(n_expert, *block)
    out = pl.pallas_call(
        functools.partial(_allsum_kernel, n_dp, n_expert),
        out_shape=jax.ShapeDtypeStruct(chunks.shape, value.dtype),
        in_specs=[pl.BlockSpec(memory_space=pltpu.VMEM)],
        out_specs=pl.BlockSpec(memory_space=pltpu.VMEM),
        scratch_shapes=[
            pltpu.VMEM(chunks.shape, chunks.dtype),
            pltpu.VMEM((n_dp,) + block, chunks.dtype),
            pltpu.VMEM(chunks.shape, chunks.dtype),
            pltpu.VMEM(block, chunks.dtype),
            pltpu.VMEM(block, chunks.dtype),
            pltpu.SemaphoreType.DMA((n_expert,)),
            pltpu.SemaphoreType.DMA((n_expert,)),
            pltpu.SemaphoreType.DMA((n_dp,)),
            pltpu.SemaphoreType.DMA((n_dp,)),
            pltpu.SemaphoreType.DMA((n_expert,)),
            pltpu.SemaphoreType.DMA((n_expert,)),
        ],
        compiler_params=pltpu.CompilerParams(collective_id=4, has_side_effects=True),
    )(chunks)
    return out.reshape(rows, cols)


def local(n_dp, n_expert, tokens, router, weight_in, weight_out, cotangent):
    experts_dev = weight_in.shape[0]
    width = tokens.shape[2]
    logits = jnp.einsum("isd,de->ise", tokens, router, preferred_element_type=jnp.float32)
    dispatch_prob = jax.nn.softmax(logits, axis=1)
    combine_prob = jax.nn.softmax(logits, axis=2)
    dispatch = dispatch_prob.astype(jnp.bfloat16)
    combine = combine_prob.astype(jnp.bfloat16)
    slots = jnp.einsum("ise,isd->ied", dispatch, tokens, preferred_element_type=jnp.float32).astype(
        jnp.bfloat16
    )
    grad_slots = jnp.einsum(
        "ise,isd->ied", combine, cotangent, preferred_element_type=jnp.float32
    ).astype(jnp.bfloat16)

    def to_owners(local_rows, cid):
        arrived = row_exchange(local_rows[0], n_expert, cid)[None]
        return lax.all_gather(arrived, "dp", axis=0, tiled=True)

    def from_owners(partial_value, cid):
        summed = lax.psum_scatter(partial_value, "dp", scatter_dimension=0, tiled=True)
        return row_exchange(summed[0], n_expert, cid)[None]

    slot_rows = to_owners(slots, 0)
    blocks = slot_rows.reshape(-1, experts_dev, width)
    pre_act = jnp.einsum("rkd,kdf->rkf", blocks, weight_in, preferred_element_type=jnp.float32)
    hidden = gelu_exact(pre_act).astype(jnp.bfloat16)
    partial_value = jnp.einsum(
        "rkf,kfd->rkd", hidden, weight_out, preferred_element_type=jnp.float32
    )
    blocks, pre_act, hidden, partial_value = (
        blocks,
        pre_act,
        hidden,
        partial_value.astype(jnp.bfloat16).reshape(slot_rows.shape),
    )
    expert_outs = from_owners(partial_value, 2)
    grad_rows = to_owners(grad_slots, 1)
    grad_blocks = grad_rows.reshape(blocks.shape)
    grad_hidden = jnp.einsum(
        "rkd,kfd->rkf", grad_blocks, weight_out, preferred_element_type=jnp.float32
    )
    _, gelu_back = jax.vjp(gelu_exact, pre_act)
    grad_pre = gelu_back(grad_hidden)[0].astype(jnp.bfloat16)
    grad_second = jnp.einsum(
        "rkf,rkd->kfd", hidden, grad_blocks, preferred_element_type=jnp.float32
    ).astype(jnp.bfloat16)
    grad_first = jnp.einsum(
        "rkd,rkf->kdf", blocks, grad_pre, preferred_element_type=jnp.float32
    ).astype(jnp.bfloat16)
    partial_back = jnp.einsum(
        "rkf,kdf->rkd", grad_pre, weight_in, preferred_element_type=jnp.float32
    )
    grad_first, grad_second, partial_back = (
        grad_first,
        grad_second,
        partial_back.astype(jnp.bfloat16).reshape(grad_rows.shape),
    )
    grad_slot_all = from_owners(partial_back, 3)
    mixed = jnp.einsum(
        "ise,ied->isd", combine, expert_outs, preferred_element_type=jnp.float32
    ).astype(jnp.bfloat16)
    grad_comb = jnp.einsum(
        "isd,ied->ise", cotangent, expert_outs, preferred_element_type=jnp.float32
    )
    grad_disp = jnp.einsum(
        "isd,ied->ise", tokens, grad_slot_all, preferred_element_type=jnp.float32
    )
    part_disp = dispatch_prob * (
        grad_disp - jnp.sum(dispatch_prob * grad_disp, axis=1, keepdims=True)
    )
    part_comb = combine_prob * (
        grad_comb - jnp.sum(combine_prob * grad_comb, axis=2, keepdims=True)
    )
    grad_logits = (part_disp + part_comb).astype(jnp.bfloat16)
    grad_tokens = (
        jnp.einsum("ise,ied->isd", dispatch, grad_slot_all, preferred_element_type=jnp.float32)
        + jnp.einsum("ise,de->isd", grad_logits, router, preferred_element_type=jnp.float32)
    ).astype(jnp.bfloat16)
    router_term = jnp.einsum("isd,ise->de", tokens, grad_logits, preferred_element_type=jnp.float32)
    grad_router = all_sum(router_term, n_dp, n_expert)
    return (mixed, grad_tokens, grad_router, grad_first, grad_second)


def solution(mesh):
    return jax.shard_map(
        functools.partial(local, mesh.shape["dp"], mesh.shape["expert"]),
        mesh=mesh,
        in_specs=(
            P(("dp", "expert"), None, None),
            P(),
            P("expert", None, "dp"),
            P("expert", "dp", None),
            P(("dp", "expert"), None, None),
        ),
        out_specs=(
            P(("dp", "expert"), None, None),
            P(("dp", "expert"), None, None),
            P(),
            P("expert", None, "dp"),
            P("expert", "dp", None),
        ),
        check_vma=False,
    )
```

```python
import functools

import jax
import jax.numpy as jnp
from jax import lax
from jax.experimental import pallas as pl
from jax.experimental.pallas import tpu as pltpu
from jax.sharding import PartitionSpec as P


def _exchange_kernel(axis, other, n, gather, x_ref, o_ref, land, send_sem, recv_sem):
    me = lax.axis_index(axis)
    fixed = lax.axis_index(other)

    def peer(j):
        if axis == "dp":
            return (j, fixed)
        return (fixed, j)

    barrier = pltpu.get_barrier_semaphore()

    @pl.loop(0, n)
    def _(j):
        @pl.when(j != me)
        def _():
            pl.semaphore_signal(barrier, inc=1, device_id=peer(j), device_id_type=pl.DeviceIdType.MESH)

    pl.semaphore_wait(barrier, n - 1)

    def copy_to(j):
        src = x_ref if gather else x_ref.at[j]
        return pltpu.make_async_remote_copy(
            src_ref=src,
            dst_ref=land.at[me],
            send_sem=send_sem.at[j],
            recv_sem=recv_sem.at[me],
            device_id=peer(j),
            device_id_type=pl.DeviceIdType.MESH,
        )

    @pl.loop(0, n)
    def _(j):
        @pl.when(j != me)
        def _():
            copy_to(j).start()

    own = x_ref[...] if gather else x_ref[me]
    o_ref[me] = own

    def arrived(j):
        src = x_ref if gather else x_ref.at[j]
        return pltpu.make_async_remote_copy(
            src_ref=src,
            dst_ref=land.at[j],
            send_sem=send_sem.at[j],
            recv_sem=recv_sem.at[j],
            device_id=peer(j),
            device_id_type=pl.DeviceIdType.MESH,
        )

    @pl.loop(0, n)
    def _(j):
        @pl.when(j != me)
        def _():
            arrived(j).wait_recv()
            o_ref[j] = land[j]
            copy_to(j).wait_send()


def exchange(x, axis, n, collective_id, gather=False):
    other = "expert" if axis == "dp" else "dp"
    block = x.shape if gather else x.shape[1:]
    out_shape = jax.ShapeDtypeStruct((n,) + tuple(block), x.dtype)
    return pl.pallas_call(
        functools.partial(_exchange_kernel, axis, other, n, gather),
        out_shape=out_shape,
        in_specs=[pl.BlockSpec(memory_space=pltpu.VMEM)],
        out_specs=pl.BlockSpec(memory_space=pltpu.VMEM),
        scratch_shapes=[
            pltpu.VMEM(out_shape.shape, x.dtype),
            pltpu.SemaphoreType.DMA((n,)),
            pltpu.SemaphoreType.DMA((n,)),
        ],
        compiler_params=pltpu.CompilerParams(collective_id=collective_id, has_side_effects=True),
    )(x)


def _row_exchange_kernel(n, rows, x_ref, o_ref, land, send_sem, recv_sem, own_sem):
    me = lax.axis_index("expert")
    fixed = lax.axis_index("dp")
    mesh_id = pl.DeviceIdType.MESH
    barrier = pltpu.get_barrier_semaphore()

    @pl.loop(0, n)
    def _(j):
        @pl.when(j != me)
        def _():
            pl.semaphore_signal(barrier, inc=1, device_id=(fixed, j), device_id_type=mesh_id)

    pl.semaphore_wait(barrier, n - 1)

    def block(ref, j):
        return ref.at[pl.ds(j * rows, rows)]

    def copy_to(j, slot):
        return pltpu.make_async_remote_copy(
            src_ref=block(x_ref, j), dst_ref=block(land, slot), send_sem=send_sem.at[j],
            recv_sem=recv_sem.at[slot], device_id=(fixed, j), device_id_type=mesh_id)

    @pl.loop(0, n)
    def _(j):
        @pl.when(j != me)
        def _():
            copy_to(j, me).start()

    own = pltpu.make_async_copy(block(x_ref, me), block(land, me), own_sem)
    own.start()

    @pl.loop(0, n)
    def _(j):
        @pl.when(j != me)
        def _():
            copy_to(j, j).wait_recv()
            copy_to(j, me).wait_send()

    own.wait()
    o_ref[...] = land[...]


def row_exchange(x, n, collective_id):
    return pl.pallas_call(
        functools.partial(_row_exchange_kernel, n, x.shape[0] // n),
        out_shape=jax.ShapeDtypeStruct(x.shape, x.dtype),
        in_specs=[pl.BlockSpec(memory_space=pltpu.VMEM)],
        out_specs=pl.BlockSpec(memory_space=pltpu.VMEM),
        scratch_shapes=[
            pltpu.VMEM(x.shape, x.dtype),
            pltpu.SemaphoreType.DMA((n,)),
            pltpu.SemaphoreType.DMA((n,)),
            pltpu.SemaphoreType.DMA(()),
        ],
        compiler_params=pltpu.CompilerParams(collective_id=collective_id, has_side_effects=True),
    )(x)


def gelu_exact(values):
    return jax.nn.gelu(values, approximate=False)


def _allsum_kernel(n_dp, n_ex, x_ref, o_ref, land1, land2, land3, red1, red2, s1, r1, s2, r2, s3, r3):
    me_d = lax.axis_index("dp")
    me_e = lax.axis_index("expert")
    mesh_id = pl.DeviceIdType.MESH
    barrier = pltpu.get_barrier_semaphore()

    @pl.loop(0, n_ex)
    def _(j):
        @pl.when(j != me_e)
        def _():
            pl.semaphore_signal(barrier, inc=1, device_id=(me_d, j), device_id_type=mesh_id)

    @pl.loop(0, n_dp)
    def _(k):
        @pl.when(k != me_d)
        def _():
            pl.semaphore_signal(barrier, inc=1, device_id=(k, me_e), device_id_type=mesh_id)

    pl.semaphore_wait(barrier, n_ex - 1 + n_dp - 1)

    def ex_copy(src, land, send, recv, j, slot):
        return pltpu.make_async_remote_copy(
            src_ref=src, dst_ref=land.at[slot], send_sem=send.at[j], recv_sem=recv.at[slot],
            device_id=(me_d, j), device_id_type=mesh_id)

    def dp_copy(src, land, send, recv, k, slot):
        return pltpu.make_async_remote_copy(
            src_ref=src, dst_ref=land.at[slot], send_sem=send.at[k], recv_sem=recv.at[slot],
            device_id=(k, me_e), device_id_type=mesh_id)

    @pl.loop(0, n_ex)
    def _(j):
        @pl.when(j != me_e)
        def _():
            ex_copy(x_ref.at[j], land1, s1, r1, j, me_e).start()

    land1[me_e] = x_ref[me_e]

    @pl.loop(0, n_ex)
    def _(j):
        @pl.when(j != me_e)
        def _():
            ex_copy(x_ref.at[j], land1, s1, r1, j, j).wait_recv()
            ex_copy(x_ref.at[j], land1, s1, r1, j, me_e).wait_send()

    red1[...] = jnp.sum(land1[...].astype(jnp.float32), axis=0).astype(red1.dtype)

    @pl.loop(0, n_dp)
    def _(k):
        @pl.when(k != me_d)
        def _():
            dp_copy(red1, land2, s2, r2, k, me_d).start()

    land2[me_d] = red1[...]

    @pl.loop(0, n_dp)
    def _(k):
        @pl.when(k != me_d)
        def _():
            dp_copy(red1, land2, s2, r2, k, k).wait_recv()
            dp_copy(red1, land2, s2, r2, k, me_d).wait_send()

    total = land2[0].astype(jnp.float32)
    for k in range(1, n_dp):
        total = total + land2[k].astype(jnp.float32)
    red2[...] = total.astype(red2.dtype)

    @pl.loop(0, n_ex)
    def _(j):
        @pl.when(j != me_e)
        def _():
            ex_copy(red2, land3, s3, r3, j, me_e).start()

    o_ref[me_e] = red2[...]

    @pl.loop(0, n_ex)
    def _(j):
        @pl.when(j != me_e)
        def _():
            ex_copy(red2, land3, s3, r3, j, j).wait_recv()
            o_ref[j] = land3[j]
            ex_copy(red2, land3, s3, r3, j, me_e).wait_send()


def all_sum(value, n_dp, n_expert):
    rows, cols = value.shape
    block = (rows // n_expert, cols)
    chunks = value.astype(jnp.bfloat16).reshape(n_expert, *block)
    out = pl.pallas_call(
        functools.partial(_allsum_kernel, n_dp, n_expert),
        out_shape=jax.ShapeDtypeStruct(chunks.shape, chunks.dtype),
        in_specs=[pl.BlockSpec(memory_space=pltpu.VMEM)],
        out_specs=pl.BlockSpec(memory_space=pltpu.VMEM),
        scratch_shapes=[
            pltpu.VMEM(chunks.shape, chunks.dtype),
            pltpu.VMEM((n_dp,) + block, chunks.dtype),
            pltpu.VMEM(chunks.shape, chunks.dtype),
            pltpu.VMEM(block, chunks.dtype),
            pltpu.VMEM(block, chunks.dtype),
            pltpu.SemaphoreType.DMA((n_expert,)),
            pltpu.SemaphoreType.DMA((n_expert,)),
            pltpu.SemaphoreType.DMA((n_dp,)),
            pltpu.SemaphoreType.DMA((n_dp,)),
            pltpu.SemaphoreType.DMA((n_expert,)),
            pltpu.SemaphoreType.DMA((n_expert,)),
        ],
        compiler_params=pltpu.CompilerParams(collective_id=4, has_side_effects=True),
    )(chunks)
    return out.reshape(rows, cols).astype(value.dtype)


def local(n_dp, n_expert, tokens, router, weight_in, weight_out, cotangent):
    experts_dev = weight_in.shape[0]
    width = tokens.shape[2]
    logits = jnp.einsum("isd,de->ise", tokens, router, preferred_element_type=jnp.float32)
    dispatch_prob = jax.nn.softmax(logits, axis=1)
    combine_prob = jax.nn.softmax(logits, axis=2)
    dispatch = dispatch_prob.astype(jnp.bfloat16)
    combine = combine_prob.astype(jnp.bfloat16)
    slots = jnp.einsum("ise,isd->ied", dispatch, tokens, preferred_element_type=jnp.float32).astype(
        jnp.bfloat16
    )
    grad_slots = jnp.einsum(
        "ise,isd->ied", combine, cotangent, preferred_element_type=jnp.float32
    ).astype(jnp.bfloat16)

    def to_owners(local_rows, cid):
        arrived = row_exchange(local_rows[0], n_expert, cid)[None]
        return lax.all_gather(arrived, "dp", axis=0, tiled=True)

    def from_owners(partial_value, cid):
        summed = lax.psum_scatter(partial_value, "dp", scatter_dimension=0, tiled=True)
        return row_exchange(summed[0], n_expert, cid)[None]

    slot_rows = to_owners(slots, 0)
    blocks = slot_rows.reshape(-1, experts_dev, width)
    pre_act = jnp.einsum("rkd,kdf->rkf", blocks, weight_in, preferred_element_type=jnp.float32)
    hidden = gelu_exact(pre_act).astype(jnp.bfloat16)
    partial_value = jnp.einsum(
        "rkf,kfd->rkd", hidden, weight_out, preferred_element_type=jnp.float32
    )
    blocks, pre_act, hidden, partial_value = (
        blocks,
        pre_act,
        hidden,
        partial_value.astype(jnp.bfloat16).reshape(slot_rows.shape),
    )
    expert_outs = from_owners(partial_value, 2)
    grad_rows = to_owners(grad_slots, 1)
    grad_blocks = grad_rows.reshape(blocks.shape)
    grad_hidden = jnp.einsum(
        "rkd,kfd->rkf", grad_blocks, weight_out, preferred_element_type=jnp.float32
    )
    _, gelu_back = jax.vjp(gelu_exact, pre_act)
    grad_pre = gelu_back(grad_hidden)[0].astype(jnp.bfloat16)
    grad_second = jnp.einsum(
        "rkf,rkd->kfd", hidden, grad_blocks, preferred_element_type=jnp.float32
    ).astype(jnp.bfloat16)
    grad_first = jnp.einsum(
        "rkd,rkf->kdf", blocks, grad_pre, preferred_element_type=jnp.float32
    ).astype(jnp.bfloat16)
    partial_back = jnp.einsum(
        "rkf,kdf->rkd", grad_pre, weight_in, preferred_element_type=jnp.float32
    )
    grad_first, grad_second, partial_back = (
        grad_first,
        grad_second,
        partial_back.astype(jnp.bfloat16).reshape(grad_rows.shape),
    )
    grad_slot_all = from_owners(partial_back, 3)
    mixed = jnp.einsum(
        "ise,ied->isd", combine, expert_outs, preferred_element_type=jnp.float32
    ).astype(jnp.bfloat16)
    grad_comb = jnp.einsum(
        "isd,ied->ise", cotangent, expert_outs, preferred_element_type=jnp.float32
    )
    grad_disp = jnp.einsum(
        "isd,ied->ise", tokens, grad_slot_all, preferred_element_type=jnp.float32
    )
    part_disp = dispatch_prob * (
        grad_disp - jnp.sum(dispatch_prob * grad_disp, axis=1, keepdims=True)
    )
    part_comb = combine_prob * (
        grad_comb - jnp.sum(combine_prob * grad_comb, axis=2, keepdims=True)
    )
    grad_logits = (part_disp + part_comb).astype(jnp.bfloat16)
    grad_tokens = (
        jnp.einsum("ise,ied->isd", dispatch, grad_slot_all, preferred_element_type=jnp.float32)
        + jnp.einsum("ise,de->isd", grad_logits, router, preferred_element_type=jnp.float32)
    ).astype(jnp.bfloat16)
    router_term = jnp.einsum("isd,ise->de", tokens, grad_logits, preferred_element_type=jnp.float32)
    grad_router = all_sum(router_term, n_dp, n_expert)
    return (mixed, grad_tokens, grad_router, grad_first, grad_second)


def solution(mesh):
    return jax.shard_map(
        functools.partial(local, mesh.shape["dp"], mesh.shape["expert"]),
        mesh=mesh,
        in_specs=(
            P(("dp", "expert"), None, None),
            P(),
            P("expert", None, "dp"),
            P("expert", "dp", None),
            P(("dp", "expert"), None, None),
        ),
        out_specs=(
            P(("dp", "expert"), None, None),
            P(("dp", "expert"), None, None),
            P(),
            P("expert", None, "dp"),
            P("expert", "dp", None),
        ),
        check_vma=False,
    )
```

```python
import functools

import jax
import jax.numpy as jnp
from jax import lax
from jax.experimental import pallas as pl
from jax.experimental.pallas import tpu as pltpu
from jax.sharding import PartitionSpec as P


def _exchange_kernel(axis, other, n, gather, x_ref, o_ref, land, send_sem, recv_sem):
    me = lax.axis_index(axis)
    fixed = lax.axis_index(other)

    def peer(j):
        if axis == "dp":
            return (j, fixed)
        return (fixed, j)

    barrier = pltpu.get_barrier_semaphore()

    @pl.loop(0, n)
    def _(j):
        @pl.when(j != me)
        def _():
            pl.semaphore_signal(barrier, inc=1, device_id=peer(j), device_id_type=pl.DeviceIdType.MESH)

    pl.semaphore_wait(barrier, n - 1)

    def copy_to(j):
        src = x_ref if gather else x_ref.at[j]
        return pltpu.make_async_remote_copy(
            src_ref=src,
            dst_ref=land.at[me],
            send_sem=send_sem.at[j],
            recv_sem=recv_sem.at[me],
            device_id=peer(j),
            device_id_type=pl.DeviceIdType.MESH,
        )

    @pl.loop(0, n)
    def _(j):
        @pl.when(j != me)
        def _():
            copy_to(j).start()

    own = x_ref[...] if gather else x_ref[me]
    o_ref[me] = own

    def arrived(j):
        src = x_ref if gather else x_ref.at[j]
        return pltpu.make_async_remote_copy(
            src_ref=src,
            dst_ref=land.at[j],
            send_sem=send_sem.at[j],
            recv_sem=recv_sem.at[j],
            device_id=peer(j),
            device_id_type=pl.DeviceIdType.MESH,
        )

    @pl.loop(0, n)
    def _(j):
        @pl.when(j != me)
        def _():
            arrived(j).wait_recv()
            o_ref[j] = land[j]
            copy_to(j).wait_send()


def exchange(x, axis, n, collective_id, gather=False):
    other = "expert" if axis == "dp" else "dp"
    block = x.shape if gather else x.shape[1:]
    out_shape = jax.ShapeDtypeStruct((n,) + tuple(block), x.dtype)
    return pl.pallas_call(
        functools.partial(_exchange_kernel, axis, other, n, gather),
        out_shape=out_shape,
        in_specs=[pl.BlockSpec(memory_space=pltpu.VMEM)],
        out_specs=pl.BlockSpec(memory_space=pltpu.VMEM),
        scratch_shapes=[
            pltpu.VMEM(out_shape.shape, x.dtype),
            pltpu.SemaphoreType.DMA((n,)),
            pltpu.SemaphoreType.DMA((n,)),
        ],
        compiler_params=pltpu.CompilerParams(collective_id=collective_id, has_side_effects=True),
    )(x)


def _row_exchange_kernel(n, rows, x_ref, o_ref, land, send_sem, recv_sem, own_sem):
    me = lax.axis_index("expert")
    fixed = lax.axis_index("dp")
    mesh_id = pl.DeviceIdType.MESH
    barrier = pltpu.get_barrier_semaphore()

    @pl.loop(0, n)
    def _(j):
        @pl.when(j != me)
        def _():
            pl.semaphore_signal(barrier, inc=1, device_id=(fixed, j), device_id_type=mesh_id)

    pl.semaphore_wait(barrier, n - 1)

    def block(ref, j):
        return ref.at[pl.ds(j * rows, rows)]

    def copy_to(j, slot):
        return pltpu.make_async_remote_copy(
            src_ref=block(x_ref, j), dst_ref=block(land, slot), send_sem=send_sem.at[j],
            recv_sem=recv_sem.at[slot], device_id=(fixed, j), device_id_type=mesh_id)

    @pl.loop(0, n)
    def _(j):
        @pl.when(j != me)
        def _():
            copy_to(j, me).start()

    own = pltpu.make_async_copy(block(x_ref, me), block(land, me), own_sem)
    own.start()

    @pl.loop(0, n)
    def _(j):
        @pl.when(j != me)
        def _():
            copy_to(j, j).wait_recv()
            copy_to(j, me).wait_send()

    own.wait()
    o_ref[...] = land[...]


def row_exchange(x, n, collective_id):
    return pl.pallas_call(
        functools.partial(_row_exchange_kernel, n, x.shape[0] // n),
        out_shape=jax.ShapeDtypeStruct(x.shape, x.dtype),
        in_specs=[pl.BlockSpec(memory_space=pltpu.VMEM)],
        out_specs=pl.BlockSpec(memory_space=pltpu.VMEM),
        scratch_shapes=[
            pltpu.VMEM(x.shape, x.dtype),
            pltpu.SemaphoreType.DMA((n,)),
            pltpu.SemaphoreType.DMA((n,)),
            pltpu.SemaphoreType.DMA(()),
        ],
        compiler_params=pltpu.CompilerParams(collective_id=collective_id, has_side_effects=True),
    )(x)


def gelu_exact(values):
    return jax.nn.gelu(values, approximate=False)


def _allsum_kernel(n_dp, n_ex, x_ref, o_ref, land1, land2, land3, red1, red2, s1, r1, s2, r2, s3, r3):
    me_d = lax.axis_index("dp")
    me_e = lax.axis_index("expert")
    mesh_id = pl.DeviceIdType.MESH
    barrier = pltpu.get_barrier_semaphore()

    @pl.loop(0, n_ex)
    def _(j):
        @pl.when(j != me_e)
        def _():
            pl.semaphore_signal(barrier, inc=1, device_id=(me_d, j), device_id_type=mesh_id)

    @pl.loop(0, n_dp)
    def _(k):
        @pl.when(k != me_d)
        def _():
            pl.semaphore_signal(barrier, inc=1, device_id=(k, me_e), device_id_type=mesh_id)

    pl.semaphore_wait(barrier, n_ex - 1 + n_dp - 1)

    def ex_copy(src, land, send, recv, j, slot):
        return pltpu.make_async_remote_copy(
            src_ref=src, dst_ref=land.at[slot], send_sem=send.at[j], recv_sem=recv.at[slot],
            device_id=(me_d, j), device_id_type=mesh_id)

    def dp_copy(src, land, send, recv, k, slot):
        return pltpu.make_async_remote_copy(
            src_ref=src, dst_ref=land.at[slot], send_sem=send.at[k], recv_sem=recv.at[slot],
            device_id=(k, me_e), device_id_type=mesh_id)

    @pl.loop(0, n_ex)
    def _(j):
        @pl.when(j != me_e)
        def _():
            ex_copy(x_ref.at[j], land1, s1, r1, j, me_e).start()

    land1[me_e] = x_ref[me_e]

    @pl.loop(0, n_ex)
    def _(j):
        @pl.when(j != me_e)
        def _():
            ex_copy(x_ref.at[j], land1, s1, r1, j, j).wait_recv()
            ex_copy(x_ref.at[j], land1, s1, r1, j, me_e).wait_send()

    red1[...] = jnp.sum(land1[...].astype(jnp.float32), axis=0).astype(red1.dtype)

    @pl.loop(0, n_dp)
    def _(k):
        @pl.when(k != me_d)
        def _():
            dp_copy(red1, land2, s2, r2, k, me_d).start()

    land2[me_d] = red1[...]

    @pl.loop(0, n_dp)
    def _(k):
        @pl.when(k != me_d)
        def _():
            dp_copy(red1, land2, s2, r2, k, k).wait_recv()
            dp_copy(red1, land2, s2, r2, k, me_d).wait_send()

    total = land2[0].astype(jnp.float32)
    for k in range(1, n_dp):
        total = total + land2[k].astype(jnp.float32)
    red2[...] = total.astype(red2.dtype)

    @pl.loop(0, n_ex)
    def _(j):
        @pl.when(j != me_e)
        def _():
            ex_copy(red2, land3, s3, r3, j, me_e).start()

    o_ref[me_e] = red2[...]

    @pl.loop(0, n_ex)
    def _(j):
        @pl.when(j != me_e)
        def _():
            ex_copy(red2, land3, s3, r3, j, j).wait_recv()
            o_ref[j] = land3[j]
            ex_copy(red2, land3, s3, r3, j, me_e).wait_send()


def all_sum(value, n_dp, n_expert):
    rows, cols = value.shape
    block = (rows // n_expert, cols)
    chunks = value.astype(jnp.bfloat16).reshape(n_expert, *block)
    out = pl.pallas_call(
        functools.partial(_allsum_kernel, n_dp, n_expert),
        out_shape=jax.ShapeDtypeStruct(chunks.shape, chunks.dtype),
        in_specs=[pl.BlockSpec(memory_space=pltpu.VMEM)],
        out_specs=pl.BlockSpec(memory_space=pltpu.VMEM),
        scratch_shapes=[
            pltpu.VMEM(chunks.shape, chunks.dtype),
            pltpu.VMEM((n_dp,) + block, chunks.dtype),
            pltpu.VMEM(chunks.shape, chunks.dtype),
            pltpu.VMEM(block, chunks.dtype),
            pltpu.VMEM(block, chunks.dtype),
            pltpu.SemaphoreType.DMA((n_expert,)),
            pltpu.SemaphoreType.DMA((n_expert,)),
            pltpu.SemaphoreType.DMA((n_dp,)),
            pltpu.SemaphoreType.DMA((n_dp,)),
            pltpu.SemaphoreType.DMA((n_expert,)),
            pltpu.SemaphoreType.DMA((n_expert,)),
        ],
        compiler_params=pltpu.CompilerParams(collective_id=4, has_side_effects=True),
    )(chunks)
    return out.reshape(rows, cols).astype(value.dtype)


def _tail_kernel(n_dp, n_ex, rows, summed_ref, tok_ref, tokt_ref, prob_ref, comb_ref,
                 gsa_ref, logit_ref, o_ref,
                 land0, xs, land1, land2, land3, red1, red2, s0, r0, own_sem, s1, r1, s2, r2, s3, r3):
    me_d = lax.axis_index("dp")
    me_e = lax.axis_index("expert")
    mesh_id = pl.DeviceIdType.MESH
    barrier = pltpu.get_barrier_semaphore()

    @pl.loop(0, n_ex)
    def _(j):
        @pl.when(j != me_e)
        def _():
            pl.semaphore_signal(barrier, inc=1, device_id=(me_d, j), device_id_type=mesh_id)

    @pl.loop(0, n_dp)
    def _(k):
        @pl.when(k != me_d)
        def _():
            pl.semaphore_signal(barrier, inc=1, device_id=(k, me_e), device_id_type=mesh_id)

    pl.semaphore_wait(barrier, n_ex - 1 + n_dp - 1)

    def row_copy(j, slot):
        return pltpu.make_async_remote_copy(
            src_ref=summed_ref.at[pl.ds(j * rows, rows)], dst_ref=land0.at[pl.ds(slot * rows, rows)],
            send_sem=s0.at[j], recv_sem=r0.at[slot], device_id=(me_d, j), device_id_type=mesh_id)

    @pl.loop(0, n_ex)
    def _(j):
        @pl.when(j != me_e)
        def _():
            row_copy(j, me_e).start()

    own = pltpu.make_async_copy(
        summed_ref.at[pl.ds(me_e * rows, rows)], land0.at[pl.ds(me_e * rows, rows)], own_sem)
    own.start()

    @pl.loop(0, n_ex)
    def _(j):
        @pl.when(j != me_e)
        def _():
            row_copy(j, j).wait_recv()
            row_copy(j, me_e).wait_send()

    own.wait()
    gsa = land0[...]
    gsa_ref[...] = gsa
    prob = prob_ref[...]
    grad_disp = lax.dot_general(tok_ref[...], gsa, (((1,), (1,)), ((), ())), preferred_element_type=jnp.float32)
    part_disp = prob * (grad_disp - jnp.sum(prob * grad_disp, axis=0, keepdims=True))
    logits = (part_disp + comb_ref[...]).astype(logit_ref.dtype)
    logit_ref[...] = logits
    term = jnp.dot(tokt_ref[...], logits, preferred_element_type=jnp.float32)
    xs[...] = term.astype(xs.dtype).reshape(xs.shape)

    def ex_copy(src, land, send, recv, j, slot):
        return pltpu.make_async_remote_copy(
            src_ref=src, dst_ref=land.at[slot], send_sem=send.at[j], recv_sem=recv.at[slot],
            device_id=(me_d, j), device_id_type=mesh_id)

    def dp_copy(src, land, send, recv, k, slot):
        return pltpu.make_async_remote_copy(
            src_ref=src, dst_ref=land.at[slot], send_sem=send.at[k], recv_sem=recv.at[slot],
            device_id=(k, me_e), device_id_type=mesh_id)

    @pl.loop(0, n_ex)
    def _(j):
        @pl.when(j != me_e)
        def _():
            ex_copy(xs.at[j], land1, s1, r1, j, me_e).start()

    land1[me_e] = xs[me_e]

    @pl.loop(0, n_ex)
    def _(j):
        @pl.when(j != me_e)
        def _():
            ex_copy(xs.at[j], land1, s1, r1, j, j).wait_recv()
            ex_copy(xs.at[j], land1, s1, r1, j, me_e).wait_send()

    red1[...] = jnp.sum(land1[...].astype(jnp.float32), axis=0).astype(red1.dtype)

    @pl.loop(0, n_dp)
    def _(k):
        @pl.when(k != me_d)
        def _():
            dp_copy(red1, land2, s2, r2, k, me_d).start()

    land2[me_d] = red1[...]

    @pl.loop(0, n_dp)
    def _(k):
        @pl.when(k != me_d)
        def _():
            dp_copy(red1, land2, s2, r2, k, k).wait_recv()
            dp_copy(red1, land2, s2, r2, k, me_d).wait_send()

    total = land2[0].astype(jnp.float32)
    for k in range(1, n_dp):
        total = total + land2[k].astype(jnp.float32)
    red2[...] = total.astype(red2.dtype)

    @pl.loop(0, n_ex)
    def _(j):
        @pl.when(j != me_e)
        def _():
            ex_copy(red2, land3, s3, r3, j, me_e).start()

    o_ref[me_e] = red2[...]

    @pl.loop(0, n_ex)
    def _(j):
        @pl.when(j != me_e)
        def _():
            ex_copy(red2, land3, s3, r3, j, j).wait_recv()
            o_ref[j] = land3[j]
            ex_copy(red2, land3, s3, r3, j, me_e).wait_send()


def tail(summed, tokens, tokens_t, prob, part_comb, n_dp, n_ex):
    width, experts = tokens_t.shape[0], prob.shape[1]
    block = (width // n_ex, experts)
    chunks = (n_ex,) + block
    bf = jnp.bfloat16
    vmem = pl.BlockSpec(memory_space=pltpu.VMEM)
    gsa, logits, out = pl.pallas_call(
        functools.partial(_tail_kernel, n_dp, n_ex, summed.shape[0] // n_ex),
        out_shape=(jax.ShapeDtypeStruct(summed.shape, summed.dtype),
                   jax.ShapeDtypeStruct(prob.shape, bf),
                   jax.ShapeDtypeStruct(chunks, bf)),
        in_specs=[vmem] * 5,
        out_specs=(vmem, vmem, vmem),
        scratch_shapes=[
            pltpu.VMEM(summed.shape, summed.dtype),
            pltpu.VMEM(chunks, bf),
            pltpu.VMEM(chunks, bf),
            pltpu.VMEM((n_dp,) + block, bf),
            pltpu.VMEM(chunks, bf),
            pltpu.VMEM(block, bf),
            pltpu.VMEM(block, bf),
            pltpu.SemaphoreType.DMA((n_ex,)),
            pltpu.SemaphoreType.DMA((n_ex,)),
            pltpu.SemaphoreType.DMA(()),
            pltpu.SemaphoreType.DMA((n_ex,)),
            pltpu.SemaphoreType.DMA((n_ex,)),
            pltpu.SemaphoreType.DMA((n_dp,)),
            pltpu.SemaphoreType.DMA((n_dp,)),
            pltpu.SemaphoreType.DMA((n_ex,)),
            pltpu.SemaphoreType.DMA((n_ex,)),
        ],
        compiler_params=pltpu.CompilerParams(collective_id=5, has_side_effects=True),
    )(summed, tokens, tokens_t, prob, part_comb)
    return gsa, logits, out.reshape(width, experts).astype(jnp.float32)


def local(n_dp, n_expert, tokens, router, weight_in, weight_out, cotangent):
    experts_dev = weight_in.shape[0]
    width = tokens.shape[2]
    logits = jnp.einsum("isd,de->ise", tokens, router, preferred_element_type=jnp.float32)
    dispatch_prob = jax.nn.softmax(logits, axis=1)
    combine_prob = jax.nn.softmax(logits, axis=2)
    dispatch = dispatch_prob.astype(jnp.bfloat16)
    combine = combine_prob.astype(jnp.bfloat16)
    slots = jnp.einsum("ise,isd->ied", dispatch, tokens, preferred_element_type=jnp.float32).astype(
        jnp.bfloat16
    )
    grad_slots = jnp.einsum(
        "ise,isd->ied", combine, cotangent, preferred_element_type=jnp.float32
    ).astype(jnp.bfloat16)

    def to_owners(local_rows, cid):
        arrived = row_exchange(local_rows[0], n_expert, cid)[None]
        return lax.all_gather(arrived, "dp", axis=0, tiled=True)

    def from_owners(partial_value, cid):
        summed = lax.psum_scatter(partial_value, "dp", scatter_dimension=0, tiled=True)
        return row_exchange(summed[0], n_expert, cid)[None]

    slot_rows = to_owners(slots, 0)
    blocks = slot_rows.reshape(-1, experts_dev, width)
    pre_act = jnp.einsum("rkd,kdf->rkf", blocks, weight_in, preferred_element_type=jnp.float32)
    hidden = gelu_exact(pre_act).astype(jnp.bfloat16)
    partial_value = jnp.einsum(
        "rkf,kfd->rkd", hidden, weight_out, preferred_element_type=jnp.float32
    )
    blocks, pre_act, hidden, partial_value = (
        blocks,
        pre_act,
        hidden,
        partial_value.astype(jnp.bfloat16).reshape(slot_rows.shape),
    )
    expert_outs = from_owners(partial_value, 2)
    grad_rows = to_owners(grad_slots, 1)
    grad_blocks = grad_rows.reshape(blocks.shape)
    grad_hidden = jnp.einsum(
        "rkd,kfd->rkf", grad_blocks, weight_out, preferred_element_type=jnp.float32
    )
    _, gelu_back = jax.vjp(gelu_exact, pre_act)
    grad_pre = gelu_back(grad_hidden)[0].astype(jnp.bfloat16)
    grad_second = jnp.einsum(
        "rkf,rkd->kfd", hidden, grad_blocks, preferred_element_type=jnp.float32
    ).astype(jnp.bfloat16)
    grad_first = jnp.einsum(
        "rkd,rkf->kdf", blocks, grad_pre, preferred_element_type=jnp.float32
    ).astype(jnp.bfloat16)
    partial_back = jnp.einsum(
        "rkf,kdf->rkd", grad_pre, weight_in, preferred_element_type=jnp.float32
    )
    grad_first, grad_second, partial_back = (
        grad_first,
        grad_second,
        partial_back.astype(jnp.bfloat16).reshape(grad_rows.shape),
    )
    summed_back = lax.psum_scatter(partial_back, "dp", scatter_dimension=0, tiled=True)[0]
    mixed = jnp.einsum(
        "ise,ied->isd", combine, expert_outs, preferred_element_type=jnp.float32
    ).astype(jnp.bfloat16)
    grad_comb = jnp.einsum(
        "isd,ied->ise", cotangent, expert_outs, preferred_element_type=jnp.float32
    )
    part_comb = combine_prob * (
        grad_comb - jnp.sum(combine_prob * grad_comb, axis=2, keepdims=True)
    )
    gsa, logits, grad_router = tail(
        summed_back, tokens[0], tokens[0].T, dispatch_prob[0], part_comb[0], n_dp, n_expert
    )
    grad_slot_all = gsa[None]
    grad_logits = logits[None]
    grad_tokens = (
        jnp.einsum("ise,ied->isd", dispatch, grad_slot_all, preferred_element_type=jnp.float32)
        + jnp.einsum("ise,de->isd", grad_logits, router, preferred_element_type=jnp.float32)
    ).astype(jnp.bfloat16)
    return (mixed, grad_tokens, grad_router, grad_first, grad_second)


def solution(mesh):
    return jax.shard_map(
        functools.partial(local, mesh.shape["dp"], mesh.shape["expert"]),
        mesh=mesh,
        in_specs=(
            P(("dp", "expert"), None, None),
            P(),
            P("expert", None, "dp"),
            P("expert", "dp", None),
            P(("dp", "expert"), None, None),
        ),
        out_specs=(
            P(("dp", "expert"), None, None),
            P(("dp", "expert"), None, None),
            P(),
            P("expert", None, "dp"),
            P("expert", "dp", None),
        ),
        check_vma=False,
    )
```

```python
import functools

import jax
import jax.numpy as jnp
from jax import lax
from jax.experimental import pallas as pl
from jax.experimental.pallas import tpu as pltpu
from jax.sharding import PartitionSpec as P


def _exchange_kernel(axis, other, n, gather, x_ref, o_ref, land, send_sem, recv_sem):
    me = lax.axis_index(axis)
    fixed = lax.axis_index(other)

    def peer(j):
        if axis == "dp":
            return (j, fixed)
        return (fixed, j)

    barrier = pltpu.get_barrier_semaphore()

    @pl.loop(0, n)
    def _(j):
        @pl.when(j != me)
        def _():
            pl.semaphore_signal(barrier, inc=1, device_id=peer(j), device_id_type=pl.DeviceIdType.MESH)

    pl.semaphore_wait(barrier, n - 1)

    def copy_to(j):
        src = x_ref if gather else x_ref.at[j]
        return pltpu.make_async_remote_copy(
            src_ref=src,
            dst_ref=land.at[me],
            send_sem=send_sem.at[j],
            recv_sem=recv_sem.at[me],
            device_id=peer(j),
            device_id_type=pl.DeviceIdType.MESH,
        )

    @pl.loop(0, n)
    def _(j):
        @pl.when(j != me)
        def _():
            copy_to(j).start()

    own = x_ref[...] if gather else x_ref[me]
    o_ref[me] = own

    def arrived(j):
        src = x_ref if gather else x_ref.at[j]
        return pltpu.make_async_remote_copy(
            src_ref=src,
            dst_ref=land.at[j],
            send_sem=send_sem.at[j],
            recv_sem=recv_sem.at[j],
            device_id=peer(j),
            device_id_type=pl.DeviceIdType.MESH,
        )

    @pl.loop(0, n)
    def _(j):
        @pl.when(j != me)
        def _():
            arrived(j).wait_recv()
            o_ref[j] = land[j]
            copy_to(j).wait_send()


def exchange(x, axis, n, collective_id, gather=False):
    other = "expert" if axis == "dp" else "dp"
    block = x.shape if gather else x.shape[1:]
    out_shape = jax.ShapeDtypeStruct((n,) + tuple(block), x.dtype)
    return pl.pallas_call(
        functools.partial(_exchange_kernel, axis, other, n, gather),
        out_shape=out_shape,
        in_specs=[pl.BlockSpec(memory_space=pltpu.VMEM)],
        out_specs=pl.BlockSpec(memory_space=pltpu.VMEM),
        scratch_shapes=[
            pltpu.VMEM(out_shape.shape, x.dtype),
            pltpu.SemaphoreType.DMA((n,)),
            pltpu.SemaphoreType.DMA((n,)),
        ],
        compiler_params=pltpu.CompilerParams(collective_id=collective_id, has_side_effects=True),
    )(x)


def _row_exchange_kernel(n, rows, x_ref, o_ref, land, send_sem, recv_sem, own_sem):
    me = lax.axis_index("expert")
    fixed = lax.axis_index("dp")
    mesh_id = pl.DeviceIdType.MESH
    barrier = pltpu.get_barrier_semaphore()

    @pl.loop(0, n)
    def _(j):
        @pl.when(j != me)
        def _():
            pl.semaphore_signal(barrier, inc=1, device_id=(fixed, j), device_id_type=mesh_id)

    pl.semaphore_wait(barrier, n - 1)

    def block(ref, j):
        return ref.at[pl.ds(j * rows, rows)]

    def copy_to(j, slot):
        return pltpu.make_async_remote_copy(
            src_ref=block(x_ref, j), dst_ref=block(land, slot), send_sem=send_sem.at[j],
            recv_sem=recv_sem.at[slot], device_id=(fixed, j), device_id_type=mesh_id)

    @pl.loop(0, n)
    def _(j):
        @pl.when(j != me)
        def _():
            copy_to(j, me).start()

    own = pltpu.make_async_copy(block(x_ref, me), block(land, me), own_sem)
    own.start()

    @pl.loop(0, n)
    def _(j):
        @pl.when(j != me)
        def _():
            copy_to(j, j).wait_recv()
            copy_to(j, me).wait_send()

    own.wait()
    o_ref[...] = land[...]


def row_exchange(x, n, collective_id):
    return pl.pallas_call(
        functools.partial(_row_exchange_kernel, n, x.shape[0] // n),
        out_shape=jax.ShapeDtypeStruct(x.shape, x.dtype),
        in_specs=[pl.BlockSpec(memory_space=pltpu.VMEM)],
        out_specs=pl.BlockSpec(memory_space=pltpu.VMEM),
        scratch_shapes=[
            pltpu.VMEM(x.shape, x.dtype),
            pltpu.SemaphoreType.DMA((n,)),
            pltpu.SemaphoreType.DMA((n,)),
            pltpu.SemaphoreType.DMA(()),
        ],
        compiler_params=pltpu.CompilerParams(collective_id=collective_id, has_side_effects=True),
    )(x)


def gelu_exact(values):
    return jax.nn.gelu(values, approximate=False)


def _allsum_kernel(n_dp, n_ex, x_ref, o_ref, land1, land2, land3, red1, red2, s1, r1, s2, r2, s3, r3):
    me_d = lax.axis_index("dp")
    me_e = lax.axis_index("expert")
    mesh_id = pl.DeviceIdType.MESH
    barrier = pltpu.get_barrier_semaphore()

    @pl.loop(0, n_ex)
    def _(j):
        @pl.when(j != me_e)
        def _():
            pl.semaphore_signal(barrier, inc=1, device_id=(me_d, j), device_id_type=mesh_id)

    @pl.loop(0, n_dp)
    def _(k):
        @pl.when(k != me_d)
        def _():
            pl.semaphore_signal(barrier, inc=1, device_id=(k, me_e), device_id_type=mesh_id)

    pl.semaphore_wait(barrier, n_ex - 1 + n_dp - 1)

    def ex_copy(src, land, send, recv, j, slot):
        return pltpu.make_async_remote_copy(
            src_ref=src, dst_ref=land.at[slot], send_sem=send.at[j], recv_sem=recv.at[slot],
            device_id=(me_d, j), device_id_type=mesh_id)

    def dp_copy(src, land, send, recv, k, slot):
        return pltpu.make_async_remote_copy(
            src_ref=src, dst_ref=land.at[slot], send_sem=send.at[k], recv_sem=recv.at[slot],
            device_id=(k, me_e), device_id_type=mesh_id)

    @pl.loop(0, n_ex)
    def _(j):
        @pl.when(j != me_e)
        def _():
            ex_copy(x_ref.at[j], land1, s1, r1, j, me_e).start()

    land1[me_e] = x_ref[me_e]

    @pl.loop(0, n_ex)
    def _(j):
        @pl.when(j != me_e)
        def _():
            ex_copy(x_ref.at[j], land1, s1, r1, j, j).wait_recv()
            ex_copy(x_ref.at[j], land1, s1, r1, j, me_e).wait_send()

    red1[...] = jnp.sum(land1[...].astype(jnp.float32), axis=0).astype(red1.dtype)

    @pl.loop(0, n_dp)
    def _(k):
        @pl.when(k != me_d)
        def _():
            dp_copy(red1, land2, s2, r2, k, me_d).start()

    land2[me_d] = red1[...]

    @pl.loop(0, n_dp)
    def _(k):
        @pl.when(k != me_d)
        def _():
            dp_copy(red1, land2, s2, r2, k, k).wait_recv()
            dp_copy(red1, land2, s2, r2, k, me_d).wait_send()

    total = land2[0].astype(jnp.float32)
    for k in range(1, n_dp):
        total = total + land2[k].astype(jnp.float32)
    red2[...] = total.astype(red2.dtype)

    @pl.loop(0, n_ex)
    def _(j):
        @pl.when(j != me_e)
        def _():
            ex_copy(red2, land3, s3, r3, j, me_e).start()

    o_ref[me_e] = red2[...]

    @pl.loop(0, n_ex)
    def _(j):
        @pl.when(j != me_e)
        def _():
            ex_copy(red2, land3, s3, r3, j, j).wait_recv()
            o_ref[j] = land3[j]
            ex_copy(red2, land3, s3, r3, j, me_e).wait_send()


def all_sum(value, n_dp, n_expert):
    rows, cols = value.shape
    block = (rows // n_expert, cols)
    chunks = value.astype(jnp.bfloat16).reshape(n_expert, *block)
    out = pl.pallas_call(
        functools.partial(_allsum_kernel, n_dp, n_expert),
        out_shape=jax.ShapeDtypeStruct(chunks.shape, chunks.dtype),
        in_specs=[pl.BlockSpec(memory_space=pltpu.VMEM)],
        out_specs=pl.BlockSpec(memory_space=pltpu.VMEM),
        scratch_shapes=[
            pltpu.VMEM(chunks.shape, chunks.dtype),
            pltpu.VMEM((n_dp,) + block, chunks.dtype),
            pltpu.VMEM(chunks.shape, chunks.dtype),
            pltpu.VMEM(block, chunks.dtype),
            pltpu.VMEM(block, chunks.dtype),
            pltpu.SemaphoreType.DMA((n_expert,)),
            pltpu.SemaphoreType.DMA((n_expert,)),
            pltpu.SemaphoreType.DMA((n_dp,)),
            pltpu.SemaphoreType.DMA((n_dp,)),
            pltpu.SemaphoreType.DMA((n_expert,)),
            pltpu.SemaphoreType.DMA((n_expert,)),
        ],
        compiler_params=pltpu.CompilerParams(collective_id=4, has_side_effects=True),
    )(chunks)
    return out.reshape(rows, cols).astype(value.dtype)


def _tail_kernel(n_dp, n_ex, rows, summed_ref, tok_ref, tokt_ref, prob_ref, comb_ref, disp_ref, router_ref,
                 gtok_ref, o_ref,
                 land0, xs, land1, land2, land3, red1, red2, s0, r0, own_sem, s1, r1, s2, r2, s3, r3):
    me_d = lax.axis_index("dp")
    me_e = lax.axis_index("expert")
    mesh_id = pl.DeviceIdType.MESH
    barrier = pltpu.get_barrier_semaphore()

    @pl.loop(0, n_ex)
    def _(j):
        @pl.when(j != me_e)
        def _():
            pl.semaphore_signal(barrier, inc=1, device_id=(me_d, j), device_id_type=mesh_id)

    @pl.loop(0, n_dp)
    def _(k):
        @pl.when(k != me_d)
        def _():
            pl.semaphore_signal(barrier, inc=1, device_id=(k, me_e), device_id_type=mesh_id)

    pl.semaphore_wait(barrier, n_ex - 1 + n_dp - 1)

    def row_copy(j, slot):
        return pltpu.make_async_remote_copy(
            src_ref=summed_ref.at[pl.ds(j * rows, rows)], dst_ref=land0.at[pl.ds(slot * rows, rows)],
            send_sem=s0.at[j], recv_sem=r0.at[slot], device_id=(me_d, j), device_id_type=mesh_id)

    @pl.loop(0, n_ex)
    def _(j):
        @pl.when(j != me_e)
        def _():
            row_copy(j, me_e).start()

    own = pltpu.make_async_copy(
        summed_ref.at[pl.ds(me_e * rows, rows)], land0.at[pl.ds(me_e * rows, rows)], own_sem)
    own.start()

    @pl.loop(0, n_ex)
    def _(j):
        @pl.when(j != me_e)
        def _():
            row_copy(j, j).wait_recv()
            row_copy(j, me_e).wait_send()

    own.wait()
    gsa = land0[...]
    prob = prob_ref[...]
    grad_disp = lax.dot_general(tok_ref[...], gsa, (((1,), (1,)), ((), ())), preferred_element_type=jnp.float32)
    part_disp = prob * (grad_disp - jnp.sum(prob * grad_disp, axis=0, keepdims=True))
    logits = (part_disp + comb_ref[...]).astype(jnp.bfloat16)
    term = jnp.dot(tokt_ref[...], logits, preferred_element_type=jnp.float32)
    xs[...] = term.astype(xs.dtype).reshape(xs.shape)

    def ex_copy(src, land, send, recv, j, slot):
        return pltpu.make_async_remote_copy(
            src_ref=src, dst_ref=land.at[slot], send_sem=send.at[j], recv_sem=recv.at[slot],
            device_id=(me_d, j), device_id_type=mesh_id)

    def dp_copy(src, land, send, recv, k, slot):
        return pltpu.make_async_remote_copy(
            src_ref=src, dst_ref=land.at[slot], send_sem=send.at[k], recv_sem=recv.at[slot],
            device_id=(k, me_e), device_id_type=mesh_id)

    @pl.loop(0, n_ex)
    def _(j):
        @pl.when(j != me_e)
        def _():
            ex_copy(xs.at[j], land1, s1, r1, j, me_e).start()

    land1[me_e] = xs[me_e]
    back = jnp.dot(disp_ref[...], gsa, preferred_element_type=jnp.float32)
    back = back + lax.dot_general(logits, router_ref[...], (((1,), (1,)), ((), ())), preferred_element_type=jnp.float32)
    gtok_ref[...] = back.astype(gtok_ref.dtype)

    @pl.loop(0, n_ex)
    def _(j):
        @pl.when(j != me_e)
        def _():
            ex_copy(xs.at[j], land1, s1, r1, j, j).wait_recv()
            ex_copy(xs.at[j], land1, s1, r1, j, me_e).wait_send()

    red1[...] = jnp.sum(land1[...].astype(jnp.float32), axis=0).astype(red1.dtype)

    @pl.loop(0, n_dp)
    def _(k):
        @pl.when(k != me_d)
        def _():
            dp_copy(red1, land2, s2, r2, k, me_d).start()

    land2[me_d] = red1[...]

    @pl.loop(0, n_dp)
    def _(k):
        @pl.when(k != me_d)
        def _():
            dp_copy(red1, land2, s2, r2, k, k).wait_recv()
            dp_copy(red1, land2, s2, r2, k, me_d).wait_send()

    total = land2[0].astype(jnp.float32)
    for k in range(1, n_dp):
        total = total + land2[k].astype(jnp.float32)
    red2[...] = total.astype(red2.dtype)

    @pl.loop(0, n_ex)
    def _(j):
        @pl.when(j != me_e)
        def _():
            ex_copy(red2, land3, s3, r3, j, me_e).start()

    o_ref[me_e] = red2[...]

    @pl.loop(0, n_ex)
    def _(j):
        @pl.when(j != me_e)
        def _():
            ex_copy(red2, land3, s3, r3, j, j).wait_recv()
            o_ref[j] = land3[j]
            ex_copy(red2, land3, s3, r3, j, me_e).wait_send()


def tail(summed, tokens, tokens_t, prob, part_comb, dispatch, router, n_dp, n_ex):
    width, experts = tokens_t.shape[0], prob.shape[1]
    block = (width // n_ex, experts)
    chunks = (n_ex,) + block
    bf = jnp.bfloat16
    vmem = pl.BlockSpec(memory_space=pltpu.VMEM)
    grad_tokens, out = pl.pallas_call(
        functools.partial(_tail_kernel, n_dp, n_ex, summed.shape[0] // n_ex),
        out_shape=(jax.ShapeDtypeStruct(tokens.shape, bf),
                   jax.ShapeDtypeStruct(chunks, bf)),
        in_specs=[vmem] * 7,
        out_specs=(vmem, vmem),
        scratch_shapes=[
            pltpu.VMEM(summed.shape, summed.dtype),
            pltpu.VMEM(chunks, bf),
            pltpu.VMEM(chunks, bf),
            pltpu.VMEM((n_dp,) + block, bf),
            pltpu.VMEM(chunks, bf),
            pltpu.VMEM(block, bf),
            pltpu.VMEM(block, bf),
            pltpu.SemaphoreType.DMA((n_ex,)),
            pltpu.SemaphoreType.DMA((n_ex,)),
            pltpu.SemaphoreType.DMA(()),
            pltpu.SemaphoreType.DMA((n_ex,)),
            pltpu.SemaphoreType.DMA((n_ex,)),
            pltpu.SemaphoreType.DMA((n_dp,)),
            pltpu.SemaphoreType.DMA((n_dp,)),
            pltpu.SemaphoreType.DMA((n_ex,)),
            pltpu.SemaphoreType.DMA((n_ex,)),
        ],
        compiler_params=pltpu.CompilerParams(collective_id=5, has_side_effects=True),
    )(summed, tokens, tokens_t, prob, part_comb, dispatch, router)
    return grad_tokens, out.reshape(width, experts).astype(jnp.float32)


def local(n_dp, n_expert, tokens, router, weight_in, weight_out, cotangent):
    experts_dev = weight_in.shape[0]
    width = tokens.shape[2]
    logits = jnp.einsum("isd,de->ise", tokens, router, preferred_element_type=jnp.float32)
    dispatch_prob = jax.nn.softmax(logits, axis=1)
    combine_prob = jax.nn.softmax(logits, axis=2)
    dispatch = dispatch_prob.astype(jnp.bfloat16)
    combine = combine_prob.astype(jnp.bfloat16)
    slots = jnp.einsum("ise,isd->ied", dispatch, tokens, preferred_element_type=jnp.float32).astype(
        jnp.bfloat16
    )
    grad_slots = jnp.einsum(
        "ise,isd->ied", combine, cotangent, preferred_element_type=jnp.float32
    ).astype(jnp.bfloat16)

    def to_owners(local_rows, cid):
        arrived = row_exchange(local_rows[0], n_expert, cid)[None]
        return lax.all_gather(arrived, "dp", axis=0, tiled=True)

    def from_owners(partial_value, cid):
        summed = lax.psum_scatter(partial_value, "dp", scatter_dimension=0, tiled=True)
        return row_exchange(summed[0], n_expert, cid)[None]

    slot_rows = to_owners(slots, 0)
    blocks = slot_rows.reshape(-1, experts_dev, width)
    pre_act = jnp.einsum("rkd,kdf->rkf", blocks, weight_in, preferred_element_type=jnp.float32)
    hidden = gelu_exact(pre_act).astype(jnp.bfloat16)
    partial_value = jnp.einsum(
        "rkf,kfd->rkd", hidden, weight_out, preferred_element_type=jnp.float32
    )
    blocks, pre_act, hidden, partial_value = (
        blocks,
        pre_act,
        hidden,
        partial_value.astype(jnp.bfloat16).reshape(slot_rows.shape),
    )
    expert_outs = from_owners(partial_value, 2)
    grad_rows = to_owners(grad_slots, 1)
    grad_blocks = grad_rows.reshape(blocks.shape)
    grad_hidden = jnp.einsum(
        "rkd,kfd->rkf", grad_blocks, weight_out, preferred_element_type=jnp.float32
    )
    _, gelu_back = jax.vjp(gelu_exact, pre_act)
    grad_pre = gelu_back(grad_hidden)[0].astype(jnp.bfloat16)
    grad_second = jnp.einsum(
        "rkf,rkd->kfd", hidden, grad_blocks, preferred_element_type=jnp.float32
    ).astype(jnp.bfloat16)
    grad_first = jnp.einsum(
        "rkd,rkf->kdf", blocks, grad_pre, preferred_element_type=jnp.float32
    ).astype(jnp.bfloat16)
    partial_back = jnp.einsum(
        "rkf,kdf->rkd", grad_pre, weight_in, preferred_element_type=jnp.float32
    )
    grad_first, grad_second, partial_back = (
        grad_first,
        grad_second,
        partial_back.astype(jnp.bfloat16).reshape(grad_rows.shape),
    )
    summed_back = lax.psum_scatter(partial_back, "dp", scatter_dimension=0, tiled=True)[0]
    mixed = jnp.einsum(
        "ise,ied->isd", combine, expert_outs, preferred_element_type=jnp.float32
    ).astype(jnp.bfloat16)
    grad_comb = jnp.einsum(
        "isd,ied->ise", cotangent, expert_outs, preferred_element_type=jnp.float32
    )
    part_comb = combine_prob * (
        grad_comb - jnp.sum(combine_prob * grad_comb, axis=2, keepdims=True)
    )
    grad_tokens, grad_router = tail(
        summed_back, tokens[0], tokens[0].T, dispatch_prob[0], part_comb[0], dispatch[0], router,
        n_dp, n_expert,
    )
    grad_tokens = grad_tokens[None]
    return (mixed, grad_tokens, grad_router, grad_first, grad_second)


def solution(mesh):
    return jax.shard_map(
        functools.partial(local, mesh.shape["dp"], mesh.shape["expert"]),
        mesh=mesh,
        in_specs=(
            P(("dp", "expert"), None, None),
            P(),
            P("expert", None, "dp"),
            P("expert", "dp", None),
            P(("dp", "expert"), None, None),
        ),
        out_specs=(
            P(("dp", "expert"), None, None),
            P(("dp", "expert"), None, None),
            P(),
            P("expert", None, "dp"),
            P("expert", "dp", None),
        ),
        check_vma=False,
    )
```

```python
import functools

import jax
import jax.numpy as jnp
from jax import lax
from jax.experimental import pallas as pl
from jax.experimental.pallas import tpu as pltpu
from jax.sharding import PartitionSpec as P


def _exchange_kernel(axis, other, n, gather, x_ref, o_ref, land, send_sem, recv_sem):
    me = lax.axis_index(axis)
    fixed = lax.axis_index(other)

    def peer(j):
        if axis == "dp":
            return (j, fixed)
        return (fixed, j)

    barrier = pltpu.get_barrier_semaphore()

    @pl.loop(0, n)
    def _(j):
        @pl.when(j != me)
        def _():
            pl.semaphore_signal(barrier, inc=1, device_id=peer(j), device_id_type=pl.DeviceIdType.MESH)

    pl.semaphore_wait(barrier, n - 1)

    def copy_to(j):
        src = x_ref if gather else x_ref.at[j]
        return pltpu.make_async_remote_copy(
            src_ref=src,
            dst_ref=land.at[me],
            send_sem=send_sem.at[j],
            recv_sem=recv_sem.at[me],
            device_id=peer(j),
            device_id_type=pl.DeviceIdType.MESH,
        )

    @pl.loop(0, n)
    def _(j):
        @pl.when(j != me)
        def _():
            copy_to(j).start()

    own = x_ref[...] if gather else x_ref[me]
    o_ref[me] = own

    def arrived(j):
        src = x_ref if gather else x_ref.at[j]
        return pltpu.make_async_remote_copy(
            src_ref=src,
            dst_ref=land.at[j],
            send_sem=send_sem.at[j],
            recv_sem=recv_sem.at[j],
            device_id=peer(j),
            device_id_type=pl.DeviceIdType.MESH,
        )

    @pl.loop(0, n)
    def _(j):
        @pl.when(j != me)
        def _():
            arrived(j).wait_recv()
            o_ref[j] = land[j]
            copy_to(j).wait_send()


def exchange(x, axis, n, collective_id, gather=False):
    other = "expert" if axis == "dp" else "dp"
    block = x.shape if gather else x.shape[1:]
    out_shape = jax.ShapeDtypeStruct((n,) + tuple(block), x.dtype)
    return pl.pallas_call(
        functools.partial(_exchange_kernel, axis, other, n, gather),
        out_shape=out_shape,
        in_specs=[pl.BlockSpec(memory_space=pltpu.VMEM)],
        out_specs=pl.BlockSpec(memory_space=pltpu.VMEM),
        scratch_shapes=[
            pltpu.VMEM(out_shape.shape, x.dtype),
            pltpu.SemaphoreType.DMA((n,)),
            pltpu.SemaphoreType.DMA((n,)),
        ],
        compiler_params=pltpu.CompilerParams(collective_id=collective_id, has_side_effects=True),
    )(x)


def _row_exchange_kernel(n, rows, x_ref, o_ref, land, send_sem, recv_sem, own_sem):
    me = lax.axis_index("expert")
    fixed = lax.axis_index("dp")
    mesh_id = pl.DeviceIdType.MESH
    barrier = pltpu.get_barrier_semaphore()

    @pl.loop(0, n)
    def _(j):
        @pl.when(j != me)
        def _():
            pl.semaphore_signal(barrier, inc=1, device_id=(fixed, j), device_id_type=mesh_id)

    pl.semaphore_wait(barrier, n - 1)

    def block(ref, j):
        return ref.at[pl.ds(j * rows, rows)]

    def copy_to(j, slot):
        return pltpu.make_async_remote_copy(
            src_ref=block(x_ref, j), dst_ref=block(land, slot), send_sem=send_sem.at[j],
            recv_sem=recv_sem.at[slot], device_id=(fixed, j), device_id_type=mesh_id)

    @pl.loop(0, n)
    def _(j):
        @pl.when(j != me)
        def _():
            copy_to(j, me).start()

    own = pltpu.make_async_copy(block(x_ref, me), block(land, me), own_sem)
    own.start()

    @pl.loop(0, n)
    def _(j):
        @pl.when(j != me)
        def _():
            copy_to(j, j).wait_recv()
            copy_to(j, me).wait_send()

    own.wait()
    o_ref[...] = land[...]


def row_exchange(x, n, collective_id):
    return pl.pallas_call(
        functools.partial(_row_exchange_kernel, n, x.shape[0] // n),
        out_shape=jax.ShapeDtypeStruct(x.shape, x.dtype),
        in_specs=[pl.BlockSpec(memory_space=pltpu.VMEM)],
        out_specs=pl.BlockSpec(memory_space=pltpu.VMEM),
        scratch_shapes=[
            pltpu.VMEM(x.shape, x.dtype),
            pltpu.SemaphoreType.DMA((n,)),
            pltpu.SemaphoreType.DMA((n,)),
            pltpu.SemaphoreType.DMA(()),
        ],
        compiler_params=pltpu.CompilerParams(collective_id=collective_id, has_side_effects=True),
    )(x)


def gelu_exact(values):
    return jax.nn.gelu(values, approximate=False)


def _relay_sum_kernel(n_chip, x_ref, o_ref, land1, pair, land2, s1, r1, s2, r2):
    me = lax.axis_index("dp")
    fixed = lax.axis_index("expert")
    core = me % 2
    chip = me // 2
    partner = me + 1 - 2 * core
    mesh_id = pl.DeviceIdType.MESH
    barrier = pltpu.get_barrier_semaphore()
    pl.semaphore_signal(barrier, inc=1, device_id=(partner, fixed), device_id_type=mesh_id)
    for h in range(n_chip):
        @pl.when(h != chip)
        def _():
            pl.semaphore_signal(barrier, inc=1, device_id=(2 * h + core, fixed), device_id_type=mesh_id)
    pl.semaphore_wait(barrier, n_chip)

    def to_partner(h):
        return pltpu.make_async_remote_copy(
            src_ref=x_ref.at[2 * h + 1 - core], dst_ref=land1.at[h], send_sem=s1.at[h], recv_sem=r1.at[h],
            device_id=(partner, fixed), device_id_type=mesh_id)

    for h in range(n_chip):
        to_partner(h).start()
    for h in range(n_chip):
        to_partner(h).wait_recv()
        pair[h] = (x_ref[2 * h + core].astype(jnp.float32) + land1[h].astype(jnp.float32)).astype(pair.dtype)
        to_partner(h).wait_send()

    def to_chip(h, slot):
        return pltpu.make_async_remote_copy(
            src_ref=pair.at[h], dst_ref=land2.at[slot], send_sem=s2.at[h], recv_sem=r2.at[slot],
            device_id=(2 * h + core, fixed), device_id_type=mesh_id)

    for h in range(n_chip):
        @pl.when(h != chip)
        def _():
            to_chip(h, chip).start()
    land2[chip] = pair[chip]
    for h in range(n_chip):
        @pl.when(h != chip)
        def _():
            to_chip(h, h).wait_recv()
            to_chip(h, chip).wait_send()
    total = land2[0].astype(jnp.float32)
    for h in range(1, n_chip):
        total = total + land2[h].astype(jnp.float32)
    o_ref[...] = total.astype(o_ref.dtype)


def relay_sum(x, collective_id):
    n_dp = x.shape[0]
    n_chip = n_dp // 2
    block = x.shape[1:]
    return pl.pallas_call(
        functools.partial(_relay_sum_kernel, n_chip),
        out_shape=jax.ShapeDtypeStruct(block, x.dtype),
        in_specs=[pl.BlockSpec(memory_space=pltpu.VMEM)],
        out_specs=pl.BlockSpec(memory_space=pltpu.VMEM),
        scratch_shapes=[
            pltpu.VMEM((n_chip,) + block, x.dtype),
            pltpu.VMEM((n_chip,) + block, x.dtype),
            pltpu.VMEM((n_chip,) + block, x.dtype),
            pltpu.SemaphoreType.DMA((n_chip,)),
            pltpu.SemaphoreType.DMA((n_chip,)),
            pltpu.SemaphoreType.DMA((n_chip,)),
            pltpu.SemaphoreType.DMA((n_chip,)),
        ],
        compiler_params=pltpu.CompilerParams(collective_id=collective_id, has_side_effects=True),
    )(x)


def _allsum_kernel(n_dp, n_ex, x_ref, o_ref, land1, land2, land3, red1, red2, s1, r1, s2, r2, s3, r3):
    me_d = lax.axis_index("dp")
    me_e = lax.axis_index("expert")
    mesh_id = pl.DeviceIdType.MESH
    barrier = pltpu.get_barrier_semaphore()

    @pl.loop(0, n_ex)
    def _(j):
        @pl.when(j != me_e)
        def _():
            pl.semaphore_signal(barrier, inc=1, device_id=(me_d, j), device_id_type=mesh_id)

    @pl.loop(0, n_dp)
    def _(k):
        @pl.when(k != me_d)
        def _():
            pl.semaphore_signal(barrier, inc=1, device_id=(k, me_e), device_id_type=mesh_id)

    pl.semaphore_wait(barrier, n_ex - 1 + n_dp - 1)

    def ex_copy(src, land, send, recv, j, slot):
        return pltpu.make_async_remote_copy(
            src_ref=src, dst_ref=land.at[slot], send_sem=send.at[j], recv_sem=recv.at[slot],
            device_id=(me_d, j), device_id_type=mesh_id)

    def dp_copy(src, land, send, recv, k, slot):
        return pltpu.make_async_remote_copy(
            src_ref=src, dst_ref=land.at[slot], send_sem=send.at[k], recv_sem=recv.at[slot],
            device_id=(k, me_e), device_id_type=mesh_id)

    @pl.loop(0, n_ex)
    def _(j):
        @pl.when(j != me_e)
        def _():
            ex_copy(x_ref.at[j], land1, s1, r1, j, me_e).start()

    land1[me_e] = x_ref[me_e]

    @pl.loop(0, n_ex)
    def _(j):
        @pl.when(j != me_e)
        def _():
            ex_copy(x_ref.at[j], land1, s1, r1, j, j).wait_recv()
            ex_copy(x_ref.at[j], land1, s1, r1, j, me_e).wait_send()

    red1[...] = jnp.sum(land1[...].astype(jnp.float32), axis=0).astype(red1.dtype)

    @pl.loop(0, n_dp)
    def _(k):
        @pl.when(k != me_d)
        def _():
            dp_copy(red1, land2, s2, r2, k, me_d).start()

    land2[me_d] = red1[...]

    @pl.loop(0, n_dp)
    def _(k):
        @pl.when(k != me_d)
        def _():
            dp_copy(red1, land2, s2, r2, k, k).wait_recv()
            dp_copy(red1, land2, s2, r2, k, me_d).wait_send()

    total = land2[0].astype(jnp.float32)
    for k in range(1, n_dp):
        total = total + land2[k].astype(jnp.float32)
    red2[...] = total.astype(red2.dtype)

    @pl.loop(0, n_ex)
    def _(j):
        @pl.when(j != me_e)
        def _():
            ex_copy(red2, land3, s3, r3, j, me_e).start()

    o_ref[me_e] = red2[...]

    @pl.loop(0, n_ex)
    def _(j):
        @pl.when(j != me_e)
        def _():
            ex_copy(red2, land3, s3, r3, j, j).wait_recv()
            o_ref[j] = land3[j]
            ex_copy(red2, land3, s3, r3, j, me_e).wait_send()


def all_sum(value, n_dp, n_expert):
    rows, cols = value.shape
    block = (rows // n_expert, cols)
    chunks = value.astype(jnp.bfloat16).reshape(n_expert, *block)
    out = pl.pallas_call(
        functools.partial(_allsum_kernel, n_dp, n_expert),
        out_shape=jax.ShapeDtypeStruct(chunks.shape, chunks.dtype),
        in_specs=[pl.BlockSpec(memory_space=pltpu.VMEM)],
        out_specs=pl.BlockSpec(memory_space=pltpu.VMEM),
        scratch_shapes=[
            pltpu.VMEM(chunks.shape, chunks.dtype),
            pltpu.VMEM((n_dp,) + block, chunks.dtype),
            pltpu.VMEM(chunks.shape, chunks.dtype),
            pltpu.VMEM(block, chunks.dtype),
            pltpu.VMEM(block, chunks.dtype),
            pltpu.SemaphoreType.DMA((n_expert,)),
            pltpu.SemaphoreType.DMA((n_expert,)),
            pltpu.SemaphoreType.DMA((n_dp,)),
            pltpu.SemaphoreType.DMA((n_dp,)),
            pltpu.SemaphoreType.DMA((n_expert,)),
            pltpu.SemaphoreType.DMA((n_expert,)),
        ],
        compiler_params=pltpu.CompilerParams(collective_id=4, has_side_effects=True),
    )(chunks)
    return out.reshape(rows, cols).astype(value.dtype)


def _tail_kernel(n_dp, n_ex, rows, summed_ref, tok_ref, tokt_ref, prob_ref, comb_ref,
                 gsa_ref, logit_ref, o_ref,
                 land0, xs, land1, land2, land3, red1, red2, s0, r0, own_sem, s1, r1, s2, r2, s3, r3):
    me_d = lax.axis_index("dp")
    me_e = lax.axis_index("expert")
    mesh_id = pl.DeviceIdType.MESH
    barrier = pltpu.get_barrier_semaphore()

    @pl.loop(0, n_ex)
    def _(j):
        @pl.when(j != me_e)
        def _():
            pl.semaphore_signal(barrier, inc=1, device_id=(me_d, j), device_id_type=mesh_id)

    @pl.loop(0, n_dp)
    def _(k):
        @pl.when(k != me_d)
        def _():
            pl.semaphore_signal(barrier, inc=1, device_id=(k, me_e), device_id_type=mesh_id)

    pl.semaphore_wait(barrier, n_ex - 1 + n_dp - 1)

    def row_copy(j, slot):
        return pltpu.make_async_remote_copy(
            src_ref=summed_ref.at[pl.ds(j * rows, rows)], dst_ref=land0.at[pl.ds(slot * rows, rows)],
            send_sem=s0.at[j], recv_sem=r0.at[slot], device_id=(me_d, j), device_id_type=mesh_id)

    @pl.loop(0, n_ex)
    def _(j):
        @pl.when(j != me_e)
        def _():
            row_copy(j, me_e).start()

    own = pltpu.make_async_copy(
        summed_ref.at[pl.ds(me_e * rows, rows)], land0.at[pl.ds(me_e * rows, rows)], own_sem)
    own.start()

    @pl.loop(0, n_ex)
    def _(j):
        @pl.when(j != me_e)
        def _():
            row_copy(j, j).wait_recv()
            row_copy(j, me_e).wait_send()

    own.wait()
    gsa = land0[...]
    gsa_ref[...] = gsa
    prob = prob_ref[...]
    grad_disp = lax.dot_general(tok_ref[...], gsa, (((1,), (1,)), ((), ())), preferred_element_type=jnp.float32)
    part_disp = prob * (grad_disp - jnp.sum(prob * grad_disp, axis=0, keepdims=True))
    logits = (part_disp + comb_ref[...]).astype(logit_ref.dtype)
    logit_ref[...] = logits
    term = jnp.dot(tokt_ref[...], logits, preferred_element_type=jnp.float32)
    xs[...] = term.astype(xs.dtype).reshape(xs.shape)

    def ex_copy(src, land, send, recv, j, slot):
        return pltpu.make_async_remote_copy(
            src_ref=src, dst_ref=land.at[slot], send_sem=send.at[j], recv_sem=recv.at[slot],
            device_id=(me_d, j), device_id_type=mesh_id)

    def dp_copy(src, land, send, recv, k, slot):
        return pltpu.make_async_remote_copy(
            src_ref=src, dst_ref=land.at[slot], send_sem=send.at[k], recv_sem=recv.at[slot],
            device_id=(k, me_e), device_id_type=mesh_id)

    @pl.loop(0, n_ex)
    def _(j):
        @pl.when(j != me_e)
        def _():
            ex_copy(xs.at[j], land1, s1, r1, j, me_e).start()

    land1[me_e] = xs[me_e]

    @pl.loop(0, n_ex)
    def _(j):
        @pl.when(j != me_e)
        def _():
            ex_copy(xs.at[j], land1, s1, r1, j, j).wait_recv()
            ex_copy(xs.at[j], land1, s1, r1, j, me_e).wait_send()

    red1[...] = jnp.sum(land1[...].astype(jnp.float32), axis=0).astype(red1.dtype)

    @pl.loop(0, n_dp)
    def _(k):
        @pl.when(k != me_d)
        def _():
            dp_copy(red1, land2, s2, r2, k, me_d).start()

    land2[me_d] = red1[...]

    @pl.loop(0, n_dp)
    def _(k):
        @pl.when(k != me_d)
        def _():
            dp_copy(red1, land2, s2, r2, k, k).wait_recv()
            dp_copy(red1, land2, s2, r2, k, me_d).wait_send()

    total = land2[0].astype(jnp.float32)
    for k in range(1, n_dp):
        total = total + land2[k].astype(jnp.float32)
    red2[...] = total.astype(red2.dtype)

    @pl.loop(0, n_ex)
    def _(j):
        @pl.when(j != me_e)
        def _():
            ex_copy(red2, land3, s3, r3, j, me_e).start()

    o_ref[me_e] = red2[...]

    @pl.loop(0, n_ex)
    def _(j):
        @pl.when(j != me_e)
        def _():
            ex_copy(red2, land3, s3, r3, j, j).wait_recv()
            o_ref[j] = land3[j]
            ex_copy(red2, land3, s3, r3, j, me_e).wait_send()


def tail(summed, tokens, tokens_t, prob, part_comb, n_dp, n_ex):
    width, experts = tokens_t.shape[0], prob.shape[1]
    block = (width // n_ex, experts)
    chunks = (n_ex,) + block
    bf = jnp.bfloat16
    vmem = pl.BlockSpec(memory_space=pltpu.VMEM)
    gsa, logits, out = pl.pallas_call(
        functools.partial(_tail_kernel, n_dp, n_ex, summed.shape[0] // n_ex),
        out_shape=(jax.ShapeDtypeStruct(summed.shape, summed.dtype),
                   jax.ShapeDtypeStruct(prob.shape, bf),
                   jax.ShapeDtypeStruct(chunks, bf)),
        in_specs=[vmem] * 5,
        out_specs=(vmem, vmem, vmem),
        scratch_shapes=[
            pltpu.VMEM(summed.shape, summed.dtype),
            pltpu.VMEM(chunks, bf),
            pltpu.VMEM(chunks, bf),
            pltpu.VMEM((n_dp,) + block, bf),
            pltpu.VMEM(chunks, bf),
            pltpu.VMEM(block, bf),
            pltpu.VMEM(block, bf),
            pltpu.SemaphoreType.DMA((n_ex,)),
            pltpu.SemaphoreType.DMA((n_ex,)),
            pltpu.SemaphoreType.DMA(()),
            pltpu.SemaphoreType.DMA((n_ex,)),
            pltpu.SemaphoreType.DMA((n_ex,)),
            pltpu.SemaphoreType.DMA((n_dp,)),
            pltpu.SemaphoreType.DMA((n_dp,)),
            pltpu.SemaphoreType.DMA((n_ex,)),
            pltpu.SemaphoreType.DMA((n_ex,)),
        ],
        compiler_params=pltpu.CompilerParams(collective_id=5, has_side_effects=True),
    )(summed, tokens, tokens_t, prob, part_comb)
    return gsa, logits, out.reshape(width, experts).astype(jnp.float32)


def local(n_dp, n_expert, tokens, router, weight_in, weight_out, cotangent):
    experts_dev = weight_in.shape[0]
    width = tokens.shape[2]
    logits = jnp.einsum("isd,de->ise", tokens, router, preferred_element_type=jnp.float32)
    dispatch_prob = jax.nn.softmax(logits, axis=1)
    combine_prob = jax.nn.softmax(logits, axis=2)
    dispatch = dispatch_prob.astype(jnp.bfloat16)
    combine = combine_prob.astype(jnp.bfloat16)
    slots = jnp.einsum("ise,isd->ied", dispatch, tokens, preferred_element_type=jnp.float32).astype(
        jnp.bfloat16
    )
    grad_slots = jnp.einsum(
        "ise,isd->ied", combine, cotangent, preferred_element_type=jnp.float32
    ).astype(jnp.bfloat16)

    def to_owners(local_rows, cid):
        arrived = row_exchange(local_rows[0], n_expert, cid)[None]
        return lax.all_gather(arrived, "dp", axis=0, tiled=True)

    def from_owners(partial_value, cid):
        summed = relay_sum(partial_value, cid + 8)
        return row_exchange(summed, n_expert, cid)[None]

    slot_rows = to_owners(slots, 0)
    blocks = slot_rows.reshape(-1, experts_dev, width)
    pre_act = jnp.einsum("rkd,kdf->rkf", blocks, weight_in, preferred_element_type=jnp.float32)
    hidden = gelu_exact(pre_act).astype(jnp.bfloat16)
    partial_value = jnp.einsum(
        "rkf,kfd->rkd", hidden, weight_out, preferred_element_type=jnp.float32
    )
    blocks, pre_act, hidden, partial_value = (
        blocks,
        pre_act,
        hidden,
        partial_value.astype(jnp.bfloat16).reshape(slot_rows.shape),
    )
    expert_outs = from_owners(partial_value, 2)
    grad_rows = to_owners(grad_slots, 1)
    grad_blocks = grad_rows.reshape(blocks.shape)
    grad_hidden = jnp.einsum(
        "rkd,kfd->rkf", grad_blocks, weight_out, preferred_element_type=jnp.float32
    )
    _, gelu_back = jax.vjp(gelu_exact, pre_act)
    grad_pre = gelu_back(grad_hidden)[0].astype(jnp.bfloat16)
    grad_second = jnp.einsum(
        "rkf,rkd->kfd", hidden, grad_blocks, preferred_element_type=jnp.float32
    ).astype(jnp.bfloat16)
    grad_first = jnp.einsum(
        "rkd,rkf->kdf", blocks, grad_pre, preferred_element_type=jnp.float32
    ).astype(jnp.bfloat16)
    partial_back = jnp.einsum(
        "rkf,kdf->rkd", grad_pre, weight_in, preferred_element_type=jnp.float32
    )
    grad_first, grad_second, partial_back = (
        grad_first,
        grad_second,
        partial_back.astype(jnp.bfloat16).reshape(grad_rows.shape),
    )
    summed_back = lax.psum_scatter(partial_back, "dp", scatter_dimension=0, tiled=True)[0]
    mixed = jnp.einsum(
        "ise,ied->isd", combine, expert_outs, preferred_element_type=jnp.float32
    ).astype(jnp.bfloat16)
    grad_comb = jnp.einsum(
        "isd,ied->ise", cotangent, expert_outs, preferred_element_type=jnp.float32
    )
    part_comb = combine_prob * (
        grad_comb - jnp.sum(combine_prob * grad_comb, axis=2, keepdims=True)
    )
    gsa, logits, grad_router = tail(
        summed_back, tokens[0], tokens[0].T, dispatch_prob[0], part_comb[0], n_dp, n_expert
    )
    grad_slot_all = gsa[None]
    grad_logits = logits[None]
    grad_tokens = (
        jnp.einsum("ise,ied->isd", dispatch, grad_slot_all, preferred_element_type=jnp.float32)
        + jnp.einsum("ise,de->isd", grad_logits, router, preferred_element_type=jnp.float32)
    ).astype(jnp.bfloat16)
    return (mixed, grad_tokens, grad_router, grad_first, grad_second)


def solution(mesh):
    return jax.shard_map(
        functools.partial(local, mesh.shape["dp"], mesh.shape["expert"]),
        mesh=mesh,
        in_specs=(
            P(("dp", "expert"), None, None),
            P(),
            P("expert", None, "dp"),
            P("expert", "dp", None),
            P(("dp", "expert"), None, None),
        ),
        out_specs=(
            P(("dp", "expert"), None, None),
            P(("dp", "expert"), None, None),
            P(),
            P("expert", None, "dp"),
            P("expert", "dp", None),
        ),
        check_vma=False,
    )
```

```python
import functools

import jax
import jax.numpy as jnp
from jax import lax
from jax.experimental import pallas as pl
from jax.experimental.pallas import tpu as pltpu
from jax.sharding import PartitionSpec as P


def _exchange_kernel(axis, other, n, gather, x_ref, o_ref, land, send_sem, recv_sem):
    me = lax.axis_index(axis)
    fixed = lax.axis_index(other)

    def peer(j):
        if axis == "dp":
            return (j, fixed)
        return (fixed, j)

    barrier = pltpu.get_barrier_semaphore()

    @pl.loop(0, n)
    def _(j):
        @pl.when(j != me)
        def _():
            pl.semaphore_signal(barrier, inc=1, device_id=peer(j), device_id_type=pl.DeviceIdType.MESH)

    pl.semaphore_wait(barrier, n - 1)

    def copy_to(j):
        src = x_ref if gather else x_ref.at[j]
        return pltpu.make_async_remote_copy(
            src_ref=src,
            dst_ref=land.at[me],
            send_sem=send_sem.at[j],
            recv_sem=recv_sem.at[me],
            device_id=peer(j),
            device_id_type=pl.DeviceIdType.MESH,
        )

    @pl.loop(0, n)
    def _(j):
        @pl.when(j != me)
        def _():
            copy_to(j).start()

    own = x_ref[...] if gather else x_ref[me]
    o_ref[me] = own

    def arrived(j):
        src = x_ref if gather else x_ref.at[j]
        return pltpu.make_async_remote_copy(
            src_ref=src,
            dst_ref=land.at[j],
            send_sem=send_sem.at[j],
            recv_sem=recv_sem.at[j],
            device_id=peer(j),
            device_id_type=pl.DeviceIdType.MESH,
        )

    @pl.loop(0, n)
    def _(j):
        @pl.when(j != me)
        def _():
            arrived(j).wait_recv()
            o_ref[j] = land[j]
            copy_to(j).wait_send()


def exchange(x, axis, n, collective_id, gather=False):
    other = "expert" if axis == "dp" else "dp"
    block = x.shape if gather else x.shape[1:]
    out_shape = jax.ShapeDtypeStruct((n,) + tuple(block), x.dtype)
    return pl.pallas_call(
        functools.partial(_exchange_kernel, axis, other, n, gather),
        out_shape=out_shape,
        in_specs=[pl.BlockSpec(memory_space=pltpu.VMEM)],
        out_specs=pl.BlockSpec(memory_space=pltpu.VMEM),
        scratch_shapes=[
            pltpu.VMEM(out_shape.shape, x.dtype),
            pltpu.SemaphoreType.DMA((n,)),
            pltpu.SemaphoreType.DMA((n,)),
        ],
        compiler_params=pltpu.CompilerParams(collective_id=collective_id, has_side_effects=True),
    )(x)


def _row_exchange_kernel(n, rows, x_ref, o_ref, land, send_sem, recv_sem, own_sem):
    me = lax.axis_index("expert")
    fixed = lax.axis_index("dp")
    mesh_id = pl.DeviceIdType.MESH
    barrier = pltpu.get_barrier_semaphore()

    @pl.loop(0, n)
    def _(j):
        @pl.when(j != me)
        def _():
            pl.semaphore_signal(barrier, inc=1, device_id=(fixed, j), device_id_type=mesh_id)

    pl.semaphore_wait(barrier, n - 1)

    def block(ref, j):
        return ref.at[pl.ds(j * rows, rows)]

    def copy_to(j, slot):
        return pltpu.make_async_remote_copy(
            src_ref=block(x_ref, j), dst_ref=block(land, slot), send_sem=send_sem.at[j],
            recv_sem=recv_sem.at[slot], device_id=(fixed, j), device_id_type=mesh_id)

    @pl.loop(0, n)
    def _(j):
        @pl.when(j != me)
        def _():
            copy_to(j, me).start()

    own = pltpu.make_async_copy(block(x_ref, me), block(land, me), own_sem)
    own.start()

    @pl.loop(0, n)
    def _(j):
        @pl.when(j != me)
        def _():
            copy_to(j, j).wait_recv()
            copy_to(j, me).wait_send()

    own.wait()
    o_ref[...] = land[...]


def row_exchange(x, n, collective_id):
    return pl.pallas_call(
        functools.partial(_row_exchange_kernel, n, x.shape[0] // n),
        out_shape=jax.ShapeDtypeStruct(x.shape, x.dtype),
        in_specs=[pl.BlockSpec(memory_space=pltpu.VMEM)],
        out_specs=pl.BlockSpec(memory_space=pltpu.VMEM),
        scratch_shapes=[
            pltpu.VMEM(x.shape, x.dtype),
            pltpu.SemaphoreType.DMA((n,)),
            pltpu.SemaphoreType.DMA((n,)),
            pltpu.SemaphoreType.DMA(()),
        ],
        compiler_params=pltpu.CompilerParams(collective_id=collective_id, has_side_effects=True),
    )(x)


def gelu_exact(values):
    return jax.nn.gelu(values, approximate=False)


def _relay_sum_kernel(n_chip, x_ref, o_ref, land1, pair, land2, s1, r1, s2, r2):
    me = lax.axis_index("dp")
    fixed = lax.axis_index("expert")
    core = me % 2
    chip = me // 2
    partner = me + 1 - 2 * core
    mesh_id = pl.DeviceIdType.MESH
    barrier = pltpu.get_barrier_semaphore()
    pl.semaphore_signal(barrier, inc=1, device_id=(partner, fixed), device_id_type=mesh_id)
    for h in range(n_chip):
        @pl.when(h != chip)
        def _():
            pl.semaphore_signal(barrier, inc=1, device_id=(2 * h + core, fixed), device_id_type=mesh_id)
    pl.semaphore_wait(barrier, n_chip)

    def to_partner(h):
        return pltpu.make_async_remote_copy(
            src_ref=x_ref.at[2 * h + 1 - core], dst_ref=land1.at[h], send_sem=s1.at[h], recv_sem=r1.at[h],
            device_id=(partner, fixed), device_id_type=mesh_id)

    for h in range(n_chip):
        to_partner(h).start()
    for h in range(n_chip):
        to_partner(h).wait_recv()
        pair[h] = (x_ref[2 * h + core].astype(jnp.float32) + land1[h].astype(jnp.float32)).astype(pair.dtype)
        to_partner(h).wait_send()

    def to_chip(h, slot):
        return pltpu.make_async_remote_copy(
            src_ref=pair.at[h], dst_ref=land2.at[slot], send_sem=s2.at[h], recv_sem=r2.at[slot],
            device_id=(2 * h + core, fixed), device_id_type=mesh_id)

    for h in range(n_chip):
        @pl.when(h != chip)
        def _():
            to_chip(h, chip).start()
    land2[chip] = pair[chip]
    for h in range(n_chip):
        @pl.when(h != chip)
        def _():
            to_chip(h, h).wait_recv()
            to_chip(h, chip).wait_send()
    total = land2[0].astype(jnp.float32)
    for h in range(1, n_chip):
        total = total + land2[h].astype(jnp.float32)
    o_ref[...] = total.astype(o_ref.dtype)


def relay_sum(x, collective_id):
    n_dp = x.shape[0]
    n_chip = n_dp // 2
    block = x.shape[1:]
    return pl.pallas_call(
        functools.partial(_relay_sum_kernel, n_chip),
        out_shape=jax.ShapeDtypeStruct(block, x.dtype),
        in_specs=[pl.BlockSpec(memory_space=pltpu.VMEM)],
        out_specs=pl.BlockSpec(memory_space=pltpu.VMEM),
        scratch_shapes=[
            pltpu.VMEM((n_chip,) + block, x.dtype),
            pltpu.VMEM((n_chip,) + block, x.dtype),
            pltpu.VMEM((n_chip,) + block, x.dtype),
            pltpu.SemaphoreType.DMA((n_chip,)),
            pltpu.SemaphoreType.DMA((n_chip,)),
            pltpu.SemaphoreType.DMA((n_chip,)),
            pltpu.SemaphoreType.DMA((n_chip,)),
        ],
        compiler_params=pltpu.CompilerParams(collective_id=collective_id, has_side_effects=True),
    )(x)


def _allsum_kernel(n_dp, n_ex, x_ref, o_ref, land1, land2, land3, red1, red2, s1, r1, s2, r2, s3, r3):
    me_d = lax.axis_index("dp")
    me_e = lax.axis_index("expert")
    mesh_id = pl.DeviceIdType.MESH
    barrier = pltpu.get_barrier_semaphore()

    @pl.loop(0, n_ex)
    def _(j):
        @pl.when(j != me_e)
        def _():
            pl.semaphore_signal(barrier, inc=1, device_id=(me_d, j), device_id_type=mesh_id)

    @pl.loop(0, n_dp)
    def _(k):
        @pl.when(k != me_d)
        def _():
            pl.semaphore_signal(barrier, inc=1, device_id=(k, me_e), device_id_type=mesh_id)

    pl.semaphore_wait(barrier, n_ex - 1 + n_dp - 1)

    def ex_copy(src, land, send, recv, j, slot):
        return pltpu.make_async_remote_copy(
            src_ref=src, dst_ref=land.at[slot], send_sem=send.at[j], recv_sem=recv.at[slot],
            device_id=(me_d, j), device_id_type=mesh_id)

    def dp_copy(src, land, send, recv, k, slot):
        return pltpu.make_async_remote_copy(
            src_ref=src, dst_ref=land.at[slot], send_sem=send.at[k], recv_sem=recv.at[slot],
            device_id=(k, me_e), device_id_type=mesh_id)

    @pl.loop(0, n_ex)
    def _(j):
        @pl.when(j != me_e)
        def _():
            ex_copy(x_ref.at[j], land1, s1, r1, j, me_e).start()

    land1[me_e] = x_ref[me_e]

    @pl.loop(0, n_ex)
    def _(j):
        @pl.when(j != me_e)
        def _():
            ex_copy(x_ref.at[j], land1, s1, r1, j, j).wait_recv()
            ex_copy(x_ref.at[j], land1, s1, r1, j, me_e).wait_send()

    red1[...] = jnp.sum(land1[...].astype(jnp.float32), axis=0).astype(red1.dtype)

    @pl.loop(0, n_dp)
    def _(k):
        @pl.when(k != me_d)
        def _():
            dp_copy(red1, land2, s2, r2, k, me_d).start()

    land2[me_d] = red1[...]

    @pl.loop(0, n_dp)
    def _(k):
        @pl.when(k != me_d)
        def _():
            dp_copy(red1, land2, s2, r2, k, k).wait_recv()
            dp_copy(red1, land2, s2, r2, k, me_d).wait_send()

    total = land2[0].astype(jnp.float32)
    for k in range(1, n_dp):
        total = total + land2[k].astype(jnp.float32)
    red2[...] = total.astype(red2.dtype)

    @pl.loop(0, n_ex)
    def _(j):
        @pl.when(j != me_e)
        def _():
            ex_copy(red2, land3, s3, r3, j, me_e).start()

    o_ref[me_e] = red2[...]

    @pl.loop(0, n_ex)
    def _(j):
        @pl.when(j != me_e)
        def _():
            ex_copy(red2, land3, s3, r3, j, j).wait_recv()
            o_ref[j] = land3[j]
            ex_copy(red2, land3, s3, r3, j, me_e).wait_send()


def all_sum(value, n_dp, n_expert):
    rows, cols = value.shape
    block = (rows // n_expert, cols)
    chunks = value.astype(jnp.bfloat16).reshape(n_expert, *block)
    out = pl.pallas_call(
        functools.partial(_allsum_kernel, n_dp, n_expert),
        out_shape=jax.ShapeDtypeStruct(chunks.shape, chunks.dtype),
        in_specs=[pl.BlockSpec(memory_space=pltpu.VMEM)],
        out_specs=pl.BlockSpec(memory_space=pltpu.VMEM),
        scratch_shapes=[
            pltpu.VMEM(chunks.shape, chunks.dtype),
            pltpu.VMEM((n_dp,) + block, chunks.dtype),
            pltpu.VMEM(chunks.shape, chunks.dtype),
            pltpu.VMEM(block, chunks.dtype),
            pltpu.VMEM(block, chunks.dtype),
            pltpu.SemaphoreType.DMA((n_expert,)),
            pltpu.SemaphoreType.DMA((n_expert,)),
            pltpu.SemaphoreType.DMA((n_dp,)),
            pltpu.SemaphoreType.DMA((n_dp,)),
            pltpu.SemaphoreType.DMA((n_expert,)),
            pltpu.SemaphoreType.DMA((n_expert,)),
        ],
        compiler_params=pltpu.CompilerParams(collective_id=4, has_side_effects=True),
    )(chunks)
    return out.reshape(rows, cols).astype(value.dtype)


def _tail_kernel(n_dp, n_ex, rows, summed_ref, tok_ref, tokt_ref, prob_ref, comb_ref,
                 gsa_ref, logit_ref, o_ref,
                 land0, xs, land1, land2, land3, red1, red2, s0, r0, own_sem, s1, r1, s2, r2, s3, r3):
    me_d = lax.axis_index("dp")
    me_e = lax.axis_index("expert")
    mesh_id = pl.DeviceIdType.MESH
    barrier = pltpu.get_barrier_semaphore()

    @pl.loop(0, n_ex)
    def _(j):
        @pl.when(j != me_e)
        def _():
            pl.semaphore_signal(barrier, inc=1, device_id=(me_d, j), device_id_type=mesh_id)

    @pl.loop(0, n_dp)
    def _(k):
        @pl.when(k != me_d)
        def _():
            pl.semaphore_signal(barrier, inc=1, device_id=(k, me_e), device_id_type=mesh_id)

    pl.semaphore_wait(barrier, n_ex - 1 + n_dp - 1)

    def row_copy(j, slot):
        return pltpu.make_async_remote_copy(
            src_ref=summed_ref.at[pl.ds(j * rows, rows)], dst_ref=land0.at[pl.ds(slot * rows, rows)],
            send_sem=s0.at[j], recv_sem=r0.at[slot], device_id=(me_d, j), device_id_type=mesh_id)

    @pl.loop(0, n_ex)
    def _(j):
        @pl.when(j != me_e)
        def _():
            row_copy(j, me_e).start()

    own = pltpu.make_async_copy(
        summed_ref.at[pl.ds(me_e * rows, rows)], land0.at[pl.ds(me_e * rows, rows)], own_sem)
    own.start()

    @pl.loop(0, n_ex)
    def _(j):
        @pl.when(j != me_e)
        def _():
            row_copy(j, j).wait_recv()
            row_copy(j, me_e).wait_send()

    own.wait()
    gsa = land0[...]
    gsa_ref[...] = gsa
    prob = prob_ref[...]
    grad_disp = lax.dot_general(tok_ref[...], gsa, (((1,), (1,)), ((), ())), preferred_element_type=jnp.float32)
    part_disp = prob * (grad_disp - jnp.sum(prob * grad_disp, axis=0, keepdims=True))
    logits = (part_disp + comb_ref[...]).astype(logit_ref.dtype)
    logit_ref[...] = logits
    term = jnp.dot(tokt_ref[...], logits, preferred_element_type=jnp.float32)
    xs[...] = term.astype(xs.dtype).reshape(xs.shape)

    def ex_copy(src, land, send, recv, j, slot):
        return pltpu.make_async_remote_copy(
            src_ref=src, dst_ref=land.at[slot], send_sem=send.at[j], recv_sem=recv.at[slot],
            device_id=(me_d, j), device_id_type=mesh_id)

    def dp_copy(src, land, send, recv, k, slot):
        return pltpu.make_async_remote_copy(
            src_ref=src, dst_ref=land.at[slot], send_sem=send.at[k], recv_sem=recv.at[slot],
            device_id=(k, me_e), device_id_type=mesh_id)

    @pl.loop(0, n_ex)
    def _(j):
        @pl.when(j != me_e)
        def _():
            ex_copy(xs.at[j], land1, s1, r1, j, me_e).start()

    land1[me_e] = xs[me_e]

    @pl.loop(0, n_ex)
    def _(j):
        @pl.when(j != me_e)
        def _():
            ex_copy(xs.at[j], land1, s1, r1, j, j).wait_recv()
            ex_copy(xs.at[j], land1, s1, r1, j, me_e).wait_send()

    red1[...] = jnp.sum(land1[...].astype(jnp.float32), axis=0).astype(red1.dtype)

    @pl.loop(0, n_dp)
    def _(k):
        @pl.when(k != me_d)
        def _():
            dp_copy(red1, land2, s2, r2, k, me_d).start()

    land2[me_d] = red1[...]

    @pl.loop(0, n_dp)
    def _(k):
        @pl.when(k != me_d)
        def _():
            dp_copy(red1, land2, s2, r2, k, k).wait_recv()
            dp_copy(red1, land2, s2, r2, k, me_d).wait_send()

    total = land2[0].astype(jnp.float32)
    for k in range(1, n_dp):
        total = total + land2[k].astype(jnp.float32)
    red2[...] = total.astype(red2.dtype)

    @pl.loop(0, n_ex)
    def _(j):
        @pl.when(j != me_e)
        def _():
            ex_copy(red2, land3, s3, r3, j, me_e).start()

    o_ref[me_e] = red2[...]

    @pl.loop(0, n_ex)
    def _(j):
        @pl.when(j != me_e)
        def _():
            ex_copy(red2, land3, s3, r3, j, j).wait_recv()
            o_ref[j] = land3[j]
            ex_copy(red2, land3, s3, r3, j, me_e).wait_send()


def tail(summed, tokens, tokens_t, prob, part_comb, n_dp, n_ex):
    width, experts = tokens_t.shape[0], prob.shape[1]
    block = (width // n_ex, experts)
    chunks = (n_ex,) + block
    bf = jnp.bfloat16
    vmem = pl.BlockSpec(memory_space=pltpu.VMEM)
    gsa, logits, out = pl.pallas_call(
        functools.partial(_tail_kernel, n_dp, n_ex, summed.shape[0] // n_ex),
        out_shape=(jax.ShapeDtypeStruct(summed.shape, summed.dtype),
                   jax.ShapeDtypeStruct(prob.shape, bf),
                   jax.ShapeDtypeStruct(chunks, bf)),
        in_specs=[vmem] * 5,
        out_specs=(vmem, vmem, vmem),
        scratch_shapes=[
            pltpu.VMEM(summed.shape, summed.dtype),
            pltpu.VMEM(chunks, bf),
            pltpu.VMEM(chunks, bf),
            pltpu.VMEM((n_dp,) + block, bf),
            pltpu.VMEM(chunks, bf),
            pltpu.VMEM(block, bf),
            pltpu.VMEM(block, bf),
            pltpu.SemaphoreType.DMA((n_ex,)),
            pltpu.SemaphoreType.DMA((n_ex,)),
            pltpu.SemaphoreType.DMA(()),
            pltpu.SemaphoreType.DMA((n_ex,)),
            pltpu.SemaphoreType.DMA((n_ex,)),
            pltpu.SemaphoreType.DMA((n_dp,)),
            pltpu.SemaphoreType.DMA((n_dp,)),
            pltpu.SemaphoreType.DMA((n_ex,)),
            pltpu.SemaphoreType.DMA((n_ex,)),
        ],
        compiler_params=pltpu.CompilerParams(collective_id=5, has_side_effects=True),
    )(summed, tokens, tokens_t, prob, part_comb)
    return gsa, logits, out.reshape(width, experts).astype(jnp.float32)


def local(n_dp, n_expert, tokens, router, weight_in, weight_out, cotangent):
    experts_dev = weight_in.shape[0]
    width = tokens.shape[2]
    logits = jnp.einsum("isd,de->ise", tokens, router, preferred_element_type=jnp.float32)
    dispatch_prob = jax.nn.softmax(logits, axis=1)
    combine_prob = jax.nn.softmax(logits, axis=2)
    dispatch = dispatch_prob.astype(jnp.bfloat16)
    combine = combine_prob.astype(jnp.bfloat16)
    slots = jnp.einsum("ise,isd->ied", dispatch, tokens, preferred_element_type=jnp.float32).astype(
        jnp.bfloat16
    )
    grad_slots = jnp.einsum(
        "ise,isd->ied", combine, cotangent, preferred_element_type=jnp.float32
    ).astype(jnp.bfloat16)

    def to_owners(local_rows, cid):
        arrived = row_exchange(local_rows[0], n_expert, cid)[None]
        return lax.all_gather(arrived, "dp", axis=0, tiled=True)

    def from_owners(partial_value, cid):
        summed = lax.psum_scatter(partial_value, "dp", scatter_dimension=0, tiled=True)
        return row_exchange(summed[0], n_expert, cid)[None]

    slot_rows = to_owners(slots, 0)
    blocks = slot_rows.reshape(-1, experts_dev, width)
    pre_act = jnp.einsum("rkd,kdf->rkf", blocks, weight_in, preferred_element_type=jnp.float32)
    hidden = gelu_exact(pre_act).astype(jnp.bfloat16)
    partial_value = jnp.einsum(
        "rkf,kfd->rkd", hidden, weight_out, preferred_element_type=jnp.float32
    )
    blocks, pre_act, hidden, partial_value = (
        blocks,
        pre_act,
        hidden,
        partial_value.astype(jnp.bfloat16).reshape(slot_rows.shape),
    )
    expert_outs = from_owners(partial_value, 2)
    grad_rows = to_owners(grad_slots, 1)
    grad_blocks = grad_rows.reshape(blocks.shape)
    grad_hidden = jnp.einsum(
        "rkd,kfd->rkf", grad_blocks, weight_out, preferred_element_type=jnp.float32
    )
    _, gelu_back = jax.vjp(gelu_exact, pre_act)
    grad_pre = gelu_back(grad_hidden)[0].astype(jnp.bfloat16)
    grad_second = jnp.einsum(
        "rkf,rkd->kfd", hidden, grad_blocks, preferred_element_type=jnp.float32
    ).astype(jnp.bfloat16)
    grad_first = jnp.einsum(
        "rkd,rkf->kdf", blocks, grad_pre, preferred_element_type=jnp.float32
    ).astype(jnp.bfloat16)
    partial_back = jnp.einsum(
        "rkf,kdf->rkd", grad_pre, weight_in, preferred_element_type=jnp.float32
    )
    grad_first, grad_second, partial_back = (
        grad_first,
        grad_second,
        partial_back.astype(jnp.bfloat16).reshape(grad_rows.shape),
    )
    summed_back = relay_sum(partial_back, 11)
    mixed = jnp.einsum(
        "ise,ied->isd", combine, expert_outs, preferred_element_type=jnp.float32
    ).astype(jnp.bfloat16)
    grad_comb = jnp.einsum(
        "isd,ied->ise", cotangent, expert_outs, preferred_element_type=jnp.float32
    )
    part_comb = combine_prob * (
        grad_comb - jnp.sum(combine_prob * grad_comb, axis=2, keepdims=True)
    )
    gsa, logits, grad_router = tail(
        summed_back, tokens[0], tokens[0].T, dispatch_prob[0], part_comb[0], n_dp, n_expert
    )
    grad_slot_all = gsa[None]
    grad_logits = logits[None]
    grad_tokens = (
        jnp.einsum("ise,ied->isd", dispatch, grad_slot_all, preferred_element_type=jnp.float32)
        + jnp.einsum("ise,de->isd", grad_logits, router, preferred_element_type=jnp.float32)
    ).astype(jnp.bfloat16)
    return (mixed, grad_tokens, grad_router, grad_first, grad_second)


def solution(mesh):
    return jax.shard_map(
        functools.partial(local, mesh.shape["dp"], mesh.shape["expert"]),
        mesh=mesh,
        in_specs=(
            P(("dp", "expert"), None, None),
            P(),
            P("expert", None, "dp"),
            P("expert", "dp", None),
            P(("dp", "expert"), None, None),
        ),
        out_specs=(
            P(("dp", "expert"), None, None),
            P(("dp", "expert"), None, None),
            P(),
            P("expert", None, "dp"),
            P("expert", "dp", None),
        ),
        check_vma=False,
    )
```
